32 devices in a mesh: seq: 2 (over x), fsdp: 16 (over z, y, core).
Axes of the slice: x: 2, y: 2, z: 4, core: 2. Of those that a mesh axis runs over, the one named last changes fastest.
Arguments:
- tokens: bfloat16 [16, 1024, 768], P('fsdp', 'seq'), may hold values from -6 to 6
- prior_logits: bfloat16 [16, 12, 1024, 1024], P('fsdp', 'seq'), may hold values from -6 to 6
- lengths: int32 [16], P('fsdp'), may hold values from 256 to 1024, as said below
- order: int32 [16, 1024], P('fsdp'), may hold values from 0 to 1023, each once within a row
- cotangent: bfloat16 [16, 1024, 768], P('fsdp', 'seq'), may hold values from -6 to 6
- w_qkv: bfloat16 [768, 2304], P('fsdp'), may hold values from -0.21875 to 0.21875
- w_out: bfloat16 [768, 768], P('fsdp'), may hold values from -3.5 to 3.5
- w_in: bfloat16 [768, 3072], P('fsdp'), may hold values from -0.21875 to 0.21875
- w_back: bfloat16 [3072, 768], P('fsdp'), may hold values from -0.109375 to 0.109375
- bias_q: bfloat16 [768], P('fsdp'), may hold values from -1.5 to 1.5
- bias_v: bfloat16 [768], P('fsdp'), may hold values from -0.25 to 0.25
- bias_o: bfloat16 [768], P('fsdp'), may hold values from -1.5 to 1.5
- gain_one: bfloat16 [768], P('fsdp'), may hold values from 0.5 to 1.5
- shift_one: bfloat16 [768], P('fsdp'), may hold values from -1.5 to 1.5
- bias_in: bfloat16 [3072], P('fsdp'), may hold values from -1.5 to 1.5
- bias_back: bfloat16 [768], P('fsdp'), may hold values from -1.5 to 1.5
- gain_two: bfloat16 [768], P('fsdp'), may hold values from 0.5 to 1.5
- shift_two: bfloat16 [768], P('fsdp'), may hold values from -1.5 to 1.5
Outputs:
- output: bfloat16 [16, 1024, 768], P('fsdp', 'seq')
- raw_logits: bfloat16 [16, 12, 1024, 1024], P('fsdp', 'seq')
- tokens_grad: bfloat16 [16, 1024, 768], P('fsdp', 'seq')
- prior_grad: bfloat16 [16, 12, 1024, 1024], P('fsdp', 'seq')
- grad_w_qkv: float32 [768, 2304], P('fsdp')
- grad_w_out: float32 [768, 768], P('fsdp')
- grad_w_in: float32 [768, 3072], P('fsdp')
- grad_w_back: float32 [3072, 768], P('fsdp')
- grad_bias_q: float32 [768], P('fsdp')
- grad_bias_v: float32 [768], P('fsdp')
- grad_bias_o: float32 [768], P('fsdp')
- grad_gain_one: float32 [768], P('fsdp')
- grad_shift_one: float32 [768], P('fsdp')
- grad_bias_in: float32 [3072], P('fsdp')
- grad_bias_back: float32 [768], P('fsdp')
- grad_gain_two: float32 [768], P('fsdp')
- grad_shift_two: float32 [768], P('fsdp')
- rms: float32 [3], replicated
The draws below stay inside these ranges and needn't reach their ends.
Inputs may be any that keep to these rules, and one draw needn't show every extreme that they name: `lengths`: positions below a sequence's length hold its tokens, the others are padding; some sequence has exactly 1024.
All inputs are finite; a program needn't handle non-finite values.
Results may differ from the reference program's by a relative error of at most 0.017.
Values may be sent and summed in bfloat16 or wider, within the bound.
No kernel may reach another device: no remote copies, remote signals or barrier semaphores. Data moves between devices by JAX's collectives and lax.ppermute only.
A program may use at most 192 MiB of HBM per device.

```python
import math
import jax
import jax.numpy as jnp
from jax import lax

D = 768
H = 12
HD = 64
FF = 3072
SEQ_LEN = 1024
SEQS = 16


def draw_lengths(key, part):
    position = jnp.arange(SEQS, dtype=jnp.int32)
    shortest = SEQ_LEN // 4
    rising = shortest + (SEQ_LEN - shortest) * position // max(SEQS - 1, 1)
    jitter = jax.random.randint(jax.random.fold_in(key, 1), (SEQS,), -(SEQ_LEN // 8), SEQ_LEN // 8 + 1)
    lengths_drawn = jnp.clip(rising + jitter, shortest, SEQ_LEN)
    chosen = jax.random.randint(jax.random.fold_in(key, 2), (), SEQS - max(SEQS // 4, 1), SEQS)
    return jnp.where(position == chosen, SEQ_LEN, lengths_drawn).astype(jnp.int32)


def with_spikes(array, rng, source, target, shards_of, factor):
    def block_of(dim):
        return (jnp.arange(array.shape[dim]) // (array.shape[dim] // shards_of)).reshape((-1,) + (1,) * (array.ndim - 1 - dim))

    first = jax.random.permutation(rng, shards_of)[block_of(target)]
    second = (block_of(target) + shards_of // 2) % shards_of
    return jnp.where((block_of(source) == first) | (block_of(source) == second), factor * array, array)


def block_levels(own_key, extent, cuts, smallest, high):
    factor_of, own = 1.0, jax.random.fold_in(own_key, 6)
    for dim, shards_of in cuts:
        steps = jnp.exp(jax.random.uniform(jax.random.fold_in(own, dim), (shards_of,), jnp.float32, smallest / len(cuts), high / len(cuts)))
        factor_of = factor_of * jnp.repeat(steps, extent[dim] // shards_of).reshape([-1 if axis == dim else 1 for axis in range(len(extent))])
    return factor_of


def scatter_about(rng, extent, deviation, bound, pieces=(), kind=jnp.bfloat16):
    level = block_levels(rng, extent, pieces, -0.22, 0.18) if pieces else 1.0
    array = jax.random.normal(rng, extent, jnp.float32) * deviation * level
    return jnp.minimum(jnp.maximum(array, -bound), bound).astype(kind)


def bell_draw_with(stream_key, shape, scale, bound, split, heavy, held_as=jnp.bfloat16):
    result = scale * jax.random.normal(stream_key, shape, jnp.float32)
    if split:
        result = result * block_levels(stream_key, shape, split, -0.22, 0.18)
    return jnp.clip(with_spikes(result, jax.random.fold_in(stream_key, 3), *heavy), -bound, bound).astype(held_as)


def setup_inputs(seed: int = 0) -> dict:
    arg_keys = jax.random.split(jax.random.key(seed), 19)
    return {
        "tokens": bell_draw_with(arg_keys[0], (SEQS, SEQ_LEN, D), 1.0, 6.0, ((0, 16), (1, 2)), (0, 2, 16, 2.0)),
        "prior_logits": scatter_about(arg_keys[1], (SEQS, H, SEQ_LEN, SEQ_LEN), 1.0, 6.0, ((0, 16), (1, 2))),
        "lengths": draw_lengths(jax.random.fold_in(arg_keys[18], 71), 0),
        "order": jax.vmap(lambda own: jax.random.permutation(own, SEQ_LEN))(jax.random.split(arg_keys[3], SEQS)).reshape((SEQS, SEQ_LEN)).astype(jnp.int32),
        "cotangent": bell_draw_with(arg_keys[4], (SEQS, SEQ_LEN, D), 1.0, 6.0, ((0, 16), (1, 2)), (0, 2, 16, 2.0)),
        "w_qkv": scatter_about(arg_keys[5], (D, 3 * D), D ** -0.5, 0.21875, ((0, 16),)),
        "w_out": scatter_about(arg_keys[6], (D, D), (max(4 * D // SEQ_LEN, 1)) ** -0.5, 3.5, ((0, 16),)),
        "w_in": scatter_about(arg_keys[7], (D, FF), D ** -0.5, 0.21875, ((0, 16),)),
        "w_back": scatter_about(arg_keys[8], (FF, D), FF ** -0.5, 0.109375, ((0, 16),)),
        "bias_q": scatter_about(arg_keys[9], (D,), 0.3, 1.5, ((0, 16),)),
        "bias_v": scatter_about(arg_keys[10], (D,), 0.05, 0.25, ((0, 16),)),
        "bias_o": scatter_about(arg_keys[11], (D,), 0.3, 1.5, ((0, 16),)),
        "gain_one": jnp.clip(1.0 + 0.1 * jax.random.normal(arg_keys[12], (D,), jnp.float32), 0.5, 1.5).astype(jnp.bfloat16),
        "shift_one": scatter_about(arg_keys[13], (D,), 0.3, 1.5, ((0, 16),)),
        "bias_in": scatter_about(arg_keys[14], (FF,), 0.3, 1.5, ((0, 16),)),
        "bias_back": scatter_about(arg_keys[15], (D,), 0.3, 1.5, ((0, 16),)),
        "gain_two": jnp.clip(1.0 + 0.1 * jax.random.normal(arg_keys[16], (D,), jnp.float32), 0.5, 1.5).astype(jnp.bfloat16),
        "shift_two": scatter_about(arg_keys[17], (D,), 0.3, 1.5, ((0, 16),)),
    }


@jax.custom_vjp
def low(v):
    return lax.optimization_barrier(v.astype(jnp.bfloat16)).astype(jnp.float32)

@jax.custom_vjp
def low_back(v):
    return v

def low_keep(v):
    return (low(v), None)

def low_pass(kept, grad):
    return (grad,)

def back_keep(v):
    return (v, None)

def back_low(kept, grad):
    return (low(grad),)
low.defvjp(low_keep, low_pass)
low_back.defvjp(back_keep, back_low)
eps_norm = 1e-05
masked_fill = -1e+30
highest = lax.Precision.HIGHEST

def layer_norm(values, gain, shift):
    average = lax.optimization_barrier(jnp.mean(values, axis=-1, keepdims=True))
    centered = values - average
    variance = lax.optimization_barrier(jnp.mean(centered * centered, axis=-1, keepdims=True))
    return centered * lax.rsqrt(variance + eps_norm) * gain + shift

def sequence_forward(params, tokens_in, prior_in, order_row, length):
    qkv_weight, proj_weight, inner_weight, outer_weight, query_bias, value_bias, proj_bias, gain_first, shift_first, inner_bias, outer_bias, gain_second, shift_second = params
    total = tokens_in.shape[0]
    heads = prior_in.shape[0]
    scale = 1.0 / math.sqrt(HD)
    joint = jnp.dot(tokens_in, qkv_weight, precision=highest)
    queries = low_back(low(joint[:, :D] + query_bias))
    key_rows = low_back(low(joint[:, D:2 * D]))
    value_rows = low_back(low(joint[:, 2 * D:] + value_bias))
    positions = jnp.arange(total, dtype=jnp.int32)
    inverse = jnp.zeros((total,), jnp.int32).at[order_row].set(positions)

    def split_heads(values):
        return values[inverse].reshape(total, heads, HD).transpose(1, 0, 2)
    scores = jnp.einsum('hqd,hkd->hqk', split_heads(queries), split_heads(key_rows), precision=highest) * scale + prior_in
    scores = low_back(scores)
    masked = jnp.where((positions < length)[None, None, :], scores, masked_fill)
    largest = lax.optimization_barrier(jnp.max(masked, axis=-1, keepdims=True))
    exponent = jnp.exp(masked - largest)
    probability = low(exponent / lax.optimization_barrier(jnp.sum(exponent, axis=-1, keepdims=True)))
    context = jnp.einsum('hqk,hkd->hqd', probability, split_heads(value_rows), precision=highest)
    context = low_back(low(context.transpose(1, 0, 2).reshape(total, D)[order_row]))
    attended = low_back(jnp.dot(context, proj_weight, precision=highest) + proj_bias)
    hidden = layer_norm(tokens_in + attended, gain_first, shift_first)
    inner = low_back(jnp.dot(low(hidden), inner_weight, precision=highest) + inner_bias)
    activated = low(jax.nn.gelu(inner, approximate=False))
    branch = low_back(jnp.dot(activated, outer_weight, precision=highest) + outer_bias)
    output = layer_norm(hidden + branch, gain_second, shift_second)
    return (output, (scores, attended, branch))

def reference(tokens, prior_logits, lengths, order, cotangent, w_qkv, w_out, w_in, w_back, bias_q, bias_v, bias_o, gain_one, shift_one, bias_in, bias_back, gain_two, shift_two):
    params = tuple((weight.astype(jnp.float32) for weight in (w_qkv, w_out, w_in, w_back, bias_q, bias_v, bias_o, gain_one, shift_one, bias_in, bias_back, gain_two, shift_two)))
    zero_grads = jax.tree.map(jnp.zeros_like, params)
    zero_stats = jnp.zeros((4,), jnp.float32)

    def per_sequence(carry, items):
        grads_total, stats = carry
        seq_tokens, seq_prior, seq_length, seq_order, seq_cot = items
        tokens_f = seq_tokens.astype(jnp.float32)
        prior_f = seq_prior.astype(jnp.float32)
        valid_rows = (seq_order < seq_length).astype(jnp.float32)[:, None]

        def forward(params_in, tokens_in, prior_in):
            return sequence_forward(params_in, tokens_in, prior_in, seq_order, seq_length)
        output, pullback, extra = jax.vjp(forward, params, tokens_f, prior_f, has_aux=True)
        grads_params, grads_tokens, grads_prior = pullback(seq_cot.astype(jnp.float32) * valid_rows)
        scores, attended, branch = extra
        new_stats = stats + jnp.stack([jnp.sum(valid_rows * tokens_f * tokens_f), jnp.sum(valid_rows * attended * attended), jnp.sum(valid_rows * branch * branch), jnp.sum(valid_rows)])
        grads_total = jax.tree.map(jnp.add, grads_total, grads_params)
        return ((grads_total, new_stats), (output.astype(jnp.bfloat16), scores.astype(jnp.bfloat16), grads_tokens.astype(jnp.bfloat16), grads_prior.astype(jnp.bfloat16)))
    (grads_total, stats), (outputs, raw, tokens_grad, prior_grad) = lax.scan(per_sequence, (zero_grads, zero_stats), (tokens, prior_logits, lengths, order, cotangent))
    rms = jnp.sqrt(stats[:3] / (stats[3] * D))
    return (outputs, raw, tokens_grad, prior_grad, grads_total[0], grads_total[1], grads_total[2], grads_total[3], grads_total[4], grads_total[5], grads_total[6], grads_total[7], grads_total[8], grads_total[9], grads_total[10], grads_total[11], grads_total[12], rms)
```

```python
import math

import jax
import jax.numpy as jnp
from jax import lax
from jax.sharding import PartitionSpec as P

HD = 64
eps_norm = 1e-05
masked_fill = -1e30
f32 = jnp.float32
bf16 = jnp.bfloat16


def layer_norm(values, gain, shift):
    average = jnp.mean(values, axis=-1, keepdims=True)
    centered = values - average
    variance = jnp.mean(centered * centered, axis=-1, keepdims=True)
    return centered * lax.rsqrt(variance + eps_norm) * gain + shift


def gelu_exact(values):
    return jax.nn.gelu(values, approximate=False)


def contract_rows(left, right):
    return lax.dot_general(left, right, (((0,), (0,)), ((), ())), preferred_element_type=f32)


def contract_cols(left, right):
    return lax.dot_general(left, right, (((1,), (1,)), ((), ())), preferred_element_type=f32)


def bits_of(count):
    return [1 << k for k in range(count.bit_length() - 1)]


def swap(value, axis, bit):
    count = lax.axis_size(axis)
    return lax.ppermute(value, axis, [(i, i ^ bit) for i in range(count)])


def gather_blocks(shard, axis):
    me = lax.axis_index(axis)
    held = shard[None]
    for bit in reversed(bits_of(lax.axis_size(axis))):
        other = swap(held, axis, bit)
        high = (me & bit) != 0
        first = jnp.where(high, other, held)
        second = jnp.where(high, held, other)
        held = jnp.stack([first, second], axis=1).reshape((-1,) + shard.shape)
    return held


def reduce_blocks(part, over_seq, wire):
    me = lax.axis_index("fsdp")
    side = lax.axis_index("seq")
    keep = part
    width = part.shape[2]
    for bit in bits_of(lax.axis_size("fsdp")):
        pairs = keep.reshape((keep.shape[0] // 2, 2) + keep.shape[1:])
        mine = ((me & bit) != 0).astype(jnp.int32)
        sent = lax.dynamic_index_in_dim(pairs, 1 - mine, 1, keepdims=False).astype(wire)
        kept = lax.dynamic_index_in_dim(pairs, mine, 1, keepdims=False)
        keep = (kept.astype(f32) + swap(sent, "fsdp", bit).astype(f32)).astype(wire)
        if over_seq and bit == 1:
            half = width // 2
            sent = lax.dynamic_slice_in_dim(keep, (1 - side) * half, half, 2)
            kept = lax.dynamic_slice_in_dim(keep, side * half, half, 2)
            keep = (kept.astype(f32) + swap(sent, "seq", 1).astype(f32)).astype(wire)
    own = keep[0]
    if not over_seq:
        return own
    other = swap(own, "seq", 1)
    return jnp.where(
        side == 0, jnp.concatenate([own, other], 1), jnp.concatenate([other, own], 1)
    )


def body(
    tokens, prior_logits, lengths, order, cotangent, w_qkv, w_out, w_in, w_back,
    bias_q, bias_v, bias_o, gain_one, shift_one, bias_in, bias_back, gain_two, shift_two,
):
    side = lax.axis_index("seq")
    me = lax.axis_index("fsdp")
    groups = lax.axis_size("fsdp")
    rows = tokens[0]
    local_count, width = rows.shape
    total = 2 * local_count
    heads_local = prior_logits.shape[1]
    local_width = heads_local * HD
    scale = 1.0 / math.sqrt(HD)
    piece = bias_q.shape[0]

    other_rows = swap(rows, "seq", 1)
    own_qkv = lax.dynamic_index_in_dim(
        w_qkv.reshape(w_qkv.shape[0], 3, 2, local_width), side, 2, keepdims=False
    ).reshape(w_qkv.shape[0], 3 * local_width)
    small = jnp.concatenate(
        [bias_q, bias_v, bias_o, gain_one, shift_one, bias_back, gain_two, shift_two, bias_in]
    )[None]
    small_all = gather_blocks(small, "fsdp")[:, 0]
    query_bias, value_bias, proj_bias, first_gain, first_shift, outer_bias, second_gain, second_shift = (
        small_all[:, k * piece : (k + 1) * piece].reshape(width).astype(f32) for k in range(8)
    )
    inner_bias = small_all[:, 8 * piece :].reshape(-1).astype(f32)
    qkv_weight = gather_blocks(own_qkv, "fsdp").reshape(width, 3 * local_width)
    proj_weight = gather_blocks(w_out, "fsdp").reshape(width, width)
    inner_weight = gather_blocks(w_in, "fsdp").reshape(width, -1)
    outer_weight = gather_blocks(w_back, "fsdp").reshape(-1, width)

    order_row = order[0]
    length = lengths[0]
    own_order = lax.dynamic_slice_in_dim(order_row, side * local_count, local_count)
    other_order = lax.dynamic_slice_in_dim(order_row, (1 - side) * local_count, local_count)
    positions = jnp.arange(total, dtype=jnp.int32)
    own_pick = (positions[:, None] == own_order[None, :]).astype(bf16)
    other_pick = (positions[:, None] == other_order[None, :]).astype(bf16)

    def to_positions(own, other):
        return (
            jnp.dot(own_pick, own, preferred_element_type=f32)
            + jnp.dot(other_pick, other, preferred_element_type=f32)
        ).astype(bf16)

    placed_rows = to_positions(rows, other_rows)
    own_cols = lambda vector: lax.dynamic_slice_in_dim(vector, side * local_width, local_width)
    joint_bias = jnp.concatenate(
        [own_cols(query_bias), jnp.zeros((local_width,), f32), own_cols(value_bias)]
    )
    joint = (jnp.dot(placed_rows, qkv_weight, preferred_element_type=f32) + joint_bias).astype(bf16)
    placed = joint.reshape(total, 3, local_width)
    query_pos = placed[:, 0].reshape(total, heads_local, HD)
    key_pos = placed[:, 1].reshape(total, heads_local, HD)
    value_pos = placed[:, 2].reshape(total, heads_local, HD)
    key_valid = (positions < length)[None, None, :]
    prior = prior_logits[0]
    block = min(512, total)
    block_count = total // block

    def block_scores(start):
        query_blk = lax.dynamic_slice_in_dim(query_pos, start, block, 0)
        prior_blk = lax.dynamic_slice_in_dim(prior, start, block, 1).astype(f32)
        scores = (
            jnp.einsum("qhd,khd->hqk", query_blk, key_pos, preferred_element_type=f32) * scale
            + prior_blk
        )
        return (query_blk, scores)

    def forward_block(block_index, carry):
        raw_buf, context_buf, lse_buf = carry
        start = block_index * block
        query_blk, scores = block_scores(start)
        masked = jnp.where(key_valid, scores, masked_fill)
        largest = jnp.max(masked, axis=-1, keepdims=True)
        exponent = jnp.exp(masked - largest)
        row_total = jnp.sum(exponent, axis=-1, keepdims=True)
        weights = (exponent / row_total).astype(bf16)
        context_blk = jnp.einsum(
            "hqk,khd->qhd", weights, value_pos, preferred_element_type=f32
        ).astype(bf16)
        raw_buf = lax.dynamic_update_slice_in_dim(raw_buf, scores.astype(bf16), start, 1)
        context_buf = lax.dynamic_update_slice_in_dim(context_buf, context_blk, start, 0)
        lse_buf = lax.dynamic_update_slice_in_dim(lse_buf, largest + jnp.log(row_total), start, 1)
        return (raw_buf, context_buf, lse_buf)

    raw_buf, context_pos, lse_buf = lax.fori_loop(
        0,
        block_count,
        forward_block,
        (
            jnp.zeros((heads_local, total, total), bf16),
            jnp.zeros((total, heads_local, HD), bf16),
            jnp.zeros((heads_local, total, 1), f32),
        ),
    )
    context_pos = context_pos.reshape(total, local_width)
    context_sent = contract_rows(other_pick, context_pos).astype(bf16)
    context_own = contract_rows(own_pick, context_pos).astype(bf16)
    context_got = swap(context_sent, "seq", 1)
    context = jnp.where(
        side == 0,
        jnp.concatenate([context_own, context_got], 1),
        jnp.concatenate([context_got, context_own], 1),
    )
    attended = jnp.dot(context, proj_weight, preferred_element_type=f32) + proj_bias
    tokens_f = rows.astype(f32)
    residual_one = tokens_f + attended
    hidden, norm_back_one = jax.vjp(layer_norm, residual_one, first_gain, first_shift)
    hidden_low = hidden.astype(bf16)
    inner = jnp.dot(hidden_low, inner_weight, preferred_element_type=f32) + inner_bias
    activated_f, gelu_back = jax.vjp(gelu_exact, inner)
    activated = activated_f.astype(bf16)
    branch = jnp.dot(activated, outer_weight, preferred_element_type=f32) + outer_bias
    residual_two = hidden + branch
    normed_two, norm_back_two = jax.vjp(layer_norm, residual_two, second_gain, second_shift)
    valid_rows = (own_order < length).astype(f32)[:, None]
    stats = jnp.stack(
        [
            jnp.sum(valid_rows * tokens_f * tokens_f),
            jnp.sum(valid_rows * attended * attended),
            jnp.sum(valid_rows * branch * branch),
            jnp.sum(valid_rows),
        ]
    )
    d_output = cotangent[0].astype(f32) * valid_rows
    d_res_two, grad_gain_two, grad_shift_two = norm_back_two(d_output)
    d_branch = d_res_two.astype(bf16)
    grad_bias_back = jnp.sum(d_branch.astype(f32), axis=0)
    grad_w_back = contract_rows(activated, d_branch).astype(bf16)
    d_activated = contract_cols(d_branch, outer_weight)
    d_inner = gelu_back(d_activated)[0].astype(bf16)
    grad_bias_in = jnp.sum(d_inner.astype(f32), axis=0)
    grad_w_in = contract_rows(hidden_low, d_inner).astype(bf16)
    d_hidden = d_res_two + contract_cols(d_inner, inner_weight)
    d_res_one, grad_gain_one, grad_shift_one = norm_back_one(d_hidden)
    d_attended = d_res_one.astype(bf16)
    grad_bias_o = jnp.sum(d_attended.astype(f32), axis=0)
    grad_w_out = contract_rows(context, d_attended).astype(bf16)
    d_context = contract_cols(d_attended, proj_weight).astype(bf16)
    d_context_own = lax.dynamic_slice_in_dim(d_context, side * local_width, local_width, 1)
    d_context_sent = lax.dynamic_slice_in_dim(d_context, (1 - side) * local_width, local_width, 1)
    d_context_pos = to_positions(d_context_own, swap(d_context_sent, "seq", 1)).reshape(
        total, heads_local, HD
    )

    out_back = reduce_blocks(grad_w_back.reshape(groups, -1, width), True, bf16)
    out_in = reduce_blocks(grad_w_in.reshape(groups, piece, -1), True, bf16)
    out_out = reduce_blocks(grad_w_out.reshape(groups, piece, width), True, bf16)
    by_owner = lambda vector: vector.reshape(groups, -1)
    vectors = jnp.concatenate(
        [by_owner(v) for v in (grad_bias_o, grad_gain_one, grad_shift_one, grad_bias_back,
                               grad_gain_two, grad_shift_two, grad_bias_in)]
        + [jnp.broadcast_to(stats[None], (groups, 4))],
        axis=1,
    )
    vectors = reduce_blocks(vectors[:, None], False, f32)
    vectors = (vectors + swap(vectors, "seq", 1))[0]
    stats = vectors[10 * piece :]
    rms = jnp.sqrt(stats[:3] / (stats[3] * width))

    def backward_block(block_index, carry):
        dprior_buf, dquery_buf, dkey_acc, dvalue_acc = carry
        start = block_index * block
        query_blk, scores = block_scores(start)
        masked = jnp.where(key_valid, scores, masked_fill)
        lse_blk = lax.dynamic_slice_in_dim(lse_buf, start, block, 1)
        probability = jnp.exp(masked - lse_blk)
        weights = probability.astype(bf16)
        dcontext_blk = lax.dynamic_slice_in_dim(d_context_pos, start, block, 0)
        d_prob = jnp.einsum("qhd,khd->hqk", dcontext_blk, value_pos, preferred_element_type=f32)
        row_term = jnp.sum(probability * d_prob, axis=-1, keepdims=True)
        d_scores = (probability * (d_prob - row_term)).astype(bf16)
        dprior_buf = lax.dynamic_update_slice_in_dim(dprior_buf, d_scores, start, 1)
        dquery_blk = (
            jnp.einsum("hqk,khd->qhd", d_scores, key_pos, preferred_element_type=f32) * scale
        )
        dquery_buf = lax.dynamic_update_slice_in_dim(dquery_buf, dquery_blk, start, 0)
        dkey_acc = (
            dkey_acc
            + jnp.einsum("hqk,qhd->khd", d_scores, query_blk, preferred_element_type=f32) * scale
        )
        dvalue_acc = dvalue_acc + jnp.einsum(
            "hqk,qhd->khd", weights, dcontext_blk, preferred_element_type=f32
        )
        return (dprior_buf, dquery_buf, dkey_acc, dvalue_acc)

    dprior_buf, dquery_buf, dkey_acc, dvalue_acc = lax.fori_loop(
        0,
        block_count,
        backward_block,
        (
            jnp.zeros((heads_local, total, total), bf16),
            jnp.zeros((total, heads_local, HD), f32),
            jnp.zeros((total, heads_local, HD), f32),
            jnp.zeros((total, heads_local, HD), f32),
        ),
    )
    d_joint = jnp.concatenate(
        [
            dquery_buf.reshape(total, local_width),
            dkey_acc.reshape(total, local_width),
            dvalue_acc.reshape(total, local_width),
        ],
        axis=1,
    ).astype(bf16)
    grad_w_qkv = contract_rows(placed_rows, d_joint).astype(bf16)
    d_rows = contract_cols(d_joint, qkv_weight).astype(bf16)
    d_rows_sent = contract_rows(other_pick, d_rows).astype(bf16)
    d_rows_own = contract_rows(own_pick, d_rows)
    tokens_grad = (d_res_one + d_rows_own + swap(d_rows_sent, "seq", 1).astype(f32)).astype(bf16)
    bias_sums = jnp.sum(d_joint.astype(f32), axis=0)
    spread = lambda vector: lax.dynamic_update_slice(
        jnp.zeros((width,), f32), vector, (side * local_width,)
    ).reshape(groups, piece)
    late = jnp.concatenate(
        [spread(bias_sums[:local_width]), spread(bias_sums[2 * local_width :])], axis=1
    )
    late = reduce_blocks(late[:, None], False, f32)
    late = (late + swap(late, "seq", 1))[0]
    own_part = reduce_blocks(grad_w_qkv.reshape(groups, piece, -1), False, bf16)
    other_part = swap(own_part, "seq", 1)
    first = jnp.where(side == 0, own_part, other_part).reshape(piece, 3, 1, local_width)
    second = jnp.where(side == 0, other_part, own_part).reshape(piece, 3, 1, local_width)
    out_qkv = jnp.concatenate([first, second], axis=2).reshape(piece, 3 * width)
    take = lambda k: vectors[k * piece : (k + 1) * piece]
    return (
        normed_two.astype(bf16)[None],
        raw_buf[None],
        tokens_grad[None],
        dprior_buf[None],
        out_qkv.astype(f32),
        out_out.astype(f32),
        out_in.astype(f32),
        out_back.astype(f32),
        late[:piece],
        late[piece:],
        take(0),
        take(1),
        take(2),
        vectors[6 * piece : 10 * piece],
        take(3),
        take(4),
        take(5),
        rms,
    )


def solution(mesh):
    shard = P("fsdp", "seq", None)
    heads = P("fsdp", "seq", None, None)
    mat = P("fsdp", None)
    vec = P("fsdp")
    return jax.shard_map(
        body,
        mesh=mesh,
        in_specs=(shard, heads, vec, mat, shard) + (mat,) * 4 + (vec,) * 9,
        out_specs=(shard, heads, shard, heads) + (mat,) * 4 + (vec,) * 9 + (P(),),
        check_vma=False,
    )
```

```python
import functools
import math

import jax
import jax.numpy as jnp
from jax import lax
from jax.experimental import pallas as pl
from jax.experimental.pallas import tpu as pltpu
from jax.sharding import PartitionSpec as P

HD = 64
eps_norm = 1e-05
masked_fill = -1e30
f32 = jnp.float32
bf16 = jnp.bfloat16
FIVE_SEQ = 3
BACK_SEQ = 2

NT = (((1,), (1,)), ((), ()))
TN = (((0,), (0,)), ((), ()))


def mm(left, right, dims=(((1,), (0,)), ((), ()))):
    return lax.dot_general(left, right, dims, preferred_element_type=f32)


def bits_of(count):
    return [1 << k for k in range(count.bit_length() - 1)]


def swap(value, axis, bit):
    count = lax.axis_size(axis)
    return lax.ppermute(value, axis, [(i, i ^ bit) for i in range(count)])


def gather_blocks(shard, axis):
    me = lax.axis_index(axis)
    held = shard[None]
    for bit in reversed(bits_of(lax.axis_size(axis))):
        other = swap(held, axis, bit)
        high = (me & bit) != 0
        first = jnp.where(high, other, held)
        second = jnp.where(high, held, other)
        held = jnp.stack([first, second], axis=1).reshape((-1,) + shard.shape)
    return held


def gather_halves(shard, early):
    side = lax.axis_index("seq")
    half = shard.shape[2] // 2
    held = lax.dynamic_slice_in_dim(shard, side * half, half, 2)[None, :, None]
    stages = list(reversed(bits_of(lax.axis_size("fsdp"))))[:-1]
    codes = [0]
    for step, bit in enumerate(stages + [0]):
        if step == min(early, len(stages)):
            held = jnp.concatenate([held, swap(held, "seq", 1)], axis=0)
        if bit:
            held = jnp.concatenate([held, swap(held, "fsdp", bit)], axis=2)
            codes = codes + [code ^ bit for code in codes]
    return held, swap(held, "fsdp", 1), codes


def sort_pieces(own, other, codes):
    me = lax.axis_index("fsdp")
    side = lax.axis_index("seq")
    count = 2 * len(codes)
    both = jnp.concatenate([own, other], axis=2)
    place = [0] * count
    for t, code in enumerate(codes):
        place[code] = t
        place[code ^ 1] = t + len(codes)
    index = jnp.take(jnp.array(place, jnp.int32), jnp.arange(count) ^ me)
    both = jnp.take(both, index, axis=2)
    return jnp.where(
        side == 0,
        jnp.concatenate([both[0], both[1]], -1),
        jnp.concatenate([both[1], both[0]], -1),
    )


def reduce_blocks(parts, seq_at):
    me = lax.axis_index("fsdp")
    side = lax.axis_index("seq")
    width = parts[0].shape[3]
    terms = [parts]

    def pick(which, axis, index, size):
        def one(group):
            cut = []
            for array in group:
                if axis == 1:
                    shape = array.shape
                    array = array.reshape((shape[0], shape[1] // 2, 2) + shape[2:])
                    cut.append(lax.dynamic_index_in_dim(array, index, 2, keepdims=False))
                else:
                    cut.append(lax.dynamic_slice_in_dim(array, index * size, size, 3))
            return jnp.concatenate(cut, 0) if len(cut) > 1 else cut[0]

        picked = [one(group) for group in terms]
        if len(picked) == 1:
            return picked[0]
        return (picked[0].astype(f32) + picked[1].astype(f32)).astype(bf16)

    stages = [("fsdp", bit) for bit in bits_of(lax.axis_size("fsdp"))]
    if seq_at is not None:
        stages.insert(seq_at, ("seq", 1))
    for axis, bit in stages:
        if axis == "fsdp":
            mine = ((me & bit) != 0).astype(jnp.int32)
            sent = pick(None, 1, 1 - mine, None)
            kept = pick(None, 1, mine, None)
        else:
            sent = pick(None, 3, 1 - side, width // 2)
            kept = pick(None, 3, side, width // 2)
        terms = [[kept], [swap(sent, axis, bit)]]
    own = (terms[0][0].astype(f32) + terms[1][0].astype(f32)).astype(bf16)[:, 0]
    if seq_at is None:
        return own
    other = swap(own, "seq", 1)
    return jnp.where(
        side == 0, jnp.concatenate([own, other], 2), jnp.concatenate([other, own], 2)
    )


def sum_all(vectors):
    for bit in bits_of(lax.axis_size("fsdp")):
        vectors = vectors + swap(vectors, "fsdp", bit)
    return vectors + swap(vectors, "seq", 1)


def attend_kernel(length_ref, q_ref, k_ref, v_ref, prior_ref, raw_ref, prob_ref, ctx_ref):
    keys = k_ref.shape[0]
    lane = lax.broadcasted_iota(jnp.int32, (1, 2 * HD), 1)
    seen = lax.broadcasted_iota(jnp.int32, (1, keys), 1) < length_ref[0]
    q = q_ref[...] * jnp.asarray(1.0 / math.sqrt(HD), bf16)
    k = k_ref[...]
    v = v_ref[...]
    parts = []
    for h in range(2):
        mine = (lane >= HD) if h else (lane < HD)
        scores = mm(jnp.where(mine, q, jnp.zeros_like(q)), k, NT) + prior_ref[h].astype(f32)
        raw_ref[h] = scores.astype(bf16)
        masked = jnp.where(seen, scores, masked_fill)
        largest = jnp.max(masked, axis=-1, keepdims=True)
        exponent = jnp.exp(masked - largest)
        inverse = 1.0 / jnp.sum(exponent, axis=-1, keepdims=True)
        prob = (exponent * inverse).astype(bf16)
        prob_ref[h] = prob
        parts.append(mm(prob, v))
    ctx_ref[...] = jnp.where(lane < HD, parts[0], parts[1]).astype(bf16)


def attend(joint, prior, length, block):
    heads, total, _ = prior.shape
    pairs = heads // 2
    wide = 2 * HD
    square = pl.BlockSpec((2, block, total), lambda t, i, *_: (t, i, 0))
    return pl.pallas_call(
        attend_kernel,
        grid_spec=pltpu.PrefetchScalarGridSpec(
            num_scalar_prefetch=1,
            grid=(pairs, total // block),
            in_specs=[
                pl.BlockSpec((block, wide), lambda t, i, *_: (i, t)),
                pl.BlockSpec((total, wide), lambda t, i, *_: (0, pairs + t)),
                pl.BlockSpec((total, wide), lambda t, i, *_: (0, 2 * pairs + t)),
                square,
            ],
            out_specs=[square, square, pl.BlockSpec((block, wide), lambda t, i, *_: (i, t))],
        ),
        out_shape=[
            jax.ShapeDtypeStruct(prior.shape, bf16),
            jax.ShapeDtypeStruct(prior.shape, bf16),
            jax.ShapeDtypeStruct((total, heads * HD), bf16),
        ],
        cost_estimate=pl.CostEstimate(
            flops=8 * heads * HD * total * total,
            transcendentals=heads * total * total,
            bytes_accessed=6 * heads * total * total,
        ),
        compiler_params=pltpu.CompilerParams(vmem_limit_bytes=56 << 20),
        name="attend",
    )(length, joint, joint, joint, prior)


def attend_back_kernel(q_ref, k_ref, v_ref, dc_ref, prob_ref, dprior_ref, dq_ref, dk_ref, dv_ref, dk_acc, dv_acc):
    step = pl.program_id(1)
    lane = lax.broadcasted_iota(jnp.int32, (1, 2 * HD), 1)
    scale = 1.0 / math.sqrt(HD)
    q = q_ref[...]
    k = k_ref[...]
    v = v_ref[...]
    dc = dc_ref[...]

    @pl.when(step == 0)
    def _():
        dk_acc[...] = jnp.zeros_like(dk_acc)
        dv_acc[...] = jnp.zeros_like(dv_acc)

    dq, dk, dv = [], [], []
    for h in range(2):
        mine = (lane >= HD) if h else (lane < HD)
        prob = prob_ref[h]
        wide = prob.astype(f32)
        d_prob = mm(jnp.where(mine, dc, jnp.zeros_like(dc)), v, NT)
        row_term = jnp.sum(wide * d_prob, axis=-1, keepdims=True)
        d_scores = (wide * (d_prob - row_term)).astype(bf16)
        dprior_ref[h] = d_scores
        dq.append(mm(d_scores, k))
        dk.append(mm(d_scores, q, TN))
        dv.append(mm(prob, dc, TN))
    first = lane < HD
    dq_ref[...] = (jnp.where(first, dq[0], dq[1]) * scale).astype(bf16)
    dk_acc[...] += jnp.where(first, dk[0], dk[1])
    dv_acc[...] += jnp.where(first, dv[0], dv[1])

    @pl.when(step == pl.num_programs(1) - 1)
    def _():
        dk_ref[...] = (dk_acc[...] * scale).astype(bf16)
        dv_ref[...] = dv_acc[...].astype(bf16)


def attend_back(joint, d_context, prob, block):
    heads, total, _ = prob.shape
    pairs = heads // 2
    wide = 2 * HD
    square = pl.BlockSpec((2, block, total), lambda t, i: (t, i, 0))
    rows = pl.BlockSpec((block, wide), lambda t, i: (i, t))
    whole = pl.BlockSpec((total, wide), lambda t, i: (0, t))
    thin = jax.ShapeDtypeStruct((total, heads * HD), bf16)
    return pl.pallas_call(
        attend_back_kernel,
        grid=(pairs, total // block),
        in_specs=[
            rows,
            pl.BlockSpec((total, wide), lambda t, i: (0, pairs + t)),
            pl.BlockSpec((total, wide), lambda t, i: (0, 2 * pairs + t)),
            rows,
            square,
        ],
        out_specs=[square, rows, whole, whole],
        out_shape=[jax.ShapeDtypeStruct(prob.shape, bf16), thin, thin, thin],
        scratch_shapes=[pltpu.VMEM((total, wide), f32)] * 2,
        cost_estimate=pl.CostEstimate(
            flops=16 * heads * HD * total * total,
            transcendentals=0,
            bytes_accessed=4 * heads * total * total,
        ),
        compiler_params=pltpu.CompilerParams(vmem_limit_bytes=56 << 20),
        name="attend_back",
    )(joint, joint, joint, d_context, prob)


def feed_kernel(
    where_ref, ctx_own_ref, ctx_got_ref, tokens_ref, cot_ref, valid_ref, vec_ref, bias_in_ref,
    *refs, codes, chunks,
):
    if codes is None:
        (five_ref, back_ref), refs = refs[:2], refs[2:]
    else:
        (five_own, five_other, back_own, back_other), refs = refs[:4], refs[4:]
    (out_ref, low_ref, act_ref, d_branch_ref, d_inner_ref, d_att_ref, d_res_ref,
     d_own_ref, d_sent_ref, sums_ref, w_five, w_back, slope, sems) = refs
    me = where_ref[0]
    side = where_ref[1]
    width = tokens_ref.shape[1]
    half = width // 2

    def copies(kind):
        made = []
        if codes is None:
            if kind == "back":
                return [pltpu.make_async_copy(back_ref, w_back, sems.at[1])]
            ks = [chunks] if kind == "out" else list(range(chunks))
            sem = sems.at[2] if kind == "out" else sems.at[0]
            return [pltpu.make_async_copy(five_ref.at[k], w_five.at[k], sem) for k in ks]
        for b in range(2):
            for a in range(2):
                for t, code in enumerate(codes):
                    block = me ^ (code ^ b)
                    column = pl.multiple_of((side ^ a) * half, 128)
                    if kind == "back":
                        source = (back_own, back_other)[b]
                        r = source.shape[3]
                        made.append(pltpu.make_async_copy(
                            source.at[a, 0, t],
                            w_back.at[pl.ds(pl.multiple_of(block * r, 16), r), pl.ds(column, half)],
                            sems.at[1]))
                    else:
                        source = (five_own, five_other)[b]
                        r = source.shape[3]
                        rows = pl.ds(pl.multiple_of(block * r, 16), r)
                        if kind == "out":
                            made.append(pltpu.make_async_copy(
                                source.at[a, chunks, t],
                                w_five.at[chunks, rows, pl.ds(column, half)], sems.at[2]))
                        else:
                            made.append(pltpu.make_async_copy(
                                source.at[a, pl.ds(0, chunks), t],
                                w_five.at[pl.ds(0, chunks), rows, pl.ds(column, half)], sems.at[0]))
        return made

    groups = {kind: copies(kind) for kind in ("out", "in", "back")}
    for kind in ("out", "in", "back"):
        for copy in groups[kind]:
            copy.start()
    vec = vec_ref[...]
    proj_bias, first_gain, first_shift, outer_bias, second_gain, second_shift = (
        vec[k : k + 1] for k in range(2, 8)
    )
    own_rows = pl.ds(pl.multiple_of(side * half, 128), half)
    other_rows = pl.ds(pl.multiple_of((1 - side) * half, 128), half)
    valid = valid_ref[...]
    for copy in groups["out"]:
        copy.wait()
    attended = (
        mm(ctx_own_ref[...], w_five[chunks, own_rows, :])
        + mm(ctx_got_ref[...], w_five[chunks, other_rows, :])
        + proj_bias
    )
    tokens_f = tokens_ref[...].astype(f32)

    def stat(row, values):
        total = jnp.sum(jnp.sum(values, axis=0, keepdims=True), axis=1, keepdims=True)
        sums_ref[row : row + 1, :] = jnp.broadcast_to(total, (1, width))

    def column_sum(row, values):
        sums_ref[row : row + 1, :] = jnp.sum(values, axis=0, keepdims=True)

    def normalize(values):
        centered = values - jnp.mean(values, axis=-1, keepdims=True)
        spread = lax.rsqrt(jnp.mean(centered * centered, axis=-1, keepdims=True) + eps_norm)
        return centered * spread, spread

    def normalize_back(grad, gain, normal, spread):
        e = grad * gain
        return spread * (
            e - jnp.mean(e, axis=-1, keepdims=True)
            - normal * jnp.mean(e * normal, axis=-1, keepdims=True)
        )

    stat(10, valid * tokens_f * tokens_f)
    stat(11, valid * attended * attended)
    stat(13, valid * jnp.ones((1, 128), f32) * (1.0 / 128.0))
    normal_one, spread_one = normalize(tokens_f + attended)
    hidden = normal_one * first_gain + first_shift
    hidden_low = hidden.astype(bf16)
    low_ref[...] = hidden_low
    for copy in groups["in"]:
        copy.wait()
    branch = jnp.zeros_like(hidden)
    for c in range(chunks):
        inner = mm(hidden_low, w_five[c]) + bias_in_ref[c : c + 1, :]
        below = 0.5 + 0.5 * lax.erf(inner * math.sqrt(0.5))
        slope[c] = below + inner * (jnp.exp(inner * inner * -0.5) * (1.0 / math.sqrt(2.0 * math.pi)))
        activated = (inner * below).astype(bf16)
        columns = slice(c * width, (c + 1) * width)
        act_ref[:, columns] = activated
        if c == 0:
            for copy in groups["back"]:
                copy.wait()
        branch = branch + mm(activated, w_back[columns, :])
    branch = branch + outer_bias
    stat(12, valid * branch * branch)
    normal_two, spread_two = normalize(hidden + branch)
    out_ref[...] = (normal_two * second_gain + second_shift).astype(bf16)
    d_output = cot_ref[...].astype(f32) * valid
    column_sum(4, d_output * normal_two)
    column_sum(5, d_output)
    d_hidden = normalize_back(d_output, second_gain, normal_two, spread_two)
    d_branch = d_hidden.astype(bf16)
    d_branch_ref[...] = d_branch
    column_sum(3, d_branch.astype(f32))
    for c in range(chunks):
        columns = slice(c * width, (c + 1) * width)
        d_inner = (mm(d_branch, w_back[columns, :], NT) * slope[c]).astype(bf16)
        d_inner_ref[c] = d_inner
        column_sum(6 + c, d_inner.astype(f32))
        d_hidden = d_hidden + mm(d_inner, w_five[c], NT)
    column_sum(1, d_hidden * normal_one)
    column_sum(2, d_hidden)
    d_res = normalize_back(d_hidden, first_gain, normal_one, spread_one)
    d_res_ref[...] = d_res
    d_att = d_res.astype(bf16)
    d_att_ref[...] = d_att
    column_sum(0, d_att.astype(f32))
    d_sent_ref[...] = mm(d_att, w_five[chunks, other_rows, :], NT).astype(bf16)
    d_own_ref[...] = mm(d_att, w_five[chunks, own_rows, :], NT).astype(bf16)


def feed(where, ctx_own, ctx_got, tokens, cot, valid, vec, bias_in, weights, codes):
    rows, width = tokens.shape
    chunks = bias_in.shape[0]
    half = width // 2
    vmem = pl.BlockSpec(memory_space=pltpu.VMEM)
    hbm = pl.BlockSpec(memory_space=pl.ANY)
    flat = lambda *shape: jax.ShapeDtypeStruct(shape, bf16)
    return pl.pallas_call(
        functools.partial(feed_kernel, codes=codes, chunks=chunks),
        in_specs=[pl.BlockSpec(memory_space=pltpu.SMEM)] + [vmem] * 7 + [hbm] * len(weights),
        out_specs=[vmem] * 10,
        out_shape=[
            flat(rows, width),
            flat(rows, width),
            flat(rows, chunks * width),
            flat(rows, width),
            flat(chunks, rows, width),
            flat(rows, width),
            jax.ShapeDtypeStruct((rows, width), f32),
            flat(rows, half),
            flat(rows, half),
            jax.ShapeDtypeStruct((16, width), f32),
        ],
        scratch_shapes=[
            pltpu.VMEM((chunks + 1, width, width), bf16),
            pltpu.VMEM((chunks * width, width), bf16),
            pltpu.VMEM((chunks, rows, width), f32),
            pltpu.SemaphoreType.DMA((3,)),
        ],
        cost_estimate=pl.CostEstimate(
            flops=2 * rows * width * width * (4 * chunks + 2),
            transcendentals=2 * rows * width * chunks,
            bytes_accessed=2 * width * width * (2 * chunks + 1) + 2 * rows * width * (2 * chunks + 8),
        ),
        compiler_params=pltpu.CompilerParams(vmem_limit_bytes=60 << 20),
        name="feed",
    )(where, ctx_own, ctx_got, tokens, cot, valid, vec, bias_in, *weights)


def body(
    tokens, prior_logits, lengths, order, cotangent, w_qkv, w_out, w_in, w_back,
    bias_q, bias_v, bias_o, gain_one, shift_one, bias_in, bias_back, gain_two, shift_two,
):
    side = lax.axis_index("seq")
    me = lax.axis_index("fsdp")
    groups = lax.axis_size("fsdp")
    rows = tokens[0]
    local_count, width = rows.shape
    total = 2 * local_count
    heads_local = prior_logits.shape[1]
    local_width = heads_local * HD
    piece = bias_q.shape[0]
    chunks = w_in.shape[1] // width

    other_rows = swap(rows, "seq", 1)
    own_qkv = lax.dynamic_index_in_dim(
        w_qkv.reshape(piece, 3, 2, local_width), side, 2, keepdims=False
    ).reshape(piece, 3 * local_width)
    small = jnp.concatenate(
        [bias_q, bias_v, bias_o, gain_one, shift_one, bias_back, gain_two, shift_two, bias_in]
    )[None]
    small_all = gather_blocks(small, "fsdp")[:, 0].astype(f32)
    vec = small_all[:, : 8 * piece].reshape(groups, 8, piece).transpose(1, 0, 2).reshape(8, width)
    inner_bias = small_all[:, 8 * piece :].reshape(chunks, width)
    qkv_weight = gather_blocks(own_qkv, "fsdp").reshape(width, 3 * local_width)
    five = jnp.concatenate(
        [w_in[:, c * width : (c + 1) * width][None] for c in range(chunks)] + [w_out[None]], 0
    )
    five_own, five_other, codes = gather_halves(five, FIVE_SEQ)
    back_own, back_other, _ = gather_halves(w_back[None], BACK_SEQ)
    if piece % 16 == 0:
        weights = (five_own, five_other, back_own, back_other)
    else:
        weights = (
            sort_pieces(five_own, five_other, codes).reshape(chunks + 1, width, width),
            sort_pieces(back_own, back_other, codes).reshape(chunks * width, width),
        )
        codes = None

    order_row = order[0]
    length = lengths[0]
    own_order = lax.dynamic_slice_in_dim(order_row, side * local_count, local_count)
    other_order = lax.dynamic_slice_in_dim(order_row, (1 - side) * local_count, local_count)
    positions = jnp.arange(total, dtype=jnp.int32)
    own_pick = (positions[:, None] == own_order[None, :]).astype(bf16)
    other_pick = (positions[:, None] == other_order[None, :]).astype(bf16)

    def to_positions(own, other):
        return (mm(own_pick, own) + mm(other_pick, other)).astype(bf16)

    placed_rows = to_positions(rows, other_rows)
    own_cols = lambda vector: lax.dynamic_slice_in_dim(vector, side * local_width, local_width)
    joint_bias = jnp.concatenate(
        [own_cols(vec[0]), jnp.zeros((local_width,), f32), own_cols(vec[1])]
    )
    joint = (mm(placed_rows, qkv_weight) + joint_bias).astype(bf16)
    raw_buf, prob_buf, context_pos = attend(joint, prior_logits[0], lengths, min(256, total))

    context_sent = mm(other_pick, context_pos, TN).astype(bf16)
    context_own = mm(own_pick, context_pos, TN).astype(bf16)
    context_got = swap(context_sent, "seq", 1)
    valid_rows = (own_order < length).astype(f32)[:, None]
    where = jnp.stack([me, side]).astype(jnp.int32)
    (out_rows, hidden_low, activated, d_branch, d_inner, d_attended, d_res_one,
     d_context_own, d_context_sent, sums) = feed(
        where, context_own, context_got, rows, cotangent[0], valid_rows, vec, inner_bias, weights, codes
    )
    d_context_got = swap(d_context_sent, "seq", 1)
    d_context_pos = to_positions(d_context_own, d_context_got)

    grad_w_back = mm(activated, d_branch, TN).astype(bf16)
    grad_w_in = jnp.stack([mm(hidden_low, d_inner[c], TN).astype(bf16) for c in range(chunks)])
    context = jnp.where(
        side == 0,
        jnp.concatenate([context_own, context_got], 1),
        jnp.concatenate([context_got, context_own], 1),
    )
    grad_w_out = mm(context, d_attended, TN).astype(bf16)
    out_back = reduce_blocks([grad_w_back.reshape(1, groups, -1, width)], 1)[0]
    out_five = reduce_blocks(
        [grad_w_in.reshape(chunks, groups, piece, width), grad_w_out.reshape(1, groups, piece, width)], 2
    )
    sums = sum_all(sums)
    rms = jnp.sqrt(sums[10:13, 0] / (sums[13, 0] * width))
    own_sums = lax.dynamic_slice_in_dim(sums[:6], me * piece, piece, 1)
    own_inner = lax.dynamic_slice_in_dim(
        sums[6 : 6 + chunks].reshape(-1), me * chunks * piece, chunks * piece
    )

    dprior_buf, d_q, d_k, d_v = attend_back(joint, d_context_pos, prob_buf, min(256, total))
    d_joint = jnp.concatenate([d_q, d_k, d_v], axis=1)
    grad_w_qkv = mm(placed_rows, d_joint, TN).astype(bf16)
    own_part = reduce_blocks([grad_w_qkv.reshape(1, groups, piece, -1)], None)[0]
    d_rows = mm(d_joint, qkv_weight, NT).astype(bf16)
    d_rows_sent = mm(other_pick, d_rows, TN).astype(bf16)
    d_rows_own = mm(own_pick, d_rows, TN)
    tokens_grad = (d_res_one + d_rows_own + swap(d_rows_sent, "seq", 1).astype(f32)).astype(bf16)
    spread = lambda part: lax.dynamic_update_slice(
        jnp.zeros((width,), f32), jnp.sum(part.astype(f32), axis=0), (side * local_width,)
    )
    late = sum_all(jnp.stack([spread(d_q), spread(d_v)]))
    late = lax.dynamic_slice_in_dim(late, me * piece, piece, 1)
    other_part = swap(own_part, "seq", 1)
    first = jnp.where(side == 0, own_part, other_part).reshape(piece, 3, 1, local_width)
    second = jnp.where(side == 0, other_part, own_part).reshape(piece, 3, 1, local_width)
    out_qkv = jnp.concatenate([first, second], axis=2).reshape(piece, 3 * width)
    out_in = out_five[:chunks].transpose(1, 0, 2).reshape(piece, chunks * width)
    return (
        out_rows[None],
        raw_buf[None],
        tokens_grad[None],
        dprior_buf[None],
        out_qkv.astype(f32),
        out_five[chunks].astype(f32),
        out_in.astype(f32),
        out_back.astype(f32),
        late[0],
        late[1],
        own_sums[0],
        own_sums[1],
        own_sums[2],
        own_inner,
        own_sums[3],
        own_sums[4],
        own_sums[5],
        rms,
    )


def solution(mesh):
    shard = P("fsdp", "seq", None)
    heads = P("fsdp", "seq", None, None)
    mat = P("fsdp", None)
    vec = P("fsdp")
    return jax.shard_map(
        body,
        mesh=mesh,
        in_specs=(shard, heads, vec, mat, shard) + (mat,) * 4 + (vec,) * 9,
        out_specs=(shard, heads, shard, heads) + (mat,) * 4 + (vec,) * 9 + (P(),),
        check_vma=False,
    )
```

```python
import functools
import math

import jax
import jax.numpy as jnp
from jax import lax
from jax.experimental import pallas as pl
from jax.experimental.pallas import tpu as pltpu
from jax.sharding import PartitionSpec as P

HD = 64
eps_norm = 1e-05
masked_fill = -1e30
f32 = jnp.float32
bf16 = jnp.bfloat16

NT = (((1,), (1,)), ((), ()))
TN = (((0,), (0,)), ((), ()))


def mm(left, right, dims=(((1,), (0,)), ((), ()))):
    return lax.dot_general(left, right, dims, preferred_element_type=f32)


def bits_of(count):
    return [1 << k for k in range(count.bit_length() - 1)]


def swap(value, axis, bit):
    count = lax.axis_size(axis)
    return lax.ppermute(value, axis, [(i, i ^ bit) for i in range(count)])


def gather_blocks(shard, axis):
    me = lax.axis_index(axis)
    held = shard[None]
    for bit in reversed(bits_of(lax.axis_size(axis))):
        other = swap(held, axis, bit)
        high = (me & bit) != 0
        first = jnp.where(high, other, held)
        second = jnp.where(high, held, other)
        held = jnp.stack([first, second], axis=1).reshape((-1,) + shard.shape)
    return held


def tie(value, *others):
    return lax.optimization_barrier((value,) + others)[0]


def chain_orders():
    rest = list(reversed(bits_of(lax.axis_size("fsdp"))))[1:-1]
    up = rest[::-1]
    return [up + ["seq"], rest[:-1] + ["seq"] + rest[-1:], ["seq"] + up]


def extend(held, stage):
    axis, bit, dim = ("seq", 1, 0) if stage == "seq" else ("fsdp", stage, 2)
    return jnp.concatenate([held, swap(held, axis, bit)], axis=dim)


def codes_for(order):
    codes = [0]
    for bit in order:
        if bit != "seq":
            codes = codes + [code ^ bit for code in codes]
    return codes


def sort_pieces(own, other, codes):
    me = lax.axis_index("fsdp")
    side = lax.axis_index("seq")
    count = 2 * len(codes)
    both = jnp.concatenate([own, other], axis=2)
    place = [0] * count
    for t, code in enumerate(codes):
        place[code] = t
        place[code ^ 1] = t + len(codes)
    index = jnp.take(jnp.array(place, jnp.int32), jnp.arange(count) ^ me)
    both = jnp.take(both, index, axis=2)
    return jnp.where(
        side == 0,
        jnp.concatenate([both[0], both[1]], -1),
        jnp.concatenate([both[1], both[0]], -1),
    )


class Reduction:
    def __init__(self, terms, order):
        self.terms = terms
        self.order = order
        self.me = lax.axis_index("fsdp")
        self.side = lax.axis_index("seq")

    def pick(self, own):
        stage = self.order[0]
        picked = []
        for array in self.terms:
            if stage == "seq":
                size = array.shape[3] // 2
                index = self.side if own else 1 - self.side
                picked.append(lax.dynamic_slice_in_dim(array, index * size, size, 3))
            else:
                low = sum(1 for b in self.order if b != "seq" and b < stage)
                shape = array.shape
                array = array.reshape(
                    (shape[0], shape[1] >> (low + 1), 2, 1 << low) + shape[2:]
                )
                mine = ((self.me & stage) != 0).astype(jnp.int32)
                array = lax.dynamic_index_in_dim(
                    array, mine if own else 1 - mine, 2, keepdims=False
                )
                picked.append(array.reshape((shape[0], shape[1] // 2) + shape[2:]))
        total = picked[0].astype(f32)
        for other in picked[1:]:
            total = total + other.astype(f32)
        return total.astype(bf16)

    def sent(self):
        return self.pick(False)

    def launch(self, sent):
        kept = self.pick(True)
        stage = self.order[0]
        self.order = self.order[1:]
        axis, bit = ("seq", 1) if stage == "seq" else ("fsdp", stage)
        self.terms = [kept, swap(sent, axis, bit)]


def sum_all(vectors):
    for bit in bits_of(lax.axis_size("fsdp")):
        vectors = vectors + swap(vectors, "fsdp", bit)
    return vectors + swap(vectors, "seq", 1)


def pack_kernel(where_ref, *refs):
    w_qkv, w_out, w_in, w_back = refs[:4]
    vectors, (qkv_ref, nine_ref, small_ref) = refs[4:13], refs[13:]
    r, width = w_out.shape
    half = width // 2
    columns = pl.ds(pl.multiple_of(where_ref[1] * half, 128), half)
    nine_ref[0, 0] = w_out[:, columns]
    for c in range(4):
        nine_ref[0, 1 + c] = w_in[:, pl.ds(pl.multiple_of(c * width + where_ref[1] * half, 128), half)]
        nine_ref[0, 5 + c] = w_back[c * r : (c + 1) * r, columns]
    for kind in range(3):
        for t in range(3):
            start = kind * width + where_ref[1] * half + t * 128
            qkv_ref[:, (3 * t + kind) * 128 : (3 * t + kind + 1) * 128] = w_qkv[
                :, pl.ds(pl.multiple_of(start, 128), 128)
            ]
    small_ref[...] = jnp.zeros_like(small_ref)
    for k, vector in enumerate(vectors):
        small_ref[k : k + 1, : vector.shape[1]] = vector[...].astype(f32)


def pack(where, w_qkv, w_out, w_in, w_back, vectors):
    r, width = w_out.shape
    vmem = pl.BlockSpec(memory_space=pltpu.VMEM)
    return pl.pallas_call(
        pack_kernel,
        in_specs=[pl.BlockSpec(memory_space=pltpu.SMEM)] + [vmem] * 13,
        out_specs=[vmem] * 3,
        out_shape=[
            jax.ShapeDtypeStruct((r, 3 * width // 2), bf16),
            jax.ShapeDtypeStruct((1, 9, r, width // 2), bf16),
            jax.ShapeDtypeStruct((16, 256), f32),
        ],
        name="pack",
    )(where, w_qkv, w_out, w_in, w_back, *[vector[None] for vector in vectors])


def attend_kernel(length_ref, q_ref, k_ref, v_ref, prior_ref, *refs):
    raw_ref, prob_ref, ctx_ref = refs[-3:]
    keys = k_ref.shape[0]
    lane = lax.broadcasted_iota(jnp.int32, (1, 2 * HD), 1)
    seen = lax.broadcasted_iota(jnp.int32, (1, keys), 1) < length_ref[0]
    q = q_ref[...] * jnp.asarray(1.0 / math.sqrt(HD), bf16)
    k = k_ref[...]
    v = v_ref[...]
    parts = []
    for h in range(2):
        mine = (lane >= HD) if h else (lane < HD)
        scores = mm(jnp.where(mine, q, jnp.zeros_like(q)), k, NT) + prior_ref[h].astype(f32)
        raw_ref[h] = scores.astype(bf16)
        masked = jnp.where(seen, scores, masked_fill)
        largest = jnp.max(masked, axis=-1, keepdims=True)
        exponent = jnp.exp(masked - largest)
        inverse = 1.0 / jnp.sum(exponent, axis=-1, keepdims=True)
        prob = (exponent * inverse).astype(bf16)
        prob_ref[h] = prob
        parts.append(mm(prob, v))
    ctx_ref[...] = jnp.where(lane < HD, parts[0], parts[1]).astype(bf16)


def attend(joint, prior, length, block, pair, held):
    heads, total, _ = prior.shape
    wide = 2 * HD
    square = pl.BlockSpec((2, block, total), lambda i, *_: (pair, i, 0))
    hbm = pl.BlockSpec(memory_space=pl.ANY)
    return pl.pallas_call(
        attend_kernel,
        grid_spec=pltpu.PrefetchScalarGridSpec(
            num_scalar_prefetch=1,
            grid=(total // block,),
            in_specs=[
                pl.BlockSpec((block, wide), lambda i, *_: (i, 3 * pair)),
                pl.BlockSpec((total, wide), lambda i, *_: (0, 3 * pair + 1)),
                pl.BlockSpec((total, wide), lambda i, *_: (0, 3 * pair + 2)),
                square,
            ]
            + [hbm] * len(held),
            out_specs=[square, square, pl.BlockSpec((block, wide), lambda i, *_: (i, 0))],
        ),
        out_shape=[
            jax.ShapeDtypeStruct(prior.shape, bf16),
            jax.ShapeDtypeStruct(prior.shape, bf16),
            jax.ShapeDtypeStruct((total, wide), bf16),
        ],
        input_output_aliases={5 + k: k for k in range(len(held))},
        cost_estimate=pl.CostEstimate(
            flops=16 * HD * total * total,
            transcendentals=2 * total * total,
            bytes_accessed=12 * total * total,
        ),
        compiler_params=pltpu.CompilerParams(vmem_limit_bytes=56 << 20),
        name="attend",
    )(length, joint, joint, joint, prior, *held)


def attend_back_kernel(q_ref, k_ref, v_ref, dc_ref, prob_ref, dprior_ref, dj_ref, bias_ref, dk_acc, dv_acc):
    step = pl.program_id(1)
    block = q_ref.shape[0]
    wide_lanes = 2 * HD
    lane = lax.broadcasted_iota(jnp.int32, (1, wide_lanes), 1)
    scale = 1.0 / math.sqrt(HD)
    q = q_ref[...]
    k = k_ref[...]
    v = v_ref[...]
    dc = dc_ref[...]

    @pl.when(step == 0)
    def _():
        dk_acc[...] = jnp.zeros_like(dk_acc)
        dv_acc[...] = jnp.zeros_like(dv_acc)
        bias_ref[...] = jnp.zeros_like(bias_ref)

    dq, dk, dv = [], [], []
    for h in range(2):
        mine = (lane >= HD) if h else (lane < HD)
        prob = prob_ref[h]
        wide = prob.astype(f32)
        d_prob = mm(jnp.where(mine, dc, jnp.zeros_like(dc)), v, NT)
        row_term = jnp.sum(wide * d_prob, axis=-1, keepdims=True)
        d_scores = (wide * (d_prob - row_term)).astype(bf16)
        dprior_ref[h] = d_scores
        dq.append(mm(d_scores, k))
        dk.append(mm(d_scores, q, TN))
        dv.append(mm(prob, dc, TN))
    first = lane < HD
    d_query = (jnp.where(first, dq[0], dq[1]) * scale).astype(bf16)
    dj_ref[pl.ds(pl.multiple_of(step * block, block), block), 0:wide_lanes] = d_query
    bias_ref[0, 0:1, :] += jnp.sum(d_query.astype(f32), axis=0, keepdims=True)
    dk_acc[...] += jnp.where(first, dk[0], dk[1])
    dv_acc[...] += jnp.where(first, dv[0], dv[1])

    @pl.when(step == pl.num_programs(1) - 1)
    def _():
        dj_ref[:, wide_lanes : 2 * wide_lanes] = (dk_acc[...] * scale).astype(bf16)
        d_value = dv_acc[...].astype(bf16)
        dj_ref[:, 2 * wide_lanes : 3 * wide_lanes] = d_value
        bias_ref[0, 1:2, :] = jnp.sum(d_value.astype(f32), axis=0, keepdims=True)


def attend_back(joint, d_context, prob, block):
    heads, total, _ = prob.shape
    pairs = heads // 2
    wide = 2 * HD
    square = pl.BlockSpec((2, block, total), lambda t, i: (t, i, 0))
    return pl.pallas_call(
        attend_back_kernel,
        grid=(pairs, total // block),
        in_specs=[
            pl.BlockSpec((block, wide), lambda t, i: (i, 3 * t)),
            pl.BlockSpec((total, wide), lambda t, i: (0, 3 * t + 1)),
            pl.BlockSpec((total, wide), lambda t, i: (0, 3 * t + 2)),
            pl.BlockSpec((block, wide), lambda t, i: (i, t)),
            square,
        ],
        out_specs=[
            square,
            pl.BlockSpec((total, 3 * wide), lambda t, i: (0, t)),
            pl.BlockSpec((1, 8, wide), lambda t, i: (t, 0, 0)),
        ],
        out_shape=[
            jax.ShapeDtypeStruct(prob.shape, bf16),
            jax.ShapeDtypeStruct((total, 3 * pairs * wide), bf16),
            jax.ShapeDtypeStruct((pairs, 8, wide), f32),
        ],
        scratch_shapes=[pltpu.VMEM((total, wide), f32)] * 2,
        cost_estimate=pl.CostEstimate(
            flops=16 * heads * HD * total * total,
            transcendentals=0,
            bytes_accessed=4 * heads * total * total,
        ),
        compiler_params=pltpu.CompilerParams(vmem_limit_bytes=56 << 20),
        name="attend_back",
    )(joint, joint, joint, d_context, prob)


def grads_kernel(where_ref, *refs):
    ctx_own_refs, ctx_got_refs, refs = refs[:3], refs[3:6], refs[6:]
    d_att_ref, low_ref, d_inner_ref, act_ref, d_branch_ref = refs[:5]
    sent_refs, kept_refs = refs[5:8], refs[8:11]
    odd = (where_ref[0] & 1) == 1
    side = where_ref[1]
    r, width = sent_refs[0].shape[2:]
    groups = 2 * sent_refs[0].shape[1]

    def put(chain, unit, first, blocks):
        blocks = blocks.astype(bf16)
        lower, upper = blocks[:, 0], blocks[:, 1]
        at = pl.ds(first, blocks.shape[0])
        sent_refs[chain][unit, at] = jnp.where(odd, lower, upper)
        kept_refs[chain][unit, at] = jnp.where(odd, upper, lower)

    d_branch = d_branch_ref[...]

    def back(c, carry):
        part = mm(act_ref[:, pl.ds(pl.multiple_of(c * width, 128), width)], d_branch, TN)
        part = part.reshape(groups // 8, 2, 4, r, width)
        put(1, 2, c * (groups // 8), part[:, :, 0])
        for q in range(3):
            put(2, q, c * (groups // 8), part[:, :, 1 + q])
        return carry

    lax.fori_loop(0, 4, back, 0)
    low = low_ref[...]

    def inner(c, carry):
        put(1, c, 0, mm(low, d_inner_ref[2 + c], TN).reshape(groups // 2, 2, r, width))
        put(0, 1 + c, 0, mm(low, d_inner_ref[c], TN).reshape(groups // 2, 2, r, width))
        return carry

    lax.fori_loop(0, 2, inner, 0)
    d_att = d_att_ref[...]
    for refs, start in ((ctx_own_refs, side), (ctx_got_refs, 1 - side)):
        part = mm(jnp.concatenate([ref[...] for ref in refs], 1), d_att, TN)
        put(0, 0, start * (groups // 4), part.reshape(groups // 4, 2, r, width))


def grads(where, ctx_own, ctx_got, d_att, low, d_inner, act, d_branch, groups):
    rows, width = d_att.shape
    vmem = pl.BlockSpec(memory_space=pltpu.VMEM)
    part = jax.ShapeDtypeStruct((3, groups // 2, width // groups, width), bf16)
    return pl.pallas_call(
        grads_kernel,
        in_specs=[pl.BlockSpec(memory_space=pltpu.SMEM)] + [vmem] * 11,
        out_specs=[vmem] * 6,
        out_shape=[part] * 6,
        cost_estimate=pl.CostEstimate(
            flops=18 * rows * width * width,
            transcendentals=0,
            bytes_accessed=18 * width * width + 24 * rows * width,
        ),
        compiler_params=pltpu.CompilerParams(vmem_limit_bytes=60 << 20),
        name="grads",
    )(where, *ctx_own, *ctx_got, d_att, low, d_inner, act, d_branch)


def feed_kernel(
    where_ref, *refs, codes, chunks,
):
    ctx_own_refs, ctx_got_refs, refs = refs[:3], refs[3:6], refs[6:]
    (tokens_ref, cot_ref, valid_ref, vec_ref, bias_in_ref), refs = refs[:5], refs[5:]
    weight_count = 2 if codes is None else 6
    weights, refs = refs[:weight_count], refs[weight_count:]
    (out_ref, low_ref, act_ref, d_branch_ref, d_inner_ref, d_att_ref, d_res_ref,
     d_own_ref, d_sent_ref, sums_ref, w_five, w_back, slope, sems) = refs
    me = where_ref[0]
    side = where_ref[1]
    width = tokens_ref.shape[1]
    half = width // 2

    def copies(chain):
        if codes is None:
            if chain == 2:
                return []
            target = (w_five, w_back)[chain]
            return [pltpu.make_async_copy(weights[chain], target, sems.at[chain])]
        made = []
        r = weights[0].shape[3]
        for b in range(2):
            source = weights[2 * chain + b]
            for a in range(2):
                column = pl.ds(pl.multiple_of((side ^ a) * half, 128), half)
                for t, code in enumerate(codes[chain]):
                    block = me ^ (code ^ b)
                    rows = pl.ds(pl.multiple_of(block * r, 16), r)
                    moves = (
                        ((0, 3, w_five.at[0:3, rows, column]),),
                        ((0, 2, w_five.at[3:5, rows, column]), (2, 1, w_back.at[block, 0:1, :, column])),
                        ((0, 3, w_back.at[block, 1:4, :, column]),),
                    )[chain]
                    for first, count, target in moves:
                        made.append(pltpu.make_async_copy(
                            source.at[a, pl.ds(first, count), t], target, sems.at[chain]))
        return made

    groups = [copies(chain) for chain in range(3)]
    for group in groups:
        for copy in group:
            copy.start()

    def back_rows(c):
        if codes is None:
            return w_back[c * width : (c + 1) * width, :]
        per = w_back.shape[0] // chunks
        return w_back[c * per : (c + 1) * per].reshape(width, width)

    vec = vec_ref[...]
    proj_bias, first_gain, first_shift, outer_bias, second_gain, second_shift = (
        vec[k : k + 1] for k in range(2, 8)
    )
    own_rows = pl.ds(pl.multiple_of(side * half, 128), half)
    other_rows = pl.ds(pl.multiple_of((1 - side) * half, 128), half)
    valid = valid_ref[...]
    for copy in groups[0]:
        copy.wait()
    ctx_own = jnp.concatenate([ref[...] for ref in ctx_own_refs], 1)
    ctx_got = jnp.concatenate([ref[...] for ref in ctx_got_refs], 1)
    attended = (
        mm(ctx_own, w_five[0, own_rows, :]) + mm(ctx_got, w_five[0, other_rows, :]) + proj_bias
    )
    tokens_f = tokens_ref[...].astype(f32)

    def stat(row, values):
        total = jnp.sum(jnp.sum(values, axis=0, keepdims=True), axis=1, keepdims=True)
        sums_ref[row : row + 1, :] = jnp.broadcast_to(total, (1, width))

    def column_sum(row, values):
        sums_ref[row : row + 1, :] = jnp.sum(values, axis=0, keepdims=True)

    def normalize(values):
        centered = values - jnp.mean(values, axis=-1, keepdims=True)
        spread = lax.rsqrt(jnp.mean(centered * centered, axis=-1, keepdims=True) + eps_norm)
        return centered * spread, spread

    def normalize_back(grad, gain, normal, spread):
        e = grad * gain
        return spread * (
            e - jnp.mean(e, axis=-1, keepdims=True)
            - normal * jnp.mean(e * normal, axis=-1, keepdims=True)
        )

    stat(10, valid * tokens_f * tokens_f)
    stat(11, valid * attended * attended)
    stat(13, valid * jnp.ones((1, 128), f32) * (1.0 / 128.0))
    normal_one, spread_one = normalize(tokens_f + attended)
    hidden = normal_one * first_gain + first_shift
    hidden_low = hidden.astype(bf16)
    low_ref[...] = hidden_low
    for copy in groups[1] + groups[2]:
        copy.wait()
    branch = jnp.zeros_like(hidden)
    for c in range(chunks):
        inner = mm(hidden_low, w_five[1 + c]) + bias_in_ref[c : c + 1, :]
        below = 0.5 + 0.5 * lax.erf(inner * math.sqrt(0.5))
        slope[c] = below + inner * (jnp.exp(inner * inner * -0.5) * (1.0 / math.sqrt(2.0 * math.pi)))
        activated = (inner * below).astype(bf16)
        columns = slice(c * width, (c + 1) * width)
        act_ref[:, columns] = activated
        branch = branch + mm(activated, back_rows(c))
    branch = branch + outer_bias
    stat(12, valid * branch * branch)
    normal_two, spread_two = normalize(hidden + branch)
    out_ref[...] = (normal_two * second_gain + second_shift).astype(bf16)
    d_output = cot_ref[...].astype(f32) * valid
    column_sum(4, d_output * normal_two)
    column_sum(5, d_output)
    d_hidden = normalize_back(d_output, second_gain, normal_two, spread_two)
    d_branch = d_hidden.astype(bf16)
    d_branch_ref[...] = d_branch
    column_sum(3, d_branch.astype(f32))
    for c in range(chunks):
        columns = slice(c * width, (c + 1) * width)
        d_inner = (mm(d_branch, back_rows(c), NT) * slope[c]).astype(bf16)
        d_inner_ref[c] = d_inner
        column_sum(6 + c, d_inner.astype(f32))
        d_hidden = d_hidden + mm(d_inner, w_five[1 + c], NT)
    column_sum(1, d_hidden * normal_one)
    column_sum(2, d_hidden)
    d_res = normalize_back(d_hidden, first_gain, normal_one, spread_one)
    d_res_ref[...] = d_res
    d_att = d_res.astype(bf16)
    d_att_ref[...] = d_att
    column_sum(0, d_att.astype(f32))
    d_sent_ref[...] = mm(d_att, w_five[0, other_rows, :], NT).astype(bf16)
    d_own_ref[...] = mm(d_att, w_five[0, own_rows, :], NT).astype(bf16)


def feed(where, ctx_own, ctx_got, tokens, cot, valid, vec, bias_in, weights, codes, groups):
    rows, width = tokens.shape
    chunks = bias_in.shape[0]
    vmem = pl.BlockSpec(memory_space=pltpu.VMEM)
    hbm = pl.BlockSpec(memory_space=pl.ANY)
    flat = lambda *shape: jax.ShapeDtypeStruct(shape, bf16)
    return pl.pallas_call(
        functools.partial(feed_kernel, codes=codes, chunks=chunks),
        in_specs=[pl.BlockSpec(memory_space=pltpu.SMEM)] + [vmem] * 11 + [hbm] * len(weights),
        out_specs=[vmem] * 10,
        out_shape=[
            flat(rows, width),
            flat(rows, width),
            flat(rows, chunks * width),
            flat(rows, width),
            flat(chunks, rows, width),
            flat(rows, width),
            jax.ShapeDtypeStruct((rows, width), f32),
        ]
        + [flat(rows, width // 2)] * 2
        + [
            jax.ShapeDtypeStruct((16, width), f32),
        ],
        scratch_shapes=[
            pltpu.VMEM((chunks + 1, width, width), bf16),
            pltpu.VMEM((groups, 4, width // groups, width) if codes else (chunks * width, width), bf16),
            pltpu.VMEM((chunks, rows, width), f32),
            pltpu.SemaphoreType.DMA((3,)),
        ],
        cost_estimate=pl.CostEstimate(
            flops=2 * rows * width * width * (4 * chunks + 2),
            transcendentals=2 * rows * width * chunks,
            bytes_accessed=2 * width * width * (2 * chunks + 1) + 2 * rows * width * (2 * chunks + 8),
        ),
        compiler_params=pltpu.CompilerParams(vmem_limit_bytes=60 << 20),
        name="feed",
    )(where, *ctx_own, *ctx_got, tokens, cot, valid, vec, bias_in, *weights)


def plain_grads(ctx_own, ctx_got, d_attended, hidden_low, d_inner, activated, d_branch, chain_order):
    side = lax.axis_index("seq")
    mine = lax.axis_index("fsdp") & 1
    groups = lax.axis_size("fsdp")
    chunks, _, width = d_inner.shape
    piece = width // groups
    back = mm(activated, d_branch, TN).astype(bf16).reshape(groups // 2, 2, chunks, piece, width)
    own = jnp.concatenate(ctx_own, 1)
    got = jnp.concatenate(ctx_got, 1)
    context = jnp.where(side == 0, jnp.concatenate([own, got], 1), jnp.concatenate([got, own], 1))
    units = [mm(context, d_attended, TN)] + [mm(hidden_low, d_inner[c], TN) for c in range(chunks)]
    units = [unit.astype(bf16).reshape(groups // 2, 2, piece, width) for unit in units]
    units = units + [back[:, :, q] for q in range(chunks)]
    reductions = []
    for c in range(3):
        stacked = jnp.stack(units[3 * c : 3 * c + 3])
        sent = lax.dynamic_index_in_dim(stacked, 1 - mine, 2, keepdims=False)
        kept = lax.dynamic_index_in_dim(stacked, mine, 2, keepdims=False)
        reductions.append(Reduction([kept, swap(sent, "fsdp", 1)], chain_order[c]))
    return reductions


def body(
    tokens, prior_logits, lengths, order, cotangent, w_qkv, w_out, w_in, w_back,
    bias_q, bias_v, bias_o, gain_one, shift_one, bias_in, bias_back, gain_two, shift_two,
):
    side = lax.axis_index("seq")
    me = lax.axis_index("fsdp")
    groups = lax.axis_size("fsdp")
    rows = tokens[0]
    local_count, width = rows.shape
    total = 2 * local_count
    heads_local = prior_logits.shape[1]
    local_width = heads_local * HD
    piece = bias_q.shape[0]
    chunks = w_in.shape[1] // width
    pairs = range(heads_local // 2)
    top, *middle = reversed(bits_of(groups))
    where = jnp.stack([me, side]).astype(jnp.int32)

    other_rows = swap(rows, "seq", 1)
    own_qkv, nine, small = pack(
        where, w_qkv, w_out, w_in, w_back,
        (bias_q, bias_v, bias_o, gain_one, shift_one, bias_back, gain_two, shift_two, bias_in),
    )
    qkv_weight = gather_blocks(own_qkv, "fsdp").reshape(width, 3 * local_width)
    nine = extend(nine[:, :, None], top)
    small_all = gather_blocks(small.astype(bf16), "fsdp").astype(f32)
    vec = small_all[:, :8, :piece].transpose(1, 0, 2).reshape(8, width)
    inner_bias = small_all[:, 8, : chunks * piece].reshape(chunks, width)
    orders = chain_orders()
    chains = [nine[:, 3 * c : 3 * c + 3] for c in range(3)]
    for step in range(len(orders[0]) - 1):
        chains = [extend(held, orders[c][step]) for c, held in enumerate(chains)]

    order_row = order[0]
    length = lengths[0]
    own_order = lax.dynamic_slice_in_dim(order_row, side * local_count, local_count)
    other_order = lax.dynamic_slice_in_dim(order_row, (1 - side) * local_count, local_count)
    positions = jnp.arange(total, dtype=jnp.int32)
    own_pick = (positions[:, None] == own_order[None, :]).astype(bf16)
    other_pick = (positions[:, None] == other_order[None, :]).astype(bf16)

    def to_positions(own, other):
        return (mm(own_pick, own) + mm(other_pick, other)).astype(bf16)

    placed_rows = to_positions(rows, other_rows)
    own_cols = lambda vector: lax.dynamic_slice_in_dim(
        vector, side * local_width, local_width
    ).reshape(-1, 2 * HD)
    bias_cols = own_cols(vec[0])
    joint_bias = jnp.stack([bias_cols, jnp.zeros_like(bias_cols), own_cols(vec[1])], 1).reshape(-1)
    joint = (mm(placed_rows, qkv_weight) + joint_bias).astype(bf16)
    joint, *chains = lax.optimization_barrier((joint, *chains))
    chains = [extend(held, orders[c][-1]) for c, held in enumerate(chains)]
    held = []
    contexts = []
    ctx_own, ctx_got = [], []
    for t in pairs:
        raw_buf, prob_buf, context_pos = attend(
            joint, prior_logits[0], lengths, min(256, total), t, held
        )
        held = [raw_buf, prob_buf]
        contexts.append(context_pos)
        ctx_got.append(swap(mm(other_pick, context_pos, TN).astype(bf16), "seq", 1))
        ctx_own.append(mm(own_pick, context_pos, TN).astype(bf16))
    chains = [tie(held, contexts[1]) for held in chains]
    pieces = [(held, swap(held, "fsdp", 1)) for held in chains]
    codes = [[0] + [top] for _ in range(3)]
    codes = [codes_for([top] + orders[c]) for c in range(3)]
    if piece % 16 == 0:
        weights = [array for pair in pieces for array in pair]
    else:
        nine = jnp.concatenate([sort_pieces(*pieces[c], codes[c]) for c in range(3)], 0)
        weights = [
            nine[:5].reshape(5, width, width),
            nine[5:].transpose(1, 0, 2, 3).reshape(chunks * width, width),
        ]
        codes = None

    valid_rows = (own_order < length).astype(f32)[:, None]
    (out_rows, hidden_low, activated, d_branch, d_inner, d_attended, d_res_one,
     d_own, d_sent, sums) = feed(
        where, ctx_own, ctx_got, rows, cotangent[0], valid_rows, vec, inner_bias, weights, codes, groups
    )
    d_got = swap(d_sent, "seq", 1)

    chain_order = [orders[c][::-1] + [top] for c in range(3)]
    if codes is not None:
        parts = grads(
            where, ctx_own, ctx_got, d_attended, hidden_low, d_inner, activated, d_branch, groups
        )
        reductions = [
            Reduction([parts[3 + c], swap(parts[c], "fsdp", 1)], chain_order[c]) for c in range(3)
        ]
    else:
        reductions = plain_grads(
            ctx_own, ctx_got, d_attended, hidden_low, d_inner, activated, d_branch, chain_order
        )
    d_context_pos = to_positions(d_own, d_got)
    sents = [reduction.sent() for reduction in reductions]
    d_context_pos, *sents = lax.optimization_barrier((d_context_pos, *sents))
    for reduction, sent in zip(reductions, sents):
        reduction.launch(sent)

    dprior_buf, d_joint, bias_sums = attend_back(joint, d_context_pos, prob_buf, min(256, total))
    grad_w_qkv = mm(placed_rows, d_joint, TN).astype(bf16).reshape(1, groups, piece, -1)
    qkv = Reduction([grad_w_qkv], bits_of(groups))
    sent = qkv.sent()
    tied = lax.optimization_barrier(
        (sent, d_joint) + tuple(term for reduction in reductions for term in reduction.terms)
    )
    sent, d_joint = tied[:2]
    for c, reduction in enumerate(reductions):
        reduction.terms = list(tied[2 + 2 * c : 4 + 2 * c])
    qkv.launch(sent)
    sents = [reduction.sent() for reduction in reductions]
    d_joint, *sents = lax.optimization_barrier((d_joint, *sents))
    for reduction, sent in zip(reductions, sents):
        reduction.launch(sent)
    spread = lambda part: lax.dynamic_update_slice(
        jnp.zeros((1, width), f32), part.reshape(1, -1), (0, side * local_width)
    )
    sums = sum_all(
        jnp.concatenate([sums[:14], spread(bias_sums[:, 0]), spread(bias_sums[:, 1])], 0)
    )
    rms = jnp.sqrt(sums[10:13, 0] / (sums[13, 0] * width))
    own_sums = lax.dynamic_slice_in_dim(sums, me * piece, piece, 1)
    own_inner = lax.dynamic_slice_in_dim(
        sums[6 : 6 + chunks].reshape(-1), me * chunks * piece, chunks * piece
    )
    d_rows = mm(d_joint, qkv_weight, NT).astype(bf16)
    d_rows_sent = mm(other_pick, d_rows, TN).astype(bf16)
    d_rows_own = mm(own_pick, d_rows, TN)
    tokens_grad = (d_res_one + d_rows_own + swap(d_rows_sent, "seq", 1).astype(f32)).astype(bf16)

    while len(qkv.order) > 1 or len(reductions[0].order) > 1:
        for reduction in [qkv] + reductions:
            if len(reduction.order) > 1:
                reduction.launch(reduction.sent())

    def by_units(array):
        return array.reshape(2, piece, len(pairs), local_width).transpose(2, 0, 1, 3)

    qkv_terms = [by_units(term[0]) for term in qkv.terms]
    merged = Reduction(
        [jnp.concatenate([r.terms[k] for r in reductions] + [qkv_terms[k]], 0) for k in range(2)],
        [top],
    )
    merged.launch(merged.sent())
    own = (merged.terms[0].astype(f32) + merged.terms[1].astype(f32)).astype(bf16)[:, 0]
    other = swap(own, "seq", 1)
    out_all = jnp.where(
        side == 0, jnp.concatenate([own, other], 2), jnp.concatenate([other, own], 2)
    ).astype(f32)
    out_qkv = (
        out_all[9:]
        .reshape(len(pairs), piece, 2, 3, 2 * HD)
        .transpose(1, 3, 2, 0, 4)
        .reshape(piece, 3 * width)
    )
    return (
        out_rows[None],
        raw_buf[None],
        tokens_grad[None],
        dprior_buf[None],
        out_qkv,
        out_all[0],
        jnp.concatenate([out_all[1 + c] for c in range(chunks)], 1),
        out_all[5:9].reshape(chunks * piece, width),
        own_sums[14],
        own_sums[15],
        own_sums[0],
        own_sums[1],
        own_sums[2],
        own_inner,
        own_sums[3],
        own_sums[4],
        own_sums[5],
        rms,
    )


def solution(mesh):
    shard = P("fsdp", "seq", None)
    heads = P("fsdp", "seq", None, None)
    mat = P("fsdp", None)
    vec = P("fsdp")
    return jax.shard_map(
        body,
        mesh=mesh,
        in_specs=(shard, heads, vec, mat, shard) + (mat,) * 4 + (vec,) * 9,
        out_specs=(shard, heads, shard, heads) + (mat,) * 4 + (vec,) * 9 + (P(),),
        check_vma=False,
    )
```

```python
import functools
import math

import jax
import jax.numpy as jnp
from jax import lax
from jax.experimental import pallas as pl
from jax.experimental.pallas import tpu as pltpu
from jax.sharding import PartitionSpec as P

HD = 64
eps_norm = 1e-05
masked_fill = -1e30
f32 = jnp.float32
bf16 = jnp.bfloat16

NT = (((1,), (1,)), ((), ()))
TN = (((0,), (0,)), ((), ()))


def mm(left, right, dims=(((1,), (0,)), ((), ()))):
    return lax.dot_general(left, right, dims, preferred_element_type=f32)


def bits_of(count):
    return [1 << k for k in range(count.bit_length() - 1)]


def swap(value, axis, bit):
    count = lax.axis_size(axis)
    return lax.ppermute(value, axis, [(i, i ^ bit) for i in range(count)])


class Gather:
    def __init__(self, shard):
        self.shape = shard.shape
        self.held = shard[None]
        self.done = []

    def step(self, bit):
        other = swap(self.held, "fsdp", bit)
        high = (lax.axis_index("fsdp") & bit) != 0
        outer = 1 << sum(1 for b in self.done if b > bit)
        self.done.append(bit)
        split = (outer, self.held.shape[0] // outer) + self.shape
        first = jnp.where(high, other, self.held).reshape(split)
        second = jnp.where(high, self.held, other).reshape(split)
        self.held = jnp.stack([first, second], axis=1).reshape((-1,) + self.shape)


def tie(value, *others):
    return lax.optimization_barrier((value,) + others)[0]


def chain_orders():
    rest = list(reversed(bits_of(lax.axis_size("fsdp"))))[1:-1]
    up = rest[::-1]
    return [up + ["seq"], rest[:-1] + ["seq"] + rest[-1:], ["seq"] + up]


def extend(held, slots, stage):
    axis, bit = ("seq", 1) if stage == "seq" else ("fsdp", stage)
    if stage == "seq":
        more = [(a ^ 1, code) for a, code in slots]
    else:
        more = [(a, code ^ stage) for a, code in slots]
    return jnp.concatenate([held, swap(held, axis, bit)], axis=0), slots + more


def sort_pieces(own, other, slots):
    me = lax.axis_index("fsdp")
    side = lax.axis_index("seq")
    count = len(slots)
    both = jnp.concatenate([own, other], axis=0)
    place = [[0] * count, [0] * count]
    for s, (a, code) in enumerate(slots):
        place[a][code] = s
        place[a][code ^ 1] = s + count
    halves = [
        jnp.take(both, jnp.take(jnp.array(place[a], jnp.int32), jnp.arange(count) ^ me), axis=0)
        for a in range(2)
    ]
    joined = jnp.where(
        side == 0, jnp.concatenate(halves, -1), jnp.concatenate(halves[::-1], -1)
    )
    return joined.transpose(1, 0, 2, 3)


class Reduction:
    def __init__(self, terms, order):
        self.terms = terms
        self.order = order
        self.me = lax.axis_index("fsdp")
        self.side = lax.axis_index("seq")

    def pick(self, own):
        stage = self.order[0]
        picked = []
        for array in self.terms:
            if stage == "seq":
                size = array.shape[3] // 2
                index = self.side if own else 1 - self.side
                picked.append(lax.dynamic_slice_in_dim(array, index * size, size, 3))
            else:
                low = sum(1 for b in self.order if b != "seq" and b < stage)
                shape = array.shape
                array = array.reshape(
                    (shape[0], shape[1] >> (low + 1), 2, 1 << low) + shape[2:]
                )
                mine = ((self.me & stage) != 0).astype(jnp.int32)
                array = lax.dynamic_index_in_dim(
                    array, mine if own else 1 - mine, 2, keepdims=False
                )
                picked.append(array.reshape((shape[0], shape[1] // 2) + shape[2:]))
        total = picked[0].astype(f32)
        for other in picked[1:]:
            total = total + other.astype(f32)
        return total.astype(bf16)

    def sent(self):
        return self.pick(False)

    def launch(self, sent):
        kept = self.pick(True)
        stage = self.order[0]
        self.order = self.order[1:]
        axis, bit = ("seq", 1) if stage == "seq" else ("fsdp", stage)
        self.terms = [kept, swap(sent, axis, bit)]


def sum_all(vectors):
    for bit in bits_of(lax.axis_size("fsdp")):
        vectors = vectors + swap(vectors, "fsdp", bit)
    return vectors + swap(vectors, "seq", 1)


def pack_kernel(where_ref, *refs):
    w_qkv, w_out, w_in, w_back = refs[:4]
    vectors, (qkv_ref, nine_ref, small_ref) = refs[4:13], refs[13:]
    r, width = w_out.shape
    half = width // 2
    columns = pl.ds(pl.multiple_of(where_ref[1] * half, 128), half)
    nine_ref[0, 0] = w_out[:, columns]
    for c in range(4):
        nine_ref[0, 1 + c] = w_in[:, pl.ds(pl.multiple_of(c * width + where_ref[1] * half, 128), half)]
        nine_ref[0, 5 + c] = w_back[c * r : (c + 1) * r, columns]
    for kind in range(3):
        for t in range(3):
            start = kind * width + where_ref[1] * half + t * 128
            qkv_ref[:, (3 * t + kind) * 128 : (3 * t + kind + 1) * 128] = w_qkv[
                :, pl.ds(pl.multiple_of(start, 128), 128)
            ]
    small_ref[...] = jnp.zeros_like(small_ref)
    for k, vector in enumerate(vectors):
        small_ref[k : k + 1, : vector.shape[1]] = vector[...].astype(f32)


def pack(where, w_qkv, w_out, w_in, w_back, vectors):
    r, width = w_out.shape
    vmem = pl.BlockSpec(memory_space=pltpu.VMEM)
    return pl.pallas_call(
        pack_kernel,
        in_specs=[pl.BlockSpec(memory_space=pltpu.SMEM)] + [vmem] * 13,
        out_specs=[vmem] * 3,
        out_shape=[
            jax.ShapeDtypeStruct((r, 3 * width // 2), bf16),
            jax.ShapeDtypeStruct((1, 9, r, width // 2), bf16),
            jax.ShapeDtypeStruct((16, 256), f32),
        ],
        name="pack",
    )(where, w_qkv, w_out, w_in, w_back, *[vector[None] for vector in vectors])


def attend_kernel(length_ref, q_ref, k_ref, v_ref, own_ref, other_ref, prior_ref, *refs):
    raw_ref, prob_ref, ctx_own_ref, ctx_sent_ref, ctx = refs[-5:]
    step = pl.program_id(0)
    block = q_ref.shape[0]
    keys = k_ref.shape[0]
    lane = lax.broadcasted_iota(jnp.int32, (1, 2 * HD), 1)
    seen = lax.broadcasted_iota(jnp.int32, (1, keys), 1) < length_ref[0]
    q = q_ref[...] * jnp.asarray(1.0 / math.sqrt(HD), bf16)
    k = k_ref[...]
    v = v_ref[...]
    parts = []
    for h in range(2):
        mine = (lane >= HD) if h else (lane < HD)
        scores = mm(jnp.where(mine, q, jnp.zeros_like(q)), k, NT) + prior_ref[h].astype(f32)
        raw_ref[h] = scores.astype(bf16)
        masked = jnp.where(seen, scores, masked_fill)
        largest = jnp.max(masked, axis=-1, keepdims=True)
        exponent = jnp.exp(masked - largest)
        inverse = 1.0 / jnp.sum(exponent, axis=-1, keepdims=True)
        prob = (exponent * inverse).astype(bf16)
        prob_ref[h] = prob
        parts.append(mm(prob, v))
    ctx[pl.ds(pl.multiple_of(step * block, block), block), :] = jnp.where(
        lane < HD, parts[0], parts[1]
    ).astype(bf16)

    @pl.when(step == pl.num_programs(0) - 1)
    def _():
        position = lax.broadcasted_iota(jnp.int32, (own_ref.shape[0], keys), 1)
        placed = ctx[...]
        for order_ref, out_ref in ((other_ref, ctx_sent_ref), (own_ref, ctx_own_ref)):
            pick = jnp.where(position == order_ref[...], 1.0, 0.0).astype(bf16)
            out_ref[...] = mm(pick, placed).astype(bf16)


def attend(joint, prior, scalars, order_column, block, pair, held):
    heads, total, _ = prior.shape
    wide = 2 * HD
    square = pl.BlockSpec((2, block, total), lambda i, *_: (pair, i, 0))
    hbm = pl.BlockSpec(memory_space=pl.ANY)
    local = order_column.shape[0] // 2
    stored = pl.BlockSpec((local, wide), lambda i, *_: (0, 0))
    return pl.pallas_call(
        attend_kernel,
        grid_spec=pltpu.PrefetchScalarGridSpec(
            num_scalar_prefetch=1,
            grid=(total // block,),
            in_specs=[
                pl.BlockSpec((block, wide), lambda i, *_: (i, 3 * pair)),
                pl.BlockSpec((total, wide), lambda i, *_: (0, 3 * pair + 1)),
                pl.BlockSpec((total, wide), lambda i, *_: (0, 3 * pair + 2)),
                pl.BlockSpec((local, 1), lambda i, scalars: (scalars[1], 0)),
                pl.BlockSpec((local, 1), lambda i, scalars: (1 - scalars[1], 0)),
                square,
            ]
            + [hbm] * len(held),
            out_specs=[square, square, stored, stored],
            scratch_shapes=[pltpu.VMEM((total, wide), bf16)],
        ),
        out_shape=[
            jax.ShapeDtypeStruct(prior.shape, bf16),
            jax.ShapeDtypeStruct(prior.shape, bf16),
            jax.ShapeDtypeStruct((local, wide), bf16),
            jax.ShapeDtypeStruct((local, wide), bf16),
        ],
        input_output_aliases={7 + k: k for k in range(len(held))},
        cost_estimate=pl.CostEstimate(
            flops=16 * HD * total * total,
            transcendentals=2 * total * total,
            bytes_accessed=12 * total * total,
        ),
        compiler_params=pltpu.CompilerParams(vmem_limit_bytes=56 << 20),
        name="attend",
    )(scalars, joint, joint, joint, order_column, order_column, prior, *held)


def attend_back_kernel(q_ref, k_ref, v_ref, dc_ref, prob_ref, *refs):
    dprior_ref, dj_ref, bias_ref, dk_acc, dv_acc = refs[-5:]
    step = pl.program_id(1)
    block = q_ref.shape[0]
    wide_lanes = 2 * HD
    lane = lax.broadcasted_iota(jnp.int32, (1, wide_lanes), 1)
    scale = 1.0 / math.sqrt(HD)
    q = q_ref[...]
    k = k_ref[...]
    v = v_ref[...]
    dc = dc_ref[...]

    @pl.when(step == 0)
    def _():
        dk_acc[...] = jnp.zeros_like(dk_acc)
        dv_acc[...] = jnp.zeros_like(dv_acc)
        bias_ref[...] = jnp.zeros_like(bias_ref)

    dq, dk, dv = [], [], []
    for h in range(2):
        mine = (lane >= HD) if h else (lane < HD)
        prob = prob_ref[h]
        wide = prob.astype(f32)
        d_prob = mm(jnp.where(mine, dc, jnp.zeros_like(dc)), v, NT)
        row_term = jnp.sum(wide * d_prob, axis=-1, keepdims=True)
        d_scores = (wide * (d_prob - row_term)).astype(bf16)
        dprior_ref[h] = d_scores
        dq.append(mm(d_scores, k))
        dk.append(mm(d_scores, q, TN))
        dv.append(mm(prob, dc, TN))
    first = lane < HD
    d_query = (jnp.where(first, dq[0], dq[1]) * scale).astype(bf16)
    dj_ref[pl.ds(pl.multiple_of(step * block, block), block), 0:wide_lanes] = d_query
    bias_ref[0, 0:1, :] += jnp.sum(d_query.astype(f32), axis=0, keepdims=True)
    dk_acc[...] += jnp.where(first, dk[0], dk[1])
    dv_acc[...] += jnp.where(first, dv[0], dv[1])

    @pl.when(step == pl.num_programs(1) - 1)
    def _():
        dj_ref[:, wide_lanes : 2 * wide_lanes] = (dk_acc[...] * scale).astype(bf16)
        d_value = dv_acc[...].astype(bf16)
        dj_ref[:, 2 * wide_lanes : 3 * wide_lanes] = d_value
        bias_ref[0, 1:2, :] = jnp.sum(d_value.astype(f32), axis=0, keepdims=True)


def attend_back(joint, d_context, prob, block, first, pairs, held):
    heads, total, _ = prob.shape
    wide = 2 * HD
    square = pl.BlockSpec((2, block, total), lambda t, i: (first + t, i, 0))
    return pl.pallas_call(
        attend_back_kernel,
        grid=(pairs, total // block),
        in_specs=[
            pl.BlockSpec((block, wide), lambda t, i: (i, 3 * (first + t))),
            pl.BlockSpec((total, wide), lambda t, i: (0, 3 * (first + t) + 1)),
            pl.BlockSpec((total, wide), lambda t, i: (0, 3 * (first + t) + 2)),
            pl.BlockSpec((block, wide), lambda t, i: (i, first + t)),
            square,
        ]
        + [pl.BlockSpec(memory_space=pl.ANY)] * len(held),
        out_specs=[
            square,
            pl.BlockSpec((total, 3 * wide), lambda t, i: (0, t)),
            pl.BlockSpec((1, 8, wide), lambda t, i: (t, 0, 0)),
        ],
        out_shape=[
            jax.ShapeDtypeStruct(prob.shape, bf16),
            jax.ShapeDtypeStruct((total, 3 * pairs * wide), bf16),
            jax.ShapeDtypeStruct((pairs, 8, wide), f32),
        ],
        input_output_aliases={5: 0} if held else {},
        scratch_shapes=[pltpu.VMEM((total, wide), f32)] * 2,
        cost_estimate=pl.CostEstimate(flops=1000, transcendentals=0, bytes_accessed=1000),
        compiler_params=pltpu.CompilerParams(vmem_limit_bytes=56 << 20),
        name="attend_back",
    )(joint, joint, joint, d_context, prob, *held)


def grads_kernel(where_ref, *refs):
    ctx_own_refs, ctx_got_refs, refs = refs[:3], refs[3:6], refs[6:]
    d_att_ref, low_ref, d_inner_ref, act_ref, d_branch_ref = refs[:5]
    sent_refs, kept_refs = refs[5:8], refs[8:11]
    odd = (where_ref[0] & 1) == 1
    side = where_ref[1]
    r, width = sent_refs[0].shape[2:]
    groups = 2 * sent_refs[0].shape[1]

    def put(chain, unit, first, blocks):
        blocks = blocks.astype(bf16)
        lower, upper = blocks[:, 0], blocks[:, 1]
        at = pl.ds(first, blocks.shape[0])
        sent_refs[chain][unit, at] = jnp.where(odd, lower, upper)
        kept_refs[chain][unit, at] = jnp.where(odd, upper, lower)

    d_branch = d_branch_ref[...]

    def back(c, carry):
        part = mm(act_ref[:, pl.ds(pl.multiple_of(c * width, 128), width)], d_branch, TN)
        part = part.reshape(groups // 8, 2, 4, r, width)
        put(1, 2, c * (groups // 8), part[:, :, 0])
        for q in range(3):
            put(2, q, c * (groups // 8), part[:, :, 1 + q])
        return carry

    lax.fori_loop(0, 4, back, 0)
    low = low_ref[...]

    def inner(c, carry):
        put(1, c, 0, mm(low, d_inner_ref[2 + c], TN).reshape(groups // 2, 2, r, width))
        put(0, 1 + c, 0, mm(low, d_inner_ref[c], TN).reshape(groups // 2, 2, r, width))
        return carry

    lax.fori_loop(0, 2, inner, 0)
    d_att = d_att_ref[...]
    for refs, start in ((ctx_own_refs, side), (ctx_got_refs, 1 - side)):
        part = mm(jnp.concatenate([ref[...] for ref in refs], 1), d_att, TN)
        put(0, 0, start * (groups // 4), part.reshape(groups // 4, 2, r, width))


def grads(where, ctx_own, ctx_got, d_att, low, d_inner, act, d_branch, groups):
    rows, width = d_att.shape
    vmem = pl.BlockSpec(memory_space=pltpu.VMEM)
    part = jax.ShapeDtypeStruct((3, groups // 2, width // groups, width), bf16)
    return pl.pallas_call(
        grads_kernel,
        in_specs=[pl.BlockSpec(memory_space=pltpu.SMEM)] + [vmem] * 11,
        out_specs=[vmem] * 6,
        out_shape=[part] * 6,
        cost_estimate=pl.CostEstimate(
            flops=18 * rows * width * width,
            transcendentals=0,
            bytes_accessed=18 * width * width + 24 * rows * width,
        ),
        compiler_params=pltpu.CompilerParams(vmem_limit_bytes=60 << 20),
        name="grads",
    )(where, *ctx_own, *ctx_got, d_att, low, d_inner, act, d_branch)


def feed_kernel(
    where_ref, *refs, codes, chunks,
):
    ctx_own_refs, ctx_got_refs, refs = refs[:3], refs[3:6], refs[6:]
    (tokens_ref, cot_ref, valid_ref, vec_ref, bias_in_ref), refs = refs[:5], refs[5:]
    weight_count = 2 if codes is None else 6
    weights, refs = refs[:weight_count], refs[weight_count:]
    (out_ref, low_ref, act_ref, d_branch_ref, d_inner_ref, d_att_ref, d_res_ref,
     d_own_ref, d_sent_ref, sums_ref, w_five, w_back, slope, sems) = refs
    me = where_ref[0]
    side = where_ref[1]
    width = tokens_ref.shape[1]
    half = width // 2

    def copies(chain):
        if codes is None:
            if chain == 2:
                return []
            target = (w_five, w_back)[chain]
            return [pltpu.make_async_copy(weights[chain], target, sems.at[chain])]
        made = []
        r = weights[0].shape[2]
        for b in range(2):
            source = weights[2 * chain + b]
            for s, (a, code) in enumerate(codes[chain]):
                column = pl.ds(pl.multiple_of((side ^ a) * half, 128), half)
                block = me ^ (code ^ b)
                rows = pl.ds(pl.multiple_of(block * r, 16), r)
                moves = (
                    ((0, 3, w_five.at[0:3, rows, column]),),
                    ((0, 2, w_five.at[3:5, rows, column]), (2, 1, w_back.at[block, 0:1, :, column])),
                    ((0, 3, w_back.at[block, 1:4, :, column]),),
                )[chain]
                for first, count, target in moves:
                    made.append(pltpu.make_async_copy(
                        source.at[s, pl.ds(first, count)], target, sems.at[chain]))
        return made

    groups = [copies(chain) for chain in range(3)]
    for group in groups:
        for copy in group:
            copy.start()

    def back_rows(c):
        if codes is None:
            return w_back[c * width : (c + 1) * width, :]
        per = w_back.shape[0] // chunks
        return w_back[c * per : (c + 1) * per].reshape(width, width)

    vec = vec_ref[...]
    proj_bias, first_gain, first_shift, outer_bias, second_gain, second_shift = (
        vec[k : k + 1] for k in range(2, 8)
    )
    own_rows = pl.ds(pl.multiple_of(side * half, 128), half)
    other_rows = pl.ds(pl.multiple_of((1 - side) * half, 128), half)
    valid = valid_ref[...]
    for copy in groups[0]:
        copy.wait()
    ctx_own = jnp.concatenate([ref[...] for ref in ctx_own_refs], 1)
    ctx_got = jnp.concatenate([ref[...] for ref in ctx_got_refs], 1)
    attended = (
        mm(ctx_own, w_five[0, own_rows, :]) + mm(ctx_got, w_five[0, other_rows, :]) + proj_bias
    )
    tokens_f = tokens_ref[...].astype(f32)

    def stat(row, values):
        total = jnp.sum(jnp.sum(values, axis=0, keepdims=True), axis=1, keepdims=True)
        sums_ref[row : row + 1, :] = jnp.broadcast_to(total, (1, width))

    def column_sum(row, values):
        sums_ref[row : row + 1, :] = jnp.sum(values, axis=0, keepdims=True)

    def normalize(values):
        centered = values - jnp.mean(values, axis=-1, keepdims=True)
        spread = lax.rsqrt(jnp.mean(centered * centered, axis=-1, keepdims=True) + eps_norm)
        return centered * spread, spread

    def normalize_back(grad, gain, normal, spread):
        e = grad * gain
        return spread * (
            e - jnp.mean(e, axis=-1, keepdims=True)
            - normal * jnp.mean(e * normal, axis=-1, keepdims=True)
        )

    stat(10, valid * tokens_f * tokens_f)
    stat(11, valid * attended * attended)
    stat(13, valid * jnp.ones((1, 128), f32) * (1.0 / 128.0))
    normal_one, spread_one = normalize(tokens_f + attended)
    hidden = normal_one * first_gain + first_shift
    hidden_low = hidden.astype(bf16)
    low_ref[...] = hidden_low
    for copy in groups[1] + groups[2]:
        copy.wait()
    branch = jnp.zeros_like(hidden)
    for c in range(chunks):
        inner = mm(hidden_low, w_five[1 + c]) + bias_in_ref[c : c + 1, :]
        below = 0.5 + 0.5 * lax.erf(inner * math.sqrt(0.5))
        slope[c] = below + inner * (jnp.exp(inner * inner * -0.5) * (1.0 / math.sqrt(2.0 * math.pi)))
        activated = (inner * below).astype(bf16)
        columns = slice(c * width, (c + 1) * width)
        act_ref[:, columns] = activated
        branch = branch + mm(activated, back_rows(c))
    branch = branch + outer_bias
    stat(12, valid * branch * branch)
    normal_two, spread_two = normalize(hidden + branch)
    out_ref[...] = (normal_two * second_gain + second_shift).astype(bf16)
    d_output = cot_ref[...].astype(f32) * valid
    column_sum(4, d_output * normal_two)
    column_sum(5, d_output)
    d_hidden = normalize_back(d_output, second_gain, normal_two, spread_two)
    d_branch = d_hidden.astype(bf16)
    d_branch_ref[...] = d_branch
    column_sum(3, d_branch.astype(f32))
    for c in range(chunks):
        columns = slice(c * width, (c + 1) * width)
        d_inner = (mm(d_branch, back_rows(c), NT) * slope[c]).astype(bf16)
        d_inner_ref[c] = d_inner
        column_sum(6 + c, d_inner.astype(f32))
        d_hidden = d_hidden + mm(d_inner, w_five[1 + c], NT)
    column_sum(1, d_hidden * normal_one)
    column_sum(2, d_hidden)
    d_res = normalize_back(d_hidden, first_gain, normal_one, spread_one)
    d_res_ref[...] = d_res
    d_att = d_res.astype(bf16)
    d_att_ref[...] = d_att
    column_sum(0, d_att.astype(f32))
    d_sent_ref[...] = mm(d_att, w_five[0, other_rows, :], NT).astype(bf16)
    d_own_ref[...] = mm(d_att, w_five[0, own_rows, :], NT).astype(bf16)


def feed(where, ctx_own, ctx_got, tokens, cot, valid, vec, bias_in, weights, codes, groups):
    rows, width = tokens.shape
    chunks = bias_in.shape[0]
    vmem = pl.BlockSpec(memory_space=pltpu.VMEM)
    hbm = pl.BlockSpec(memory_space=pl.ANY)
    flat = lambda *shape: jax.ShapeDtypeStruct(shape, bf16)
    return pl.pallas_call(
        functools.partial(feed_kernel, codes=codes, chunks=chunks),
        in_specs=[pl.BlockSpec(memory_space=pltpu.SMEM)] + [vmem] * 11 + [hbm] * len(weights),
        out_specs=[vmem] * 10,
        out_shape=[
            flat(rows, width),
            flat(rows, width),
            flat(rows, chunks * width),
            flat(rows, width),
            flat(chunks, rows, width),
            flat(rows, width),
            jax.ShapeDtypeStruct((rows, width), f32),
        ]
        + [flat(rows, width // 2)] * 2
        + [
            jax.ShapeDtypeStruct((16, width), f32),
        ],
        scratch_shapes=[
            pltpu.VMEM((chunks + 1, width, width), bf16),
            pltpu.VMEM((groups, 4, width // groups, width) if codes else (chunks * width, width), bf16),
            pltpu.VMEM((chunks, rows, width), f32),
            pltpu.SemaphoreType.DMA((3,)),
        ],
        cost_estimate=pl.CostEstimate(
            flops=2 * rows * width * width * (4 * chunks + 2),
            transcendentals=2 * rows * width * chunks,
            bytes_accessed=2 * width * width * (2 * chunks + 1) + 2 * rows * width * (2 * chunks + 8),
        ),
        compiler_params=pltpu.CompilerParams(vmem_limit_bytes=60 << 20),
        name="feed",
    )(where, *ctx_own, *ctx_got, tokens, cot, valid, vec, bias_in, *weights)


def plain_grads(ctx_own, ctx_got, d_attended, hidden_low, d_inner, activated, d_branch, chain_order):
    side = lax.axis_index("seq")
    mine = lax.axis_index("fsdp") & 1
    groups = lax.axis_size("fsdp")
    chunks, _, width = d_inner.shape
    piece = width // groups
    back = mm(activated, d_branch, TN).astype(bf16).reshape(groups // 2, 2, chunks, piece, width)
    own = jnp.concatenate(ctx_own, 1)
    got = jnp.concatenate(ctx_got, 1)
    context = jnp.where(side == 0, jnp.concatenate([own, got], 1), jnp.concatenate([got, own], 1))
    units = [mm(context, d_attended, TN)] + [mm(hidden_low, d_inner[c], TN) for c in range(chunks)]
    units = [unit.astype(bf16).reshape(groups // 2, 2, piece, width) for unit in units]
    units = units + [back[:, :, q] for q in range(chunks)]
    reductions = []
    for c in range(3):
        stacked = jnp.stack(units[3 * c : 3 * c + 3])
        sent = lax.dynamic_index_in_dim(stacked, 1 - mine, 2, keepdims=False)
        kept = lax.dynamic_index_in_dim(stacked, mine, 2, keepdims=False)
        reductions.append(Reduction([kept, swap(sent, "fsdp", 1)], chain_order[c]))
    return reductions


def body(
    tokens, prior_logits, lengths, order, cotangent, w_qkv, w_out, w_in, w_back,
    bias_q, bias_v, bias_o, gain_one, shift_one, bias_in, bias_back, gain_two, shift_two,
):
    side = lax.axis_index("seq")
    me = lax.axis_index("fsdp")
    groups = lax.axis_size("fsdp")
    rows = tokens[0]
    local_count, width = rows.shape
    total = 2 * local_count
    heads_local = prior_logits.shape[1]
    local_width = heads_local * HD
    piece = bias_q.shape[0]
    chunks = w_in.shape[1] // width
    pairs = range(heads_local // 2)
    top, *middle = reversed(bits_of(groups))
    where = jnp.stack([me, side]).astype(jnp.int32)

    other_rows = swap(rows, "seq", 1)
    own_qkv, nine, small = pack(
        where, w_qkv, w_out, w_in, w_back,
        (bias_q, bias_v, bias_o, gain_one, shift_one, bias_back, gain_two, shift_two, bias_in),
    )
    ascending = bits_of(groups)
    small_chain = Gather(small.astype(bf16))
    qkv_chain = Gather(own_qkv)
    qkv_order = ascending[-2:] + ascending[:-2][::-1]
    for bit in ascending[:-2]:
        small_chain.step(bit)
    qkv_chain.step(qkv_order[0])
    for k in (1, 2):
        small_chain.held, qkv_chain.held = lax.optimization_barrier(
            (small_chain.held, qkv_chain.held)
        )
        qkv_chain.step(qkv_order[k])
        small_chain.step(ascending[len(ascending) - 3 + k])
    small_chain.held, qkv_chain.held = lax.optimization_barrier((small_chain.held, qkv_chain.held))
    for bit in qkv_order[3:]:
        qkv_chain.step(bit)
    small_all = small_chain.held.astype(f32)
    qkv_weight = qkv_chain.held.reshape(width, 3 * local_width)
    vec = small_all[:, :8, :piece].transpose(1, 0, 2).reshape(8, width)
    inner_bias = small_all[:, 8, : chunks * piece].reshape(chunks, width)
    orders = chain_orders()
    nine, slots = extend(nine, [(0, 0)], top)
    chains = [(nine[:, 3 * c : 3 * c + 3], slots) for c in range(3)]
    for step in range(len(orders[0]) - 1):
        chains = [extend(*chain, orders[c][step]) for c, chain in enumerate(chains)]

    order_row = order[0]
    length = lengths[0]
    scalars = jnp.stack([length, side]).astype(jnp.int32)
    order_column = order_row[:, None]
    own_order = lax.dynamic_slice_in_dim(order_row, side * local_count, local_count)
    other_order = lax.dynamic_slice_in_dim(order_row, (1 - side) * local_count, local_count)
    positions = jnp.arange(total, dtype=jnp.int32)
    own_pick = (positions[:, None] == own_order[None, :]).astype(bf16)
    other_pick = (positions[:, None] == other_order[None, :]).astype(bf16)

    def to_positions(own, other):
        return (mm(own_pick, own) + mm(other_pick, other)).astype(bf16)

    rows, order_column = lax.optimization_barrier((rows, order_column))
    placed_rows = to_positions(rows, other_rows)
    own_cols = lambda vector: lax.dynamic_slice_in_dim(
        vector, side * local_width, local_width
    ).reshape(-1, 2 * HD)
    bias_cols = own_cols(vec[0])
    joint_bias = jnp.stack([bias_cols, jnp.zeros_like(bias_cols), own_cols(vec[1])], 1).reshape(-1)
    joint = (mm(placed_rows, qkv_weight) + joint_bias).astype(bf16)
    joint, *held = lax.optimization_barrier((joint, *[chain[0] for chain in chains]))
    chains = [extend(held[c], chains[c][1], orders[c][-1]) for c in range(3)]
    codes = [chain[1] for chain in chains]
    held = []
    ctx_own, ctx_got = [], []
    for t in pairs:
        raw_buf, prob_buf, own, sent = attend(
            joint, prior_logits[0], scalars, order_column, min(256, total), t, held
        )
        held = [raw_buf, prob_buf]
        ctx_own.append(own)
        ctx_got.append(swap(sent, "seq", 1))
    chains = [tie(chain[0], ctx_own[1]) for chain in chains]
    pieces = [(held, swap(held, "fsdp", 1)) for held in chains]
    if piece % 16 == 0:
        weights = [array for pair in pieces for array in pair]
    else:
        nine = jnp.concatenate([sort_pieces(*pieces[c], codes[c]) for c in range(3)], 0)
        weights = [
            nine[:5].reshape(5, width, width),
            nine[5:].transpose(1, 0, 2, 3).reshape(chunks * width, width),
        ]
        codes = None

    valid_rows = (own_order < length).astype(f32)[:, None]
    (out_rows, hidden_low, activated, d_branch, d_inner, d_attended, d_res_one,
     d_own, d_sent, sums) = feed(
        where, ctx_own, ctx_got, rows, cotangent[0], valid_rows, vec, inner_bias, weights, codes, groups
    )
    d_got = swap(d_sent, "seq", 1)

    chain_order = [orders[c][::-1] + [top] for c in range(3)]
    if codes is not None:
        parts = grads(
            where, ctx_own, ctx_got, d_attended, hidden_low, d_inner, activated, d_branch, groups
        )
        d_got, *parts = lax.optimization_barrier((d_got, *parts))
        reductions = [
            Reduction([parts[3 + c], swap(parts[c], "fsdp", 1)], chain_order[c]) for c in range(3)
        ]
    else:
        reductions = plain_grads(
            ctx_own, ctx_got, d_attended, hidden_low, d_inner, activated, d_branch, chain_order
        )
    d_context_pos = to_positions(d_own, d_got)
    dprior_buf, d_first, bias_first = attend_back(
        joint, d_context_pos, prob_buf, min(256, total), 0, 1, []
    )
    def fence(*values):
        terms = tuple(term for reduction in reductions for term in reduction.terms)
        tied = lax.optimization_barrier(values + terms)
        for c, reduction in enumerate(reductions):
            reduction.terms = list(tied[len(values) + 2 * c : len(values) + 2 * c + 2])
        return tied[: len(values)]

    (dprior_buf,) = fence(dprior_buf)
    sents = [reduction.sent() for reduction in reductions]
    dprior_buf, *sents = lax.optimization_barrier((dprior_buf, *sents))
    for reduction, sent in zip(reductions, sents):
        reduction.launch(sent)
    dprior_buf, d_rest, bias_rest = attend_back(
        joint, d_context_pos, prob_buf, min(256, total), 1, len(pairs) - 1, [dprior_buf]
    )
    (d_rest,) = fence(d_rest)
    d_joint = jnp.concatenate([d_first, d_rest], 1)
    bias_sums = jnp.concatenate([bias_first, bias_rest], 0)
    grad_w_qkv = mm(placed_rows, d_joint, TN).astype(bf16).reshape(1, groups, piece, -1)
    qkv = Reduction([grad_w_qkv], bits_of(groups))
    sent = qkv.sent()
    sent, d_joint = fence(sent, d_joint)
    qkv.launch(sent)
    sents = [reduction.sent() for reduction in reductions]
    d_joint, sums, bias_sums, *rest = lax.optimization_barrier(
        (d_joint, sums, bias_sums, *qkv.terms, *sents)
    )
    qkv.terms, sents = rest[:2], rest[2:]
    for reduction, sent in zip(reductions, sents):
        reduction.launch(sent)
    spread = lambda part: lax.dynamic_update_slice(
        jnp.zeros((1, width), f32), part.reshape(1, -1), (0, side * local_width)
    )
    sums = sum_all(
        jnp.concatenate([sums[:14], spread(bias_sums[:, 0]), spread(bias_sums[:, 1])], 0)
    )
    rms = jnp.sqrt(sums[10:13, 0] / (sums[13, 0] * width))
    own_sums = lax.dynamic_slice_in_dim(sums, me * piece, piece, 1)
    own_inner = lax.dynamic_slice_in_dim(
        sums[6 : 6 + chunks].reshape(-1), me * chunks * piece, chunks * piece
    )
    d_rows = mm(d_joint, qkv_weight, NT).astype(bf16)
    d_rows_sent = mm(other_pick, d_rows, TN).astype(bf16)
    (d_rows_sent,) = fence(d_rows_sent)
    d_rows_own = mm(own_pick, d_rows, TN)
    d_rows_got = swap(d_rows_sent, "seq", 1)

    while len(qkv.order) > 1 or len(reductions[0].order) > 1:
        for reduction in [qkv] + reductions:
            if len(reduction.order) > 1:
                reduction.launch(reduction.sent())

    def by_units(array):
        return array.reshape(2, piece, len(pairs), local_width).transpose(2, 0, 1, 3)

    qkv_terms = [by_units(term[0]) for term in qkv.terms]
    merged = Reduction(
        [jnp.concatenate([r.terms[k] for r in reductions] + [qkv_terms[k]], 0) for k in range(2)],
        [top],
    )
    *merged.terms, d_rows_got = lax.optimization_barrier((*merged.terms, d_rows_got))
    tokens_grad = (d_res_one + d_rows_own + d_rows_got.astype(f32)).astype(bf16)
    merged.launch(merged.sent())
    own = (merged.terms[0].astype(f32) + merged.terms[1].astype(f32)).astype(bf16)[:, 0]
    other = swap(own, "seq", 1)
    out_all = jnp.where(
        side == 0, jnp.concatenate([own, other], 2), jnp.concatenate([other, own], 2)
    ).astype(f32)
    out_qkv = (
        out_all[9:]
        .reshape(len(pairs), piece, 2, 3, 2 * HD)
        .transpose(1, 3, 2, 0, 4)
        .reshape(piece, 3 * width)
    )
    return (
        out_rows[None],
        raw_buf[None],
        tokens_grad[None],
        dprior_buf[None],
        out_qkv,
        out_all[0],
        jnp.concatenate([out_all[1 + c] for c in range(chunks)], 1),
        out_all[5:9].reshape(chunks * piece, width),
        own_sums[14],
        own_sums[15],
        own_sums[0],
        own_sums[1],
        own_sums[2],
        own_inner,
        own_sums[3],
        own_sums[4],
        own_sums[5],
        rms,
    )


def solution(mesh):
    shard = P("fsdp", "seq", None)
    heads = P("fsdp", "seq", None, None)
    mat = P("fsdp", None)
    vec = P("fsdp")
    return jax.shard_map(
        body,
        mesh=mesh,
        in_specs=(shard, heads, vec, mat, shard) + (mat,) * 4 + (vec,) * 9,
        out_specs=(shard, heads, shard, heads) + (mat,) * 4 + (vec,) * 9 + (P(),),
        check_vma=False,
    )
```

```python
import functools
import math

import jax
import jax.numpy as jnp
from jax import lax
from jax.experimental import pallas as pl
from jax.experimental.pallas import tpu as pltpu
from jax.sharding import PartitionSpec as P

HD = 64
eps_norm = 1e-05
masked_fill = -1e30
f32 = jnp.float32
bf16 = jnp.bfloat16

NT = (((1,), (1,)), ((), ()))
TN = (((0,), (0,)), ((), ()))


def mm(left, right, dims=(((1,), (0,)), ((), ()))):
    return lax.dot_general(left, right, dims, preferred_element_type=f32)


def bits_of(count):
    return [1 << k for k in range(count.bit_length() - 1)]


def swap(value, axis, bit):
    count = lax.axis_size(axis)
    return lax.ppermute(value, axis, [(i, i ^ bit) for i in range(count)])


class Gather:
    def __init__(self, shard):
        self.shape = shard.shape
        self.held = shard[None]
        self.done = []

    def step(self, bit):
        other = swap(self.held, "fsdp", bit)
        high = (lax.axis_index("fsdp") & bit) != 0
        outer = 1 << sum(1 for b in self.done if b > bit)
        self.done.append(bit)
        split = (outer, self.held.shape[0] // outer) + self.shape
        first = jnp.where(high, other, self.held).reshape(split)
        second = jnp.where(high, self.held, other).reshape(split)
        self.held = jnp.stack([first, second], axis=1).reshape((-1,) + self.shape)

    def top_two(self, low, high):
        me = lax.axis_index("fsdp")
        mine = ((me & low) != 0) * 1 + ((me & high) != 0) * 2
        got = [swap(self.held, "fsdp", peer) for peer in (low, high, low | high)]
        four = jnp.stack([self.held] + got)
        self.done += [low, high]
        self.held = jnp.concatenate(
            [lax.dynamic_index_in_dim(four, z ^ mine, 0, keepdims=False) for z in range(4)], 0
        )


def tie(value, *others):
    return lax.optimization_barrier((value,) + others)[0]


def chain_orders():
    rest = list(reversed(bits_of(lax.axis_size("fsdp"))))[1:-1]
    up = rest[::-1]
    return [up + ["seq"], rest[:-1] + ["seq"] + rest[-1:], ["seq"] + up]


def receive(held, stage):
    return swap(held, "seq", 1) if stage == "seq" else swap(held, "fsdp", stage)


def more_slots(slots, stage):
    if stage == "seq":
        return slots + [(a ^ 1, code) for a, code in slots]
    return slots + [(a, code ^ stage) for a, code in slots]


def join(held, got):
    return jnp.concatenate([held, got], axis=0)


def sort_pieces(own, other, slots):
    me = lax.axis_index("fsdp")
    side = lax.axis_index("seq")
    count = len(slots)
    both = jnp.concatenate([own, other], axis=0)
    place = [[0] * count, [0] * count]
    for s, (a, code) in enumerate(slots):
        place[a][code] = s
        place[a][code ^ 1] = s + count
    halves = [
        jnp.take(both, jnp.take(jnp.array(place[a], jnp.int32), jnp.arange(count) ^ me), axis=0)
        for a in range(2)
    ]
    joined = jnp.where(
        side == 0, jnp.concatenate(halves, -1), jnp.concatenate(halves[::-1], -1)
    )
    return joined.transpose(1, 0, 2, 3)


class Reduction:
    def __init__(self, terms, order):
        self.terms = terms
        self.order = order
        self.me = lax.axis_index("fsdp")
        self.side = lax.axis_index("seq")

    def pick(self, own):
        stage = self.order[0]
        picked = []
        for array in self.terms:
            if stage == "seq":
                size = array.shape[3] // 2
                index = self.side if own else 1 - self.side
                picked.append(lax.dynamic_slice_in_dim(array, index * size, size, 3))
            else:
                low = sum(1 for b in self.order if b != "seq" and b < stage)
                shape = array.shape
                array = array.reshape(
                    (shape[0], shape[1] >> (low + 1), 2, 1 << low) + shape[2:]
                )
                mine = ((self.me & stage) != 0).astype(jnp.int32)
                array = lax.dynamic_index_in_dim(
                    array, mine if own else 1 - mine, 2, keepdims=False
                )
                picked.append(array.reshape((shape[0], shape[1] // 2) + shape[2:]))
        total = picked[0].astype(f32)
        for other in picked[1:]:
            total = total + other.astype(f32)
        return total.astype(bf16)

    def sent(self):
        return self.pick(False)

    def launch(self, sent):
        kept = self.pick(True)
        stage = self.order[0]
        self.order = self.order[1:]
        axis, bit = ("seq", 1) if stage == "seq" else ("fsdp", stage)
        self.terms = [kept, swap(sent, axis, bit)]


def pack_kernel(where_ref, *refs):
    w_qkv, w_out, w_in, w_back = refs[:4]
    vectors, (qkv_ref, nine_ref, small_ref) = refs[4:13], refs[13:]
    r, width = w_out.shape
    half = width // 2
    columns = pl.ds(pl.multiple_of(where_ref[1] * half, 128), half)
    nine_ref[0, 0] = w_out[:, columns]
    for c in range(4):
        nine_ref[0, 1 + c] = w_in[:, pl.ds(pl.multiple_of(c * width + where_ref[1] * half, 128), half)]
        nine_ref[0, 5 + c] = w_back[c * r : (c + 1) * r, columns]
    for kind in range(3):
        for t in range(3):
            start = kind * width + where_ref[1] * half + t * 128
            qkv_ref[:, (3 * t + kind) * 128 : (3 * t + kind + 1) * 128] = w_qkv[
                :, pl.ds(pl.multiple_of(start, 128), 128)
            ]
    small_ref[...] = jnp.zeros_like(small_ref)
    for k, vector in enumerate(vectors):
        small_ref[k : k + 1, : vector.shape[1]] = vector[...].astype(f32)


def pack(where, w_qkv, w_out, w_in, w_back, vectors):
    r, width = w_out.shape
    vmem = pl.BlockSpec(memory_space=pltpu.VMEM)
    return pl.pallas_call(
        pack_kernel,
        in_specs=[pl.BlockSpec(memory_space=pltpu.SMEM)] + [vmem] * 13,
        out_specs=[vmem] * 3,
        out_shape=[
            jax.ShapeDtypeStruct((r, 3 * width // 2), bf16),
            jax.ShapeDtypeStruct((1, 9, r, width // 2), bf16),
            jax.ShapeDtypeStruct((16, 256), f32),
        ],
        name="pack",
    )(where, w_qkv, w_out, w_in, w_back, *[vector[None] for vector in vectors])


def attend_kernel(length_ref, q_ref, k_ref, v_ref, own_ref, other_ref, prior_ref, *refs):
    raw_ref, prob_ref, ctx_own_ref, ctx_sent_ref, ctx = refs[-5:]
    step = pl.program_id(0)
    block = q_ref.shape[0]
    keys = k_ref.shape[0]
    lane = lax.broadcasted_iota(jnp.int32, (1, 2 * HD), 1)
    seen = lax.broadcasted_iota(jnp.int32, (1, keys), 1) < length_ref[0]
    q = q_ref[...] * jnp.asarray(1.0 / math.sqrt(HD), bf16)
    k = k_ref[...]
    v = v_ref[...]
    parts = []
    for h in range(2):
        mine = (lane >= HD) if h else (lane < HD)
        scores = mm(jnp.where(mine, q, jnp.zeros_like(q)), k, NT) + prior_ref[h].astype(f32)
        raw_ref[h] = scores.astype(bf16)
        masked = jnp.where(seen, scores, masked_fill)
        largest = jnp.max(masked, axis=-1, keepdims=True)
        exponent = jnp.exp(masked - largest)
        inverse = 1.0 / jnp.sum(exponent, axis=-1, keepdims=True)
        prob = (exponent * inverse).astype(bf16)
        prob_ref[h] = prob
        parts.append(mm(prob, v))
    ctx[pl.ds(pl.multiple_of(step * block, block), block), :] = jnp.where(
        lane < HD, parts[0], parts[1]
    ).astype(bf16)

    @pl.when(step == pl.num_programs(0) - 1)
    def _():
        position = lax.broadcasted_iota(jnp.int32, (own_ref.shape[0], keys), 1)
        placed = ctx[...]
        for order_ref, out_ref in ((other_ref, ctx_sent_ref), (own_ref, ctx_own_ref)):
            pick = jnp.where(position == order_ref[...], 1.0, 0.0).astype(bf16)
            out_ref[...] = mm(pick, placed).astype(bf16)


def attend(joint, prior, scalars, order_column, block, pair, held):
    heads, total, _ = prior.shape
    wide = 2 * HD
    square = pl.BlockSpec((2, block, total), lambda i, *_: (pair, i, 0))
    hbm = pl.BlockSpec(memory_space=pl.ANY)
    local = order_column.shape[0] // 2
    stored = pl.BlockSpec((local, wide), lambda i, *_: (0, 0))
    return pl.pallas_call(
        attend_kernel,
        grid_spec=pltpu.PrefetchScalarGridSpec(
            num_scalar_prefetch=1,
            grid=(total // block,),
            in_specs=[
                pl.BlockSpec((block, wide), lambda i, *_: (i, 3 * pair)),
                pl.BlockSpec((total, wide), lambda i, *_: (0, 3 * pair + 1)),
                pl.BlockSpec((total, wide), lambda i, *_: (0, 3 * pair + 2)),
                pl.BlockSpec((local, 1), lambda i, scalars: (scalars[1], 0)),
                pl.BlockSpec((local, 1), lambda i, scalars: (1 - scalars[1], 0)),
                square,
            ]
            + [hbm] * len(held),
            out_specs=[square, square, stored, stored],
            scratch_shapes=[pltpu.VMEM((total, wide), bf16)],
        ),
        out_shape=[
            jax.ShapeDtypeStruct(prior.shape, bf16),
            jax.ShapeDtypeStruct(prior.shape, bf16),
            jax.ShapeDtypeStruct((local, wide), bf16),
            jax.ShapeDtypeStruct((local, wide), bf16),
        ],
        input_output_aliases={7 + k: k for k in range(len(held))},
        cost_estimate=pl.CostEstimate(flops=1000, transcendentals=0, bytes_accessed=1000),
        compiler_params=pltpu.CompilerParams(vmem_limit_bytes=56 << 20),
        name="attend",
    )(scalars, joint, joint, joint, order_column, order_column, prior, *held)


def attend_back_kernel(q_ref, k_ref, v_ref, dc_ref, prob_ref, *refs):
    dprior_ref, dj_ref, bias_ref, dk_acc, dv_acc = refs[-5:]
    step = pl.program_id(1)
    block = q_ref.shape[0]
    wide_lanes = 2 * HD
    lane = lax.broadcasted_iota(jnp.int32, (1, wide_lanes), 1)
    scale = 1.0 / math.sqrt(HD)
    q = q_ref[...]
    k = k_ref[...]
    v = v_ref[...]
    dc = dc_ref[...]

    @pl.when(step == 0)
    def _():
        dk_acc[...] = jnp.zeros_like(dk_acc)
        dv_acc[...] = jnp.zeros_like(dv_acc)
        bias_ref[...] = jnp.zeros_like(bias_ref)

    dq, dk, dv = [], [], []
    for h in range(2):
        mine = (lane >= HD) if h else (lane < HD)
        prob = prob_ref[h]
        wide = prob.astype(f32)
        d_prob = mm(jnp.where(mine, dc, jnp.zeros_like(dc)), v, NT)
        row_term = jnp.sum(wide * d_prob, axis=-1, keepdims=True)
        d_scores = (wide * (d_prob - row_term)).astype(bf16)
        dprior_ref[h] = d_scores
        dq.append(mm(d_scores, k))
        dk.append(mm(d_scores, q, TN))
        dv.append(mm(prob, dc, TN))
    first = lane < HD
    d_query = (jnp.where(first, dq[0], dq[1]) * scale).astype(bf16)
    dj_ref[pl.ds(pl.multiple_of(step * block, block), block), 0:wide_lanes] = d_query
    bias_ref[0, 0:1, :] += jnp.sum(d_query.astype(f32), axis=0, keepdims=True)
    dk_acc[...] += jnp.where(first, dk[0], dk[1])
    dv_acc[...] += jnp.where(first, dv[0], dv[1])

    @pl.when(step == pl.num_programs(1) - 1)
    def _():
        dj_ref[:, wide_lanes : 2 * wide_lanes] = (dk_acc[...] * scale).astype(bf16)
        d_value = dv_acc[...].astype(bf16)
        dj_ref[:, 2 * wide_lanes : 3 * wide_lanes] = d_value
        bias_ref[0, 1:2, :] = jnp.sum(d_value.astype(f32), axis=0, keepdims=True)


def attend_back(joint, d_context, prob, block, first, pairs, held):
    heads, total, _ = prob.shape
    wide = 2 * HD
    square = pl.BlockSpec((2, block, total), lambda t, i: (first + t, i, 0))
    return pl.pallas_call(
        attend_back_kernel,
        grid=(pairs, total // block),
        in_specs=[
            pl.BlockSpec((block, wide), lambda t, i: (i, 3 * (first + t))),
            pl.BlockSpec((total, wide), lambda t, i: (0, 3 * (first + t) + 1)),
            pl.BlockSpec((total, wide), lambda t, i: (0, 3 * (first + t) + 2)),
            pl.BlockSpec((block, wide), lambda t, i: (i, first + t)),
            square,
        ]
        + [pl.BlockSpec(memory_space=pl.ANY)] * len(held),
        out_specs=[
            square,
            pl.BlockSpec((total, 3 * wide), lambda t, i: (0, first + t)),
            pl.BlockSpec((1, 8, wide), lambda t, i: (first + t, 0, 0)),
        ],
        out_shape=[
            jax.ShapeDtypeStruct(prob.shape, bf16),
            jax.ShapeDtypeStruct((total, 3 * heads * HD), bf16),
            jax.ShapeDtypeStruct((heads // 2, 8, wide), f32),
        ],
        input_output_aliases={5 + k: k for k in range(len(held))},
        scratch_shapes=[pltpu.VMEM((total, wide), f32)] * 2,
        cost_estimate=pl.CostEstimate(flops=1000, transcendentals=0, bytes_accessed=1000),
        compiler_params=pltpu.CompilerParams(vmem_limit_bytes=56 << 20),
        name="attend_back",
    )(joint, joint, joint, d_context, prob, *held)


def put_blocks(sent_ref, kept_ref, odd, unit, first, blocks):
    blocks = blocks.astype(bf16)
    lower, upper = blocks[:, 0], blocks[:, 1]
    at = pl.ds(first, blocks.shape[0])
    sent_ref[unit, at] = jnp.where(odd, lower, upper)
    kept_ref[unit, at] = jnp.where(odd, upper, lower)


def back_grads_kernel(where_ref, act_ref, d_branch_ref, sent_ref, kept_ref):
    odd = (where_ref[0] & 1) == 1
    chunks, half_groups, r, width = sent_ref.shape
    each = half_groups // chunks
    d_branch = d_branch_ref[...]

    def chunk(c, carry):
        part = mm(act_ref[:, pl.ds(pl.multiple_of(c * width, 128), width)], d_branch, TN)
        part = part.reshape(each, 2, chunks, r, width)
        for q in range(chunks):
            put_blocks(sent_ref, kept_ref, odd, q, c * each, part[:, :, q])
        return carry

    lax.fori_loop(0, chunks, chunk, 0)


def grads_kernel(where_ref, *refs):
    ctx_own_refs, ctx_got_refs, refs = refs[:3], refs[3:6], refs[6:]
    d_att_ref, low_ref, d_inner_ref, first_sent, first_kept, rest_sent, rest_kept = refs
    odd = (where_ref[0] & 1) == 1
    side = where_ref[1]
    r, width = first_sent.shape[2:]
    groups = 2 * first_sent.shape[1]
    low = low_ref[...]

    def inner(c):
        return mm(low, d_inner_ref[c], TN).reshape(groups // 2, 2, r, width)

    def chunk(c, carry):
        put_blocks(rest_sent, rest_kept, odd, c, 0, inner(1 + c))
        return carry

    put_blocks(first_sent, first_kept, odd, 1, 0, inner(0))
    lax.fori_loop(0, rest_sent.shape[0], chunk, 0)
    d_att = d_att_ref[...]
    for part_refs, start in ((ctx_own_refs, side), (ctx_got_refs, 1 - side)):
        part = mm(jnp.concatenate([ref[...] for ref in part_refs], 1), d_att, TN)
        part = part.reshape(groups // 4, 2, r, width)
        put_blocks(first_sent, first_kept, odd, 0, start * (groups // 4), part)


def kernel_grads(kernel, units, where, arrays, groups, name):
    rows, width = arrays[-1].shape[-2:]
    vmem = pl.BlockSpec(memory_space=pltpu.VMEM)
    parts = [
        jax.ShapeDtypeStruct((count, groups // 2, width // groups, width), bf16)
        for count in units
        for _ in range(2)
    ]
    return pl.pallas_call(
        kernel,
        in_specs=[pl.BlockSpec(memory_space=pltpu.SMEM)] + [vmem] * len(arrays),
        out_specs=[vmem] * len(parts),
        out_shape=parts,
        cost_estimate=pl.CostEstimate(flops=1000, transcendentals=0, bytes_accessed=1000),
        compiler_params=pltpu.CompilerParams(vmem_limit_bytes=60 << 20),
        name=name,
    )(where, *arrays)


def feed_kernel(
    where_ref, *refs, codes, chunks,
):
    ctx_own_refs, ctx_got_refs, refs = refs[:3], refs[3:6], refs[6:]
    (tokens_ref, cot_ref, valid_ref, vec_ref, bias_in_ref), refs = refs[:5], refs[5:]
    weight_count = 2 if codes is None else 6
    weights, refs = refs[:weight_count], refs[weight_count:]
    (out_ref, low_ref, act_ref, d_branch_ref, d_inner_ref, d_att_ref, d_res_ref,
     d_own_ref, d_sent_ref, sums_ref, w_five, w_back, slope, sems) = refs
    me = where_ref[0]
    side = where_ref[1]
    width = tokens_ref.shape[1]
    half = width // 2

    def copies(chain):
        if codes is None:
            if chain == 2:
                return []
            target = (w_five, w_back)[chain]
            return [pltpu.make_async_copy(weights[chain], target, sems.at[chain])]
        made = []
        r = weights[0].shape[2]
        for b in range(2):
            source = weights[2 * chain + b]
            for s, (a, code) in enumerate(codes[chain]):
                column = pl.ds(pl.multiple_of((side ^ a) * half, 128), half)
                block = me ^ (code ^ b)
                rows = pl.ds(pl.multiple_of(block * r, 16), r)
                moves = (
                    ((0, 3, w_five.at[0:3, rows, column]),),
                    ((0, 2, w_five.at[3:5, rows, column]), (2, 1, w_back.at[block, 0:1, :, column])),
                    ((0, 3, w_back.at[block, 1:4, :, column]),),
                )[chain]
                for first, count, target in moves:
                    made.append(pltpu.make_async_copy(
                        source.at[s, pl.ds(first, count)], target, sems.at[chain]))
        return made

    groups = [copies(chain) for chain in range(3)]
    for group in groups:
        for copy in group:
            copy.start()

    def back_rows(c):
        if codes is None:
            return w_back[c * width : (c + 1) * width, :]
        per = w_back.shape[0] // chunks
        return w_back[c * per : (c + 1) * per].reshape(width, width)

    vec = vec_ref[...]
    proj_bias, first_gain, first_shift, outer_bias, second_gain, second_shift = (
        vec[k : k + 1] for k in range(2, 8)
    )
    own_rows = pl.ds(pl.multiple_of(side * half, 128), half)
    other_rows = pl.ds(pl.multiple_of((1 - side) * half, 128), half)
    valid = valid_ref[...]
    for copy in groups[0]:
        copy.wait()
    ctx_own = jnp.concatenate([ref[...] for ref in ctx_own_refs], 1)
    ctx_got = jnp.concatenate([ref[...] for ref in ctx_got_refs], 1)
    attended = (
        mm(ctx_own, w_five[0, own_rows, :]) + mm(ctx_got, w_five[0, other_rows, :]) + proj_bias
    )
    tokens_f = tokens_ref[...].astype(f32)

    def stat(row, values):
        total = jnp.sum(jnp.sum(values, axis=0, keepdims=True), axis=1, keepdims=True)
        sums_ref[row : row + 1, :] = jnp.broadcast_to(total, (1, width))

    def column_sum(row, values):
        sums_ref[row : row + 1, :] = jnp.sum(values, axis=0, keepdims=True)

    def normalize(values):
        centered = values - jnp.mean(values, axis=-1, keepdims=True)
        spread = lax.rsqrt(jnp.mean(centered * centered, axis=-1, keepdims=True) + eps_norm)
        return centered * spread, spread

    def normalize_back(grad, gain, normal, spread):
        e = grad * gain
        return spread * (
            e - jnp.mean(e, axis=-1, keepdims=True)
            - normal * jnp.mean(e * normal, axis=-1, keepdims=True)
        )

    stat(10, valid * tokens_f * tokens_f)
    stat(11, valid * attended * attended)
    stat(13, valid * jnp.ones((1, 128), f32) * (1.0 / 128.0))
    normal_one, spread_one = normalize(tokens_f + attended)
    hidden = normal_one * first_gain + first_shift
    hidden_low = hidden.astype(bf16)
    low_ref[...] = hidden_low
    for copy in groups[1] + groups[2]:
        copy.wait()
    branch = jnp.zeros_like(hidden)
    for c in range(chunks):
        inner = mm(hidden_low, w_five[1 + c]) + bias_in_ref[c : c + 1, :]
        below = 0.5 + 0.5 * lax.erf(inner * math.sqrt(0.5))
        slope[c] = below + inner * (jnp.exp(inner * inner * -0.5) * (1.0 / math.sqrt(2.0 * math.pi)))
        activated = (inner * below).astype(bf16)
        columns = slice(c * width, (c + 1) * width)
        act_ref[:, columns] = activated
        branch = branch + mm(activated, back_rows(c))
    branch = branch + outer_bias
    stat(12, valid * branch * branch)
    normal_two, spread_two = normalize(hidden + branch)
    out_ref[...] = (normal_two * second_gain + second_shift).astype(bf16)
    d_output = cot_ref[...].astype(f32) * valid
    column_sum(4, d_output * normal_two)
    column_sum(5, d_output)
    d_hidden = normalize_back(d_output, second_gain, normal_two, spread_two)
    d_branch = d_hidden.astype(bf16)
    d_branch_ref[...] = d_branch
    column_sum(3, d_branch.astype(f32))
    for c in range(chunks):
        columns = slice(c * width, (c + 1) * width)
        d_inner = (mm(d_branch, back_rows(c), NT) * slope[c]).astype(bf16)
        d_inner_ref[c] = d_inner
        column_sum(6 + c, d_inner.astype(f32))
        d_hidden = d_hidden + mm(d_inner, w_five[1 + c], NT)
    column_sum(1, d_hidden * normal_one)
    column_sum(2, d_hidden)
    d_res = normalize_back(d_hidden, first_gain, normal_one, spread_one)
    d_res_ref[...] = d_res
    d_att = d_res.astype(bf16)
    d_att_ref[...] = d_att
    column_sum(0, d_att.astype(f32))
    d_sent_ref[...] = mm(d_att, w_five[0, other_rows, :], NT).astype(bf16)
    d_own_ref[...] = mm(d_att, w_five[0, own_rows, :], NT).astype(bf16)


def feed(where, ctx_own, ctx_got, tokens, cot, valid, vec, bias_in, weights, codes, groups):
    rows, width = tokens.shape
    chunks = bias_in.shape[0]
    vmem = pl.BlockSpec(memory_space=pltpu.VMEM)
    hbm = pl.BlockSpec(memory_space=pl.ANY)
    flat = lambda *shape: jax.ShapeDtypeStruct(shape, bf16)
    return pl.pallas_call(
        functools.partial(feed_kernel, codes=codes, chunks=chunks),
        in_specs=[pl.BlockSpec(memory_space=pltpu.SMEM)] + [vmem] * 11 + [hbm] * len(weights),
        out_specs=[vmem] * 10,
        out_shape=[
            flat(rows, width),
            flat(rows, width),
            flat(rows, chunks * width),
            flat(rows, width),
            flat(chunks, rows, width),
            flat(rows, width),
            jax.ShapeDtypeStruct((rows, width), f32),
        ]
        + [flat(rows, width // 2)] * 2
        + [
            jax.ShapeDtypeStruct((16, width), f32),
        ],
        scratch_shapes=[
            pltpu.VMEM((chunks + 1, width, width), bf16),
            pltpu.VMEM((groups, 4, width // groups, width) if codes else (chunks * width, width), bf16),
            pltpu.VMEM((chunks, rows, width), f32),
            pltpu.SemaphoreType.DMA((3,)),
        ],
        cost_estimate=pl.CostEstimate(
            flops=2 * rows * width * width * (4 * chunks + 2),
            transcendentals=2 * rows * width * chunks,
            bytes_accessed=2 * width * width * (2 * chunks + 1) + 2 * rows * width * (2 * chunks + 8),
        ),
        compiler_params=pltpu.CompilerParams(vmem_limit_bytes=60 << 20),
        name="feed",
    )(where, *ctx_own, *ctx_got, tokens, cot, valid, vec, bias_in, *weights)


def plain_grads(ctx_own, ctx_got, d_attended, hidden_low, d_inner, activated, d_branch, chain_order):
    side = lax.axis_index("seq")
    mine = lax.axis_index("fsdp") & 1
    groups = lax.axis_size("fsdp")
    chunks, _, width = d_inner.shape
    piece = width // groups
    back = mm(activated, d_branch, TN).astype(bf16).reshape(groups // 2, 2, chunks, piece, width)
    own = jnp.concatenate(ctx_own, 1)
    got = jnp.concatenate(ctx_got, 1)
    context = jnp.where(side == 0, jnp.concatenate([own, got], 1), jnp.concatenate([got, own], 1))
    units = [mm(context, d_attended, TN)] + [mm(hidden_low, d_inner[c], TN) for c in range(chunks)]
    units = [unit.astype(bf16).reshape(groups // 2, 2, piece, width) for unit in units]
    units = units + [back[:, :, q] for q in range(chunks)]
    reductions = []
    for c, (first, last) in enumerate(((0, 2), (2, 5), (5, 9))):
        stacked = jnp.stack(units[first:last])
        sent = lax.dynamic_index_in_dim(stacked, 1 - mine, 2, keepdims=False)
        kept = lax.dynamic_index_in_dim(stacked, mine, 2, keepdims=False)
        reductions.append(Reduction([kept, swap(sent, "fsdp", 1)], chain_order[c]))
    return reductions


def body(
    tokens, prior_logits, lengths, order, cotangent, w_qkv, w_out, w_in, w_back,
    bias_q, bias_v, bias_o, gain_one, shift_one, bias_in, bias_back, gain_two, shift_two,
):
    side = lax.axis_index("seq")
    me = lax.axis_index("fsdp")
    groups = lax.axis_size("fsdp")
    rows = tokens[0]
    local_count, width = rows.shape
    total = 2 * local_count
    heads_local = prior_logits.shape[1]
    local_width = heads_local * HD
    piece = bias_q.shape[0]
    chunks = w_in.shape[1] // width
    pairs = range(heads_local // 2)
    top, *middle = reversed(bits_of(groups))
    where = jnp.stack([me, side]).astype(jnp.int32)

    other_rows = swap(rows, "seq", 1)
    own_qkv, nine, small = pack(
        where, w_qkv, w_out, w_in, w_back,
        (bias_q, bias_v, bias_o, gain_one, shift_one, bias_back, gain_two, shift_two, bias_in),
    )
    ascending = bits_of(groups)
    small_chain = Gather(small.astype(bf16))
    qkv_chain = Gather(own_qkv)
    *lower, low_bit, high_bit = ascending
    small_chain.step(lower[0])
    qkv_chain.top_two(low_bit, high_bit)
    order_column = order[0][:, None]
    small_chain.held, rows, order_column, qkv_chain.held = lax.optimization_barrier(
        (small_chain.held, rows, order_column, qkv_chain.held)
    )
    for bit in lower[1:]:
        small_chain.step(bit)
    for k, bit in enumerate(lower[::-1]):
        qkv_chain.step(bit)
        if k == 0:
            small_chain.held, qkv_chain.held = lax.optimization_barrier(
                (small_chain.held, qkv_chain.held)
            )
            small_chain.top_two(low_bit, high_bit)
    small_all = small_chain.held.astype(f32)
    qkv_weight = qkv_chain.held.reshape(width, 3 * local_width)
    vec = small_all[:, :8, :piece].transpose(1, 0, 2).reshape(8, width)
    inner_bias = small_all[:, 8, : chunks * piece].reshape(chunks, width)
    orders = chain_orders()
    nine = join(nine, receive(nine, top))
    chains = [nine[:, 3 * c : 3 * c + 3] for c in range(3)]
    codes = [[(0, 0), (0, top)]] * 3
    for step in range(len(orders[0])):
        codes = [more_slots(codes[c], orders[c][step]) for c in range(3)]
    for step in range(len(orders[0]) - 2):
        chains = [join(chains[c], receive(chains[c], orders[c][step])) for c in range(3)]
    third = [receive(chains[c], orders[c][-2]) for c in range(3)]

    order_row = order[0]
    length = lengths[0]
    scalars = jnp.stack([length, side]).astype(jnp.int32)
    own_order = lax.dynamic_slice_in_dim(order_row, side * local_count, local_count)
    other_order = lax.dynamic_slice_in_dim(order_row, (1 - side) * local_count, local_count)
    positions = jnp.arange(total, dtype=jnp.int32)
    own_pick = (positions[:, None] == own_order[None, :]).astype(bf16)
    other_pick = (positions[:, None] == other_order[None, :]).astype(bf16)

    def to_positions(own, other):
        return (mm(own_pick, own) + mm(other_pick, other)).astype(bf16)

    placed_rows = to_positions(rows, other_rows)
    own_cols = lambda vector: lax.dynamic_slice_in_dim(
        vector, side * local_width, local_width
    ).reshape(-1, 2 * HD)
    bias_cols = own_cols(vec[0])
    joint_bias = jnp.stack([bias_cols, jnp.zeros_like(bias_cols), own_cols(vec[1])], 1).reshape(-1)
    joint = (mm(placed_rows, qkv_weight) + joint_bias).astype(bf16)
    held = []
    ctx_own, ctx_got = [], []
    for t in pairs:
        raw_buf, prob_buf, own, sent = attend(
            joint, prior_logits[0], scalars, order_column, min(256, total), t, held
        )
        held = [raw_buf, prob_buf]
        if t == 0:
            joint, own, *tied = lax.optimization_barrier((joint, own, *chains, *third))
            chains = [join(tied[c], tied[3 + c]) for c in range(3)]
            joint, *chains = lax.optimization_barrier((joint, *chains))
            last = [receive(chains[c], orders[c][-1]) for c in range(3)]
        if t == len(pairs) - 2:
            joint, *ctx_got = lax.optimization_barrier((joint, *ctx_got))
        if t == len(pairs) - 1:
            own, sent, *tied = lax.optimization_barrier((own, sent, *ctx_got, *chains, *last))
            ctx_got = tied[:t]
            chains = [join(tied[t + c], tied[t + 3 + c]) for c in range(3)]
        ctx_own.append(own)
        ctx_got.append(swap(sent, "seq", 1))
    pieces = [(held, swap(held, "fsdp", 1)) for held in chains]
    if piece % 16 == 0:
        weights = [array for pair in pieces for array in pair]
    else:
        nine = jnp.concatenate([sort_pieces(*pieces[c], codes[c]) for c in range(3)], 0)
        weights = [
            nine[:5].reshape(5, width, width),
            nine[5:].transpose(1, 0, 2, 3).reshape(chunks * width, width),
        ]
        codes = None

    valid_rows = (own_order < length).astype(f32)[:, None]
    (out_rows, hidden_low, activated, d_branch, d_inner, d_attended, d_res_one,
     d_own, d_sent, sums) = feed(
        where, ctx_own, ctx_got, rows, cotangent[0], valid_rows, vec, inner_bias, weights, codes, groups
    )
    d_got = swap(d_sent, "seq", 1)

    chain_order = [orders[c][::-1] + [top] for c in range(3)]
    if codes is not None:
        back_parts = kernel_grads(
            back_grads_kernel, [chunks], where, [activated, d_branch], groups, "back_grads"
        )
        back_terms = [back_parts[1], swap(back_parts[0], "fsdp", 1)]
        d_inner, back_kept = lax.optimization_barrier((d_inner, back_parts[1]))
        parts = kernel_grads(
            grads_kernel, [2, chunks - 1], where,
            [*ctx_own, *ctx_got, d_attended, hidden_low, d_inner], groups, "grads",
        )
        d_got, *rest = lax.optimization_barrier((d_got, *parts[2:]))
        parts = list(parts[:2]) + rest
        back_terms[0] = back_kept
        reductions = [
            Reduction([parts[1], swap(parts[0], "fsdp", 1)], chain_order[0]),
            Reduction([parts[3], swap(parts[2], "fsdp", 1)], chain_order[1]),
            Reduction(back_terms, chain_order[2]),
        ]
    else:
        reductions = plain_grads(
            ctx_own, ctx_got, d_attended, hidden_low, d_inner, activated, d_branch, chain_order
        )

    def fence(*values):
        terms = tuple(term for reduction in reductions for term in reduction.terms)
        tied = lax.optimization_barrier(values + terms)
        for c, reduction in enumerate(reductions):
            reduction.terms = list(tied[len(values) + 2 * c : len(values) + 2 * c + 2])
        return tied[: len(values)]

    def advance(*values):
        sents = [reduction.sent() for reduction in reductions]
        tied = lax.optimization_barrier((*values, *sents))
        for reduction, sent in zip(reductions, tied[len(values) :]):
            reduction.launch(sent)
        return tied[: len(values)]

    d_context_pos = to_positions(d_own, d_got)
    (d_context_pos,) = fence(d_context_pos)
    (d_context_pos,) = advance(d_context_pos)
    block = min(256, total)
    held = []
    for t in pairs:
        if t == len(pairs) - 1:
            held = fence(*held)
            held = advance(*held)
        held = attend_back(joint, d_context_pos, prob_buf, block, t, 1, held)
    dprior_buf, d_joint, bias_sums = fence(*held)
    grad_w_qkv = mm(placed_rows, d_joint, TN).astype(bf16).reshape(1, groups, piece, -1)
    qkv = Reduction([grad_w_qkv], bits_of(groups))
    spread = lambda part: lax.dynamic_update_slice(
        jnp.zeros((1, width), f32), part.reshape(1, -1), (0, side * local_width)
    )
    sums = jnp.concatenate([sums[:14], spread(bias_sums[:, 0]), spread(bias_sums[:, 1])], 0)
    sent, sums, d_joint = advance(qkv.sent(), sums, d_joint)
    sums_got = [swap(sums, "fsdp", qkv.order[0])]
    qkv.launch(sent)
    d_rows = mm(d_joint, qkv_weight, NT).astype(bf16)
    d_rows_sent = mm(other_pick, d_rows, TN).astype(bf16)
    while len(reductions[0].order) > 1:
        (d_rows_sent,) = fence(d_rows_sent)
        (d_rows_sent,) = advance(d_rows_sent)

    d_rows_sent, sums, *rest = fence(d_rows_sent, sums, *sums_got, *qkv.terms)
    sums = sums + sum(rest[:-2])
    qkv.terms = rest[-2:]
    nine = Reduction(
        [jnp.concatenate([reduction.terms[k] for reduction in reductions], 0) for k in range(2)],
        [top],
    )
    d_rows_sent, sums, nine_sent, sent = lax.optimization_barrier(
        (d_rows_sent, sums, nine.sent(), qkv.sent())
    )
    nine.launch(nine_sent)
    d_rows_got = swap(d_rows_sent, "seq", 1)
    sums_got = [swap(sums, "fsdp", qkv.order[0])]
    qkv.launch(sent)
    while len(qkv.order) > 2:
        sums, *rest = lax.optimization_barrier((sums, *sums_got, *qkv.terms))
        sums = sums + sum(rest[:-2])
        qkv.terms = rest[-2:]
        sums_got = [swap(sums, "fsdp", qkv.order[0])]
        qkv.launch(qkv.sent())
    d_rows_own = mm(own_pick, d_rows, TN)

    d_rows_got, sums, sums_got[0], *rest = lax.optimization_barrier(
        (d_rows_got, sums, sums_got[0], *nine.terms, *qkv.terms)
    )
    sums = sums + sums_got[0]
    own_nine = (rest[0].astype(f32) + rest[1].astype(f32)).astype(bf16)[:, 0]
    four = (rest[2].astype(f32) + rest[3].astype(f32)).astype(bf16)[0]
    mine = ((me & low_bit) != 0) * 1 + ((me & high_bit) != 0) * 2
    peers = (low_bit, high_bit, low_bit | high_bit)
    blocks = [
        lax.dynamic_index_in_dim(four, mine ^ k, 0, keepdims=False) for k in range(4)
    ]
    own_nine, sums, *blocks = lax.optimization_barrier((own_nine, sums, *blocks))
    other_nine = swap(own_nine, "seq", 1)
    blocks[1:] = [swap(blocks[1 + k], "fsdp", peers[k]) for k in range(3)]
    sums_got = [swap(sums, "fsdp", peer) for peer in peers]
    tokens_grad = (d_res_one + d_rows_own + d_rows_got.astype(f32)).astype(bf16)

    other_nine, own_nine, sums, *rest = lax.optimization_barrier(
        (other_nine, own_nine, sums, *blocks, *sums_got)
    )
    own_qkv = sum(block.astype(f32) for block in rest[:4]).astype(bf16)
    sums = sums + sum(rest[4:])
    other_qkv = swap(own_qkv, "seq", 1)
    sums = sums + swap(sums, "seq", 1)

    def by_side(own, other, axis):
        return jnp.where(
            side == 0, jnp.concatenate([own, other], axis), jnp.concatenate([other, own], axis)
        ).astype(f32)

    out_nine = by_side(own_nine, other_nine, 2)
    shape = (piece, len(pairs), 3, 1, 2 * HD)
    out_qkv = by_side(own_qkv.reshape(shape), other_qkv.reshape(shape), 3)
    out_qkv = out_qkv.transpose(0, 2, 3, 1, 4).reshape(piece, 3 * width)
    rms = jnp.sqrt(sums[10:13, 0] / (sums[13, 0] * width))
    own_sums = lax.dynamic_slice_in_dim(sums, me * piece, piece, 1)
    own_inner = lax.dynamic_slice_in_dim(
        sums[6 : 6 + chunks].reshape(-1), me * chunks * piece, chunks * piece
    )
    return (
        out_rows[None],
        raw_buf[None],
        tokens_grad[None],
        dprior_buf[None],
        out_qkv,
        out_nine[0],
        jnp.concatenate([out_nine[1 + c] for c in range(chunks)], 1),
        out_nine[5:9].reshape(chunks * piece, width),
        own_sums[14],
        own_sums[15],
        own_sums[0],
        own_sums[1],
        own_sums[2],
        own_inner,
        own_sums[3],
        own_sums[4],
        own_sums[5],
        rms,
    )


def solution(mesh):
    shard = P("fsdp", "seq", None)
    heads = P("fsdp", "seq", None, None)
    mat = P("fsdp", None)
    vec = P("fsdp")
    return jax.shard_map(
        body,
        mesh=mesh,
        in_specs=(shard, heads, vec, mat, shard) + (mat,) * 4 + (vec,) * 9,
        out_specs=(shard, heads, shard, heads) + (mat,) * 4 + (vec,) * 9 + (P(),),
        check_vma=False,
    )
```

```python
import functools
import math

import jax
import jax.numpy as jnp
from jax import lax
from jax.experimental import pallas as pl
from jax.experimental.pallas import tpu as pltpu
from jax.sharding import PartitionSpec as P

HD = 64
eps_norm = 1e-05
masked_fill = -1e30
f32 = jnp.float32
bf16 = jnp.bfloat16

NT = (((1,), (1,)), ((), ()))
TN = (((0,), (0,)), ((), ()))


def mm(left, right, dims=(((1,), (0,)), ((), ()))):
    return lax.dot_general(left, right, dims, preferred_element_type=f32)


def bits_of(count):
    return [1 << k for k in range(count.bit_length() - 1)]


def swap(value, axis, bit):
    count = lax.axis_size(axis)
    return lax.ppermute(value, axis, [(i, i ^ bit) for i in range(count)])


class Gather:
    def __init__(self, shard):
        self.shape = shard.shape
        self.held = shard[None]
        self.done = []

    def step(self, bit):
        other = swap(self.held, "fsdp", bit)
        high = (lax.axis_index("fsdp") & bit) != 0
        outer = 1 << sum(1 for b in self.done if b > bit)
        self.done.append(bit)
        split = (outer, self.held.shape[0] // outer) + self.shape
        first = jnp.where(high, other, self.held).reshape(split)
        second = jnp.where(high, self.held, other).reshape(split)
        self.held = jnp.stack([first, second], axis=1).reshape((-1,) + self.shape)

    def top_two(self, low, high):
        me = lax.axis_index("fsdp")
        mine = ((me & low) != 0) * 1 + ((me & high) != 0) * 2
        got = [swap(self.held, "fsdp", peer) for peer in (low, high, low | high)]
        four = jnp.stack([self.held] + got)
        self.done += [low, high]
        self.held = jnp.concatenate(
            [lax.dynamic_index_in_dim(four, z ^ mine, 0, keepdims=False) for z in range(4)], 0
        )


def tie(value, *others):
    return lax.optimization_barrier((value,) + others)[0]


def chain_orders():
    rest = list(reversed(bits_of(lax.axis_size("fsdp"))))[1:-1]
    up = rest[::-1]
    return [up + ["seq"], rest[:-1] + ["seq"] + rest[-1:], ["seq"] + up]


def receive(held, stage):
    return swap(held, "seq", 1) if stage == "seq" else swap(held, "fsdp", stage)


def more_slots(slots, stage):
    if stage == "seq":
        return slots + [(a ^ 1, code) for a, code in slots]
    return slots + [(a, code ^ stage) for a, code in slots]


def join(held, got):
    return jnp.concatenate([held, got], axis=0)


def sort_pieces(own, other, slots):
    me = lax.axis_index("fsdp")
    side = lax.axis_index("seq")
    count = len(slots)
    both = jnp.concatenate([own, other], axis=0)
    place = [[0] * count, [0] * count]
    for s, (a, code) in enumerate(slots):
        place[a][code] = s
        place[a][code ^ 1] = s + count
    halves = [
        jnp.take(both, jnp.take(jnp.array(place[a], jnp.int32), jnp.arange(count) ^ me), axis=0)
        for a in range(2)
    ]
    joined = jnp.where(
        side == 0, jnp.concatenate(halves, -1), jnp.concatenate(halves[::-1], -1)
    )
    return joined.transpose(1, 0, 2, 3)


class Reduction:
    def __init__(self, terms, order):
        self.terms = terms
        self.order = order
        self.me = lax.axis_index("fsdp")
        self.side = lax.axis_index("seq")

    def pick(self, own):
        stage = self.order[0]
        picked = []
        for array in self.terms:
            if stage == "seq":
                size = array.shape[3] // 2
                index = self.side if own else 1 - self.side
                picked.append(lax.dynamic_slice_in_dim(array, index * size, size, 3))
            else:
                low = sum(1 for b in self.order if b != "seq" and b < stage)
                shape = array.shape
                array = array.reshape(
                    (shape[0], shape[1] >> (low + 1), 2, 1 << low) + shape[2:]
                )
                mine = ((self.me & stage) != 0).astype(jnp.int32)
                array = lax.dynamic_index_in_dim(
                    array, mine if own else 1 - mine, 2, keepdims=False
                )
                picked.append(array.reshape((shape[0], shape[1] // 2) + shape[2:]))
        total = picked[0].astype(f32)
        for other in picked[1:]:
            total = total + other.astype(f32)
        return total.astype(bf16)

    def sent(self):
        return self.pick(False)

    def launch(self, sent):
        kept = self.pick(True)
        stage = self.order[0]
        self.order = self.order[1:]
        axis, bit = ("seq", 1) if stage == "seq" else ("fsdp", stage)
        self.terms = [kept, swap(sent, axis, bit)]


def pack_kernel(where_ref, *refs):
    w_qkv, w_out, w_in, w_back = refs[:4]
    vectors, (qkv_ref, nine_ref, small_ref) = refs[4:13], refs[13:]
    r, width = w_out.shape
    half = width // 2
    columns = pl.ds(pl.multiple_of(where_ref[1] * half, 128), half)
    nine_ref[0, 0] = w_out[:, columns]
    for c in range(4):
        nine_ref[0, 1 + c] = w_in[:, pl.ds(pl.multiple_of(c * width + where_ref[1] * half, 128), half)]
        nine_ref[0, 5 + c] = w_back[c * r : (c + 1) * r, columns]
    for kind in range(3):
        for t in range(3):
            start = kind * width + where_ref[1] * half + t * 128
            qkv_ref[:, (3 * t + kind) * 128 : (3 * t + kind + 1) * 128] = w_qkv[
                :, pl.ds(pl.multiple_of(start, 128), 128)
            ]
    small_ref[...] = jnp.zeros_like(small_ref)
    for k, vector in enumerate(vectors):
        small_ref[k : k + 1, : vector.shape[1]] = vector[...].astype(f32)


def pack(where, w_qkv, w_out, w_in, w_back, vectors):
    r, width = w_out.shape
    vmem = pl.BlockSpec(memory_space=pltpu.VMEM)
    return pl.pallas_call(
        pack_kernel,
        in_specs=[pl.BlockSpec(memory_space=pltpu.SMEM)] + [vmem] * 13,
        out_specs=[vmem] * 3,
        out_shape=[
            jax.ShapeDtypeStruct((r, 3 * width // 2), bf16),
            jax.ShapeDtypeStruct((1, 9, r, width // 2), bf16),
            jax.ShapeDtypeStruct((16, 256), f32),
        ],
        name="pack",
    )(where, w_qkv, w_out, w_in, w_back, *[vector[None] for vector in vectors])


def attend_kernel(length_ref, q_ref, k_ref, v_ref, own_ref, other_ref, prior_ref, *refs):
    raw_ref, prob_ref, ctx_own_ref, ctx_sent_ref, ctx = refs[-5:]
    step = pl.program_id(0)
    block = q_ref.shape[0]
    keys = k_ref.shape[0]
    lane = lax.broadcasted_iota(jnp.int32, (1, 2 * HD), 1)
    seen = lax.broadcasted_iota(jnp.int32, (1, keys), 1) < length_ref[0]
    q = q_ref[...] * jnp.asarray(1.0 / math.sqrt(HD), bf16)
    k = k_ref[...]
    v = v_ref[...]
    parts = []
    for h in range(2):
        mine = (lane >= HD) if h else (lane < HD)
        scores = mm(jnp.where(mine, q, jnp.zeros_like(q)), k, NT) + prior_ref[h].astype(f32)
        raw_ref[h] = scores.astype(bf16)
        masked = jnp.where(seen, scores, masked_fill)
        largest = jnp.max(masked, axis=-1, keepdims=True)
        exponent = jnp.exp(masked - largest)
        inverse = 1.0 / jnp.sum(exponent, axis=-1, keepdims=True)
        prob = (exponent * inverse).astype(bf16)
        prob_ref[h] = prob
        parts.append(mm(prob, v))
    ctx[pl.ds(pl.multiple_of(step * block, block), block), :] = jnp.where(
        lane < HD, parts[0], parts[1]
    ).astype(bf16)

    @pl.when(step == pl.num_programs(0) - 1)
    def _():
        position = lax.broadcasted_iota(jnp.int32, (own_ref.shape[0], keys), 1)
        placed = ctx[...]
        for order_ref, out_ref in ((other_ref, ctx_sent_ref), (own_ref, ctx_own_ref)):
            pick = jnp.where(position == order_ref[...], 1.0, 0.0).astype(bf16)
            out_ref[...] = mm(pick, placed).astype(bf16)


def attend(joint, prior, scalars, order_column, block, pair, held):
    heads, total, _ = prior.shape
    wide = 2 * HD
    square = pl.BlockSpec((2, block, total), lambda i, *_: (pair, i, 0))
    hbm = pl.BlockSpec(memory_space=pl.ANY)
    local = order_column.shape[0] // 2
    stored = pl.BlockSpec((local, wide), lambda i, *_: (0, 0))
    return pl.pallas_call(
        attend_kernel,
        grid_spec=pltpu.PrefetchScalarGridSpec(
            num_scalar_prefetch=1,
            grid=(total // block,),
            in_specs=[
                pl.BlockSpec((block, wide), lambda i, *_: (i, 3 * pair)),
                pl.BlockSpec((total, wide), lambda i, *_: (0, 3 * pair + 1)),
                pl.BlockSpec((total, wide), lambda i, *_: (0, 3 * pair + 2)),
                pl.BlockSpec((local, 1), lambda i, scalars: (scalars[1], 0)),
                pl.BlockSpec((local, 1), lambda i, scalars: (1 - scalars[1], 0)),
                square,
            ]
            + [hbm] * len(held),
            out_specs=[square, square, stored, stored],
            scratch_shapes=[pltpu.VMEM((total, wide), bf16)],
        ),
        out_shape=[
            jax.ShapeDtypeStruct(prior.shape, bf16),
            jax.ShapeDtypeStruct(prior.shape, bf16),
            jax.ShapeDtypeStruct((local, wide), bf16),
            jax.ShapeDtypeStruct((local, wide), bf16),
        ],
        input_output_aliases={7 + k: k for k in range(len(held))},
        cost_estimate=pl.CostEstimate(flops=1000, transcendentals=0, bytes_accessed=1000),
        compiler_params=pltpu.CompilerParams(vmem_limit_bytes=56 << 20),
        name="attend",
    )(scalars, joint, joint, joint, order_column, order_column, prior, *held)


def attend_back_kernel(q_ref, k_ref, v_ref, dc_ref, prob_ref, *refs):
    dprior_ref, dj_ref, bias_ref, dk_acc, dv_acc = refs[-5:]
    step = pl.program_id(1)
    block = q_ref.shape[0]
    wide_lanes = 2 * HD
    lane = lax.broadcasted_iota(jnp.int32, (1, wide_lanes), 1)
    scale = 1.0 / math.sqrt(HD)
    q = q_ref[...]
    k = k_ref[...]
    v = v_ref[...]
    dc = dc_ref[...]

    @pl.when(step == 0)
    def _():
        dk_acc[...] = jnp.zeros_like(dk_acc)
        dv_acc[...] = jnp.zeros_like(dv_acc)
        bias_ref[...] = jnp.zeros_like(bias_ref)

    dq, dk, dv = [], [], []
    for h in range(2):
        mine = (lane >= HD) if h else (lane < HD)
        prob = prob_ref[h]
        wide = prob.astype(f32)
        d_prob = mm(jnp.where(mine, dc, jnp.zeros_like(dc)), v, NT)
        row_term = jnp.sum(wide * d_prob, axis=-1, keepdims=True)
        d_scores = (wide * (d_prob - row_term)).astype(bf16)
        dprior_ref[h] = d_scores
        dq.append(mm(d_scores, k))
        dk.append(mm(d_scores, q, TN))
        dv.append(mm(prob, dc, TN))
    first = lane < HD
    d_query = (jnp.where(first, dq[0], dq[1]) * scale).astype(bf16)
    dj_ref[pl.ds(pl.multiple_of(step * block, block), block), 0:wide_lanes] = d_query
    bias_ref[0:1, :] += jnp.sum(d_query.astype(f32), axis=0, keepdims=True)
    dk_acc[...] += jnp.where(first, dk[0], dk[1])
    dv_acc[...] += jnp.where(first, dv[0], dv[1])

    @pl.when(step == pl.num_programs(1) - 1)
    def _():
        dj_ref[:, wide_lanes : 2 * wide_lanes] = (dk_acc[...] * scale).astype(bf16)
        d_value = dv_acc[...].astype(bf16)
        dj_ref[:, 2 * wide_lanes : 3 * wide_lanes] = d_value
        bias_ref[1:2, :] = jnp.sum(d_value.astype(f32), axis=0, keepdims=True)


def attend_back(joint, d_context, prob, block, first, pairs, held):
    heads, total, _ = prob.shape
    wide = 2 * HD
    square = pl.BlockSpec((2, block, total), lambda t, i: (first + t, i, 0))
    return pl.pallas_call(
        attend_back_kernel,
        grid=(pairs, total // block),
        in_specs=[
            pl.BlockSpec((block, wide), lambda t, i: (i, 3 * (first + t))),
            pl.BlockSpec((total, wide), lambda t, i: (0, 3 * (first + t) + 1)),
            pl.BlockSpec((total, wide), lambda t, i: (0, 3 * (first + t) + 2)),
            pl.BlockSpec((block, wide), lambda t, i: (i, first + t)),
            square,
        ]
        + [pl.BlockSpec(memory_space=pl.ANY)] * len(held),
        out_specs=[
            square,
            pl.BlockSpec((total, 3 * wide), lambda t, i: (0, first + t)),
            pl.BlockSpec((8, wide), lambda t, i: (0, first + t)),
        ],
        out_shape=[
            jax.ShapeDtypeStruct(prob.shape, bf16),
            jax.ShapeDtypeStruct((total, 3 * heads * HD), bf16),
            jax.ShapeDtypeStruct((8, heads * HD), f32),
        ],
        input_output_aliases={5 + k: k for k in range(len(held))},
        scratch_shapes=[pltpu.VMEM((total, wide), f32)] * 2,
        cost_estimate=pl.CostEstimate(flops=1000, transcendentals=0, bytes_accessed=1000),
        compiler_params=pltpu.CompilerParams(vmem_limit_bytes=56 << 20),
        name="attend_back",
    )(joint, joint, joint, d_context, prob, *held)


def put_blocks(sent_ref, kept_ref, odd, unit, first, blocks):
    blocks = blocks.astype(bf16)
    lower, upper = blocks[:, 0], blocks[:, 1]
    at = pl.ds(first, blocks.shape[0])
    sent_ref[unit, at] = jnp.where(odd, lower, upper)
    kept_ref[unit, at] = jnp.where(odd, upper, lower)


def back_grads_kernel(where_ref, act_ref, d_branch_ref, sent_ref, kept_ref):
    odd = (where_ref[0] & 1) == 1
    chunks, half_groups, r, width = sent_ref.shape
    each = half_groups // chunks
    d_branch = d_branch_ref[...]

    def chunk(c, carry):
        part = mm(act_ref[:, pl.ds(pl.multiple_of(c * width, 128), width)], d_branch, TN)
        part = part.reshape(each, 2, chunks, r, width)
        for q in range(chunks):
            put_blocks(sent_ref, kept_ref, odd, q, c * each, part[:, :, q])
        return carry

    lax.fori_loop(0, chunks, chunk, 0)


def grads_kernel(where_ref, *refs):
    ctx_own_refs, ctx_got_refs, refs = refs[:3], refs[3:6], refs[6:]
    d_att_ref, low_ref, d_inner_ref, first_sent, first_kept, rest_sent, rest_kept = refs
    odd = (where_ref[0] & 1) == 1
    side = where_ref[1]
    r, width = first_sent.shape[2:]
    groups = 2 * first_sent.shape[1]
    low = low_ref[...]

    def inner(c):
        return mm(low, d_inner_ref[c], TN).reshape(groups // 2, 2, r, width)

    def chunk(c, carry):
        put_blocks(rest_sent, rest_kept, odd, c, 0, inner(1 + c))
        return carry

    put_blocks(first_sent, first_kept, odd, 1, 0, inner(0))
    lax.fori_loop(0, rest_sent.shape[0], chunk, 0)
    d_att = d_att_ref[...]
    for part_refs, start in ((ctx_own_refs, side), (ctx_got_refs, 1 - side)):
        part = mm(jnp.concatenate([ref[...] for ref in part_refs], 1), d_att, TN)
        part = part.reshape(groups // 4, 2, r, width)
        put_blocks(first_sent, first_kept, odd, 0, start * (groups // 4), part)


def kernel_grads(kernel, units, where, arrays, groups, name):
    rows, width = arrays[-1].shape[-2:]
    vmem = pl.BlockSpec(memory_space=pltpu.VMEM)
    parts = [
        jax.ShapeDtypeStruct((count, groups // 2, width // groups, width), bf16)
        for count in units
        for _ in range(2)
    ]
    return pl.pallas_call(
        kernel,
        in_specs=[pl.BlockSpec(memory_space=pltpu.SMEM)] + [vmem] * len(arrays),
        out_specs=[vmem] * len(parts),
        out_shape=parts,
        cost_estimate=pl.CostEstimate(flops=1000, transcendentals=0, bytes_accessed=1000),
        compiler_params=pltpu.CompilerParams(vmem_limit_bytes=60 << 20),
        name=name,
    )(where, *arrays)


def feed_kernel(
    where_ref, *refs, codes, chunks,
):
    ctx_own_refs, ctx_got_refs, refs = refs[:3], refs[3:6], refs[6:]
    (tokens_ref, cot_ref, valid_ref, vec_ref, bias_in_ref), refs = refs[:5], refs[5:]
    weight_count = 2 if codes is None else 6
    weights, refs = refs[:weight_count], refs[weight_count:]
    (out_ref, low_ref, act_ref, d_branch_ref, d_inner_ref, d_att_ref, d_res_ref,
     d_own_ref, d_sent_ref, sums_ref, w_five, w_back, slope, sems) = refs
    me = where_ref[0]
    side = where_ref[1]
    width = tokens_ref.shape[1]
    half = width // 2

    def copies(chain):
        if codes is None:
            if chain == 2:
                return []
            target = (w_five, w_back)[chain]
            return [pltpu.make_async_copy(weights[chain], target, sems.at[chain])]
        made = []
        r = weights[0].shape[2]
        for b in range(2):
            source = weights[2 * chain + b]
            for s, (a, code) in enumerate(codes[chain]):
                column = pl.ds(pl.multiple_of((side ^ a) * half, 128), half)
                block = me ^ (code ^ b)
                rows = pl.ds(pl.multiple_of(block * r, 16), r)
                moves = (
                    ((0, 3, w_five.at[0:3, rows, column]),),
                    ((0, 2, w_five.at[3:5, rows, column]), (2, 1, w_back.at[block, 0:1, :, column])),
                    ((0, 3, w_back.at[block, 1:4, :, column]),),
                )[chain]
                for first, count, target in moves:
                    made.append(pltpu.make_async_copy(
                        source.at[s, pl.ds(first, count)], target, sems.at[chain]))
        return made

    groups = [copies(chain) for chain in range(3)]
    for group in groups:
        for copy in group:
            copy.start()

    def back_rows(c):
        if codes is None:
            return w_back[pl.ds(pl.multiple_of(c * width, 128), width), :]
        per = w_back.shape[0] // chunks
        return w_back[pl.ds(c * per, per)].reshape(width, width)

    vec = vec_ref[...]
    proj_bias, first_gain, first_shift, outer_bias, second_gain, second_shift = (
        vec[k : k + 1] for k in range(2, 8)
    )
    own_rows = pl.ds(pl.multiple_of(side * half, 128), half)
    other_rows = pl.ds(pl.multiple_of((1 - side) * half, 128), half)
    valid = valid_ref[...]
    for copy in groups[0]:
        copy.wait()
    ctx_own = jnp.concatenate([ref[...] for ref in ctx_own_refs], 1)
    ctx_got = jnp.concatenate([ref[...] for ref in ctx_got_refs], 1)
    attended = (
        mm(ctx_own, w_five[0, own_rows, :]) + mm(ctx_got, w_five[0, other_rows, :]) + proj_bias
    )
    tokens_f = tokens_ref[...].astype(f32)

    def stat(row, values):
        total = jnp.sum(jnp.sum(values, axis=0, keepdims=True), axis=1, keepdims=True)
        sums_ref[row : row + 1, :] = jnp.broadcast_to(total, (1, width))

    def column_sum(row, values):
        sums_ref[row : row + 1, :] = jnp.sum(values, axis=0, keepdims=True)

    def normalize(values):
        centered = values - jnp.mean(values, axis=-1, keepdims=True)
        spread = lax.rsqrt(jnp.mean(centered * centered, axis=-1, keepdims=True) + eps_norm)
        return centered * spread, spread

    def normalize_back(grad, gain, normal, spread):
        e = grad * gain
        return spread * (
            e - jnp.mean(e, axis=-1, keepdims=True)
            - normal * jnp.mean(e * normal, axis=-1, keepdims=True)
        )

    stat(10, valid * tokens_f * tokens_f)
    stat(11, valid * attended * attended)
    stat(13, valid * jnp.ones((1, 128), f32) * (1.0 / 128.0))
    normal_one, spread_one = normalize(tokens_f + attended)
    hidden = normal_one * first_gain + first_shift
    hidden_low = hidden.astype(bf16)
    low_ref[...] = hidden_low
    for copy in groups[1] + groups[2]:
        copy.wait()

    def forward(c, branch):
        inner = mm(hidden_low, w_five[1 + c]) + bias_in_ref[pl.ds(c, 1), :]
        below = 0.5 + 0.5 * lax.erf(inner * math.sqrt(0.5))
        slope[c] = below + inner * (jnp.exp(inner * inner * -0.5) * (1.0 / math.sqrt(2.0 * math.pi)))
        activated = (inner * below).astype(bf16)
        act_ref[:, pl.ds(pl.multiple_of(c * width, 128), width)] = activated
        return branch + mm(activated, back_rows(c))

    branch = lax.fori_loop(0, chunks, forward, jnp.zeros_like(hidden))
    branch = branch + outer_bias
    stat(12, valid * branch * branch)
    normal_two, spread_two = normalize(hidden + branch)
    out_ref[...] = (normal_two * second_gain + second_shift).astype(bf16)
    d_output = cot_ref[...].astype(f32) * valid
    column_sum(4, d_output * normal_two)
    column_sum(5, d_output)
    d_hidden = normalize_back(d_output, second_gain, normal_two, spread_two)
    d_branch = d_hidden.astype(bf16)
    d_branch_ref[...] = d_branch
    column_sum(3, d_branch.astype(f32))

    def backward(c, d_hidden):
        d_inner = (mm(d_branch, back_rows(c), NT) * slope[c]).astype(bf16)
        d_inner_ref[c] = d_inner
        sums_ref[pl.ds(6 + c, 1), :] = jnp.sum(d_inner.astype(f32), axis=0, keepdims=True)
        return d_hidden + mm(d_inner, w_five[1 + c], NT)

    d_hidden = lax.fori_loop(0, chunks, backward, d_hidden)
    column_sum(1, d_hidden * normal_one)
    column_sum(2, d_hidden)
    d_res = normalize_back(d_hidden, first_gain, normal_one, spread_one)
    d_res_ref[...] = d_res
    d_att = d_res.astype(bf16)
    d_att_ref[...] = d_att
    column_sum(0, d_att.astype(f32))
    d_sent_ref[...] = mm(d_att, w_five[0, other_rows, :], NT).astype(bf16)
    d_own_ref[...] = mm(d_att, w_five[0, own_rows, :], NT).astype(bf16)


def feed(where, ctx_own, ctx_got, tokens, cot, valid, vec, bias_in, weights, codes, groups):
    rows, width = tokens.shape
    chunks = bias_in.shape[0]
    vmem = pl.BlockSpec(memory_space=pltpu.VMEM)
    hbm = pl.BlockSpec(memory_space=pl.ANY)
    flat = lambda *shape: jax.ShapeDtypeStruct(shape, bf16)
    return pl.pallas_call(
        functools.partial(feed_kernel, codes=codes, chunks=chunks),
        in_specs=[pl.BlockSpec(memory_space=pltpu.SMEM)] + [vmem] * 11 + [hbm] * len(weights),
        out_specs=[vmem] * 10,
        out_shape=[
            flat(rows, width),
            flat(rows, width),
            flat(rows, chunks * width),
            flat(rows, width),
            flat(chunks, rows, width),
            flat(rows, width),
            jax.ShapeDtypeStruct((rows, width), f32),
        ]
        + [flat(rows, width // 2)] * 2
        + [
            jax.ShapeDtypeStruct((16, width), f32),
        ],
        scratch_shapes=[
            pltpu.VMEM((chunks + 1, width, width), bf16),
            pltpu.VMEM((groups, 4, width // groups, width) if codes else (chunks * width, width), bf16),
            pltpu.VMEM((chunks, rows, width), f32),
            pltpu.SemaphoreType.DMA((3,)),
        ],
        cost_estimate=pl.CostEstimate(
            flops=2 * rows * width * width * (4 * chunks + 2),
            transcendentals=2 * rows * width * chunks,
            bytes_accessed=2 * width * width * (2 * chunks + 1) + 2 * rows * width * (2 * chunks + 8),
        ),
        compiler_params=pltpu.CompilerParams(vmem_limit_bytes=60 << 20),
        name="feed",
    )(where, *ctx_own, *ctx_got, tokens, cot, valid, vec, bias_in, *weights)


def plain_grads(ctx_own, ctx_got, d_attended, hidden_low, d_inner, activated, d_branch, chain_order):
    side = lax.axis_index("seq")
    mine = lax.axis_index("fsdp") & 1
    groups = lax.axis_size("fsdp")
    chunks, _, width = d_inner.shape
    piece = width // groups
    back = mm(activated, d_branch, TN).astype(bf16).reshape(groups // 2, 2, chunks, piece, width)
    own = jnp.concatenate(ctx_own, 1)
    got = jnp.concatenate(ctx_got, 1)
    context = jnp.where(side == 0, jnp.concatenate([own, got], 1), jnp.concatenate([got, own], 1))
    units = [mm(context, d_attended, TN)] + [mm(hidden_low, d_inner[c], TN) for c in range(chunks)]
    units = [unit.astype(bf16).reshape(groups // 2, 2, piece, width) for unit in units]
    units = units + [back[:, :, q] for q in range(chunks)]
    reductions = []
    for c, (first, last) in enumerate(((0, 2), (2, 5), (5, 9))):
        stacked = jnp.stack(units[first:last])
        sent = lax.dynamic_index_in_dim(stacked, 1 - mine, 2, keepdims=False)
        kept = lax.dynamic_index_in_dim(stacked, mine, 2, keepdims=False)
        reductions.append(Reduction([kept, swap(sent, "fsdp", 1)], chain_order[c]))
    return reductions


def body(
    tokens, prior_logits, lengths, order, cotangent, w_qkv, w_out, w_in, w_back,
    bias_q, bias_v, bias_o, gain_one, shift_one, bias_in, bias_back, gain_two, shift_two,
):
    side = lax.axis_index("seq")
    me = lax.axis_index("fsdp")
    groups = lax.axis_size("fsdp")
    rows = tokens[0]
    local_count, width = rows.shape
    total = 2 * local_count
    heads_local = prior_logits.shape[1]
    local_width = heads_local * HD
    piece = bias_q.shape[0]
    chunks = w_in.shape[1] // width
    pairs = range(heads_local // 2)
    top, *middle = reversed(bits_of(groups))
    where = jnp.stack([me, side]).astype(jnp.int32)

    other_rows = swap(rows, "seq", 1)
    own_qkv, nine, small = pack(
        where, w_qkv, w_out, w_in, w_back,
        (bias_q, bias_v, bias_o, gain_one, shift_one, bias_back, gain_two, shift_two, bias_in),
    )
    ascending = bits_of(groups)
    small_chain = Gather(small.astype(bf16))
    qkv_chain = Gather(own_qkv)
    *lower, low_bit, high_bit = ascending
    small_chain.step(lower[0])
    qkv_chain.top_two(low_bit, high_bit)
    order_column = order[0][:, None]
    small_chain.held, rows, order_column, qkv_chain.held = lax.optimization_barrier(
        (small_chain.held, rows, order_column, qkv_chain.held)
    )
    for bit in lower[1:]:
        small_chain.step(bit)
    for k, bit in enumerate(lower[::-1]):
        qkv_chain.step(bit)
        if k == 0:
            small_chain.held, qkv_chain.held = lax.optimization_barrier(
                (small_chain.held, qkv_chain.held)
            )
            small_chain.top_two(low_bit, high_bit)
    small_all = small_chain.held.astype(f32)
    qkv_weight = qkv_chain.held.reshape(width, 3 * local_width)
    vec = small_all[:, :8, :piece].transpose(1, 0, 2).reshape(8, width)
    inner_bias = small_all[:, 8, : chunks * piece].reshape(chunks, width)
    orders = chain_orders()
    nine = join(nine, receive(nine, top))
    chains = [nine[:, 3 * c : 3 * c + 3] for c in range(3)]
    codes = [[(0, 0), (0, top)]] * 3
    for step in range(len(orders[0])):
        codes = [more_slots(codes[c], orders[c][step]) for c in range(3)]
    for step in range(len(orders[0]) - 2):
        chains = [join(chains[c], receive(chains[c], orders[c][step])) for c in range(3)]
    third = [receive(chains[c], orders[c][-2]) for c in range(3)]

    order_row = order[0]
    length = lengths[0]
    scalars = jnp.stack([length, side]).astype(jnp.int32)
    own_order = lax.dynamic_slice_in_dim(order_row, side * local_count, local_count)
    other_order = lax.dynamic_slice_in_dim(order_row, (1 - side) * local_count, local_count)
    positions = jnp.arange(total, dtype=jnp.int32)
    own_pick = (positions[:, None] == own_order[None, :]).astype(bf16)
    other_pick = (positions[:, None] == other_order[None, :]).astype(bf16)

    def to_positions(own, other):
        return (mm(own_pick, own) + mm(other_pick, other)).astype(bf16)

    placed_rows = to_positions(rows, other_rows)
    own_cols = lambda vector: lax.dynamic_slice_in_dim(
        vector, side * local_width, local_width
    ).reshape(-1, 2 * HD)
    bias_cols = own_cols(vec[0])
    joint_bias = jnp.stack([bias_cols, jnp.zeros_like(bias_cols), own_cols(vec[1])], 1).reshape(-1)
    joint = (mm(placed_rows, qkv_weight) + joint_bias).astype(bf16)
    held = []
    ctx_own, ctx_got = [], []
    for t in pairs:
        raw_buf, prob_buf, own, sent = attend(
            joint, prior_logits[0], scalars, order_column, min(256, total), t, held
        )
        held = [raw_buf, prob_buf]
        if t == 0:
            joint, own, *tied = lax.optimization_barrier((joint, own, *chains, *third))
            chains = [join(tied[c], tied[3 + c]) for c in range(3)]
            joint, *chains = lax.optimization_barrier((joint, *chains))
            last = [receive(chains[c], orders[c][-1]) for c in range(3)]
        if t == len(pairs) - 1:
            own, sent, *tied = lax.optimization_barrier((own, sent, *ctx_got, *chains, *last))
            ctx_got = tied[:t]
            chains = [join(tied[t + c], tied[t + 3 + c]) for c in range(3)]
        ctx_own.append(own)
        ctx_got.append(swap(sent, "seq", 1))
    pieces = [(held, swap(held, "fsdp", 1)) for held in chains]
    if piece % 16 == 0:
        weights = [array for pair in pieces for array in pair]
    else:
        nine = jnp.concatenate([sort_pieces(*pieces[c], codes[c]) for c in range(3)], 0)
        weights = [
            nine[:5].reshape(5, width, width),
            nine[5:].transpose(1, 0, 2, 3).reshape(chunks * width, width),
        ]
        codes = None

    valid_rows = (own_order < length).astype(f32)[:, None]
    (out_rows, hidden_low, activated, d_branch, d_inner, d_attended, d_res_one,
     d_own, d_sent, sums) = feed(
        where, ctx_own, ctx_got, rows, cotangent[0], valid_rows, vec, inner_bias, weights, codes, groups
    )
    d_got = swap(d_sent, "seq", 1)

    chain_order = [orders[c][::-1] + [top] for c in range(3)]
    if codes is not None:
        back_parts = kernel_grads(
            back_grads_kernel, [chunks], where, [activated, d_branch], groups, "back_grads"
        )
        back_terms = [back_parts[1], swap(back_parts[0], "fsdp", 1)]
        d_inner, back_kept = lax.optimization_barrier((d_inner, back_parts[1]))
        parts = kernel_grads(
            grads_kernel, [2, chunks - 1], where,
            [*ctx_own, *ctx_got, d_attended, hidden_low, d_inner], groups, "grads",
        )
        d_got, *rest = lax.optimization_barrier((d_got, *parts[2:]))
        parts = list(parts[:2]) + rest
        back_terms[0] = back_kept
        reductions = [
            Reduction([parts[1], swap(parts[0], "fsdp", 1)], chain_order[0]),
            Reduction([parts[3], swap(parts[2], "fsdp", 1)], chain_order[1]),
            Reduction(back_terms, chain_order[2]),
        ]
    else:
        reductions = plain_grads(
            ctx_own, ctx_got, d_attended, hidden_low, d_inner, activated, d_branch, chain_order
        )

    def fence(*values):
        terms = tuple(term for reduction in reductions for term in reduction.terms)
        tied = lax.optimization_barrier(values + terms)
        for c, reduction in enumerate(reductions):
            reduction.terms = list(tied[len(values) + 2 * c : len(values) + 2 * c + 2])
        return tied[: len(values)]

    def advance(*values):
        sents = [reduction.sent() for reduction in reductions]
        tied = lax.optimization_barrier((*values, *sents))
        for reduction, sent in zip(reductions, tied[len(values) :]):
            reduction.launch(sent)
        return tied[: len(values)]

    d_context_pos = to_positions(d_own, d_got)
    (d_context_pos,) = fence(d_context_pos)
    (d_context_pos,) = advance(d_context_pos)
    block = min(256, total)
    held = []
    held = attend_back(joint, d_context_pos, prob_buf, block, 0, len(pairs) - 1, held)
    held = advance(*fence(*held))
    held = attend_back(joint, d_context_pos, prob_buf, block, len(pairs) - 1, 1, held)
    dprior_buf, d_joint, bias_sums = fence(*held)
    grad_w_qkv = mm(placed_rows, d_joint, TN).astype(bf16).reshape(1, groups, piece, -1)
    qkv = Reduction([grad_w_qkv], bits_of(groups))
    bias_row = jnp.concatenate([bias_sums[0:1], bias_sums[1:2]], 1)
    own_row = lax.broadcasted_iota(jnp.int32, (2, width), 0) == side
    sums = jnp.concatenate([sums[:14], jnp.where(own_row, bias_row, 0.0)], 0)
    sent, sums, d_joint = advance(qkv.sent(), sums, d_joint)
    sums_got = [swap(sums, "fsdp", qkv.order[0])]
    qkv.launch(sent)
    d_rows = mm(d_joint, qkv_weight, NT).astype(bf16)
    d_rows_sent = mm(other_pick, d_rows, TN).astype(bf16)
    while len(reductions[0].order) > 1:
        (d_rows_sent,) = fence(d_rows_sent)
        (d_rows_sent,) = advance(d_rows_sent)

    d_rows_sent, sums, *rest = fence(d_rows_sent, sums, *sums_got, *qkv.terms)
    sums = sums + sum(rest[:-2])
    qkv.terms = rest[-2:]
    nine = Reduction(
        [jnp.concatenate([reduction.terms[k] for reduction in reductions], 0) for k in range(2)],
        [top],
    )
    d_rows_sent, sums, nine_sent, sent = lax.optimization_barrier(
        (d_rows_sent, sums, nine.sent(), qkv.sent())
    )
    nine.launch(nine_sent)
    d_rows_got = swap(d_rows_sent, "seq", 1)
    sums_got = [swap(sums, "fsdp", qkv.order[0])]
    qkv.launch(sent)
    while len(qkv.order) > 2:
        sums, *rest = lax.optimization_barrier((sums, *sums_got, *qkv.terms))
        sums = sums + sum(rest[:-2])
        qkv.terms = rest[-2:]
        sums_got = [swap(sums, "fsdp", qkv.order[0])]
        qkv.launch(qkv.sent())
    d_rows_own = mm(own_pick, d_rows, TN)
    low_bit, high_bit = qkv.order
    sums = sums + sums_got[0]
    sums_got = [swap(sums, "fsdp", low_bit)]

    d_rows_got, sums, sums_got[0], *rest = lax.optimization_barrier(
        (d_rows_got, sums, sums_got[0], *nine.terms, *qkv.terms)
    )
    sums = sums + sums_got[0]
    own_nine = (rest[0].astype(f32) + rest[1].astype(f32)).astype(bf16)[:, 0]
    four = (rest[2].astype(f32) + rest[3].astype(f32)).astype(bf16)[0]
    mine = ((me & low_bit) != 0) * 1 + ((me & high_bit) != 0) * 2
    peers = (low_bit, high_bit, low_bit | high_bit)
    blocks = [
        lax.dynamic_index_in_dim(four, mine ^ k, 0, keepdims=False) for k in range(4)
    ]
    own_nine, sums, *blocks = lax.optimization_barrier((own_nine, sums, *blocks))
    other_nine = swap(own_nine, "seq", 1)
    blocks[1:] = [swap(blocks[1 + k], "fsdp", peers[k]) for k in range(3)]
    sums_got = [swap(sums, "fsdp", high_bit)]
    tokens_grad = (d_res_one + d_rows_own + d_rows_got.astype(f32)).astype(bf16)

    other_nine, own_nine, sums, *rest = lax.optimization_barrier(
        (other_nine, own_nine, sums, *blocks, *sums_got)
    )
    own_qkv = sum(block.astype(f32) for block in rest[:4]).astype(bf16)
    sums = sums + sum(rest[4:])
    other_qkv = swap(own_qkv, "seq", 1)
    sums = sums + swap(sums, "seq", 1)

    def by_side(own, other, axis):
        return jnp.where(
            side == 0, jnp.concatenate([own, other], axis), jnp.concatenate([other, own], axis)
        ).astype(f32)

    out_nine = by_side(own_nine, other_nine, 2)
    shape = (piece, len(pairs), 3, 1, 2 * HD)
    out_qkv = by_side(own_qkv.reshape(shape), other_qkv.reshape(shape), 3)
    out_qkv = out_qkv.transpose(0, 2, 3, 1, 4).reshape(piece, 3 * width)
    rms = jnp.sqrt(sums[10:13, 0] / (sums[13, 0] * width))
    own_sums = lax.dynamic_slice_in_dim(sums, me * piece, piece, 1)
    bias_grads = jnp.concatenate(
        [sums[14:15].reshape(2, local_width), sums[15:16].reshape(2, local_width)], 1
    )
    bias_grads = lax.dynamic_slice_in_dim(bias_grads, me * piece, piece, 1)
    own_inner = lax.dynamic_slice_in_dim(
        sums[6 : 6 + chunks].reshape(-1), me * chunks * piece, chunks * piece
    )
    return (
        out_rows[None],
        raw_buf[None],
        tokens_grad[None],
        dprior_buf[None],
        out_qkv,
        out_nine[0],
        jnp.concatenate([out_nine[1 + c] for c in range(chunks)], 1),
        out_nine[5:9].reshape(chunks * piece, width),
        bias_grads[0],
        bias_grads[1],
        own_sums[0],
        own_sums[1],
        own_sums[2],
        own_inner,
        own_sums[3],
        own_sums[4],
        own_sums[5],
        rms,
    )


def solution(mesh):
    shard = P("fsdp", "seq", None)
    heads = P("fsdp", "seq", None, None)
    mat = P("fsdp", None)
    vec = P("fsdp")
    return jax.shard_map(
        body,
        mesh=mesh,
        in_specs=(shard, heads, vec, mat, shard) + (mat,) * 4 + (vec,) * 9,
        out_specs=(shard, heads, shard, heads) + (mat,) * 4 + (vec,) * 9 + (P(),),
        check_vma=False,
    )
```

```python
import functools
import math

import jax
import jax.numpy as jnp
from jax import lax
from jax.experimental import pallas as pl
from jax.experimental.pallas import tpu as pltpu
from jax.sharding import PartitionSpec as P

HD = 64
eps_norm = 1e-05
masked_fill = -1e30
f32 = jnp.float32
bf16 = jnp.bfloat16

NT = (((1,), (1,)), ((), ()))
TN = (((0,), (0,)), ((), ()))


def mm(left, right, dims=(((1,), (0,)), ((), ()))):
    return lax.dot_general(left, right, dims, preferred_element_type=f32)


def bits_of(count):
    return [1 << k for k in range(count.bit_length() - 1)]


def swap(value, axis, bit):
    count = lax.axis_size(axis)
    return lax.ppermute(value, axis, [(i, i ^ bit) for i in range(count)])


class Gather:
    def __init__(self, shard):
        self.shape = shard.shape
        self.held = shard[None]
        self.done = []

    def step(self, bit):
        other = swap(self.held, "fsdp", bit)
        high = (lax.axis_index("fsdp") & bit) != 0
        outer = 1 << sum(1 for b in self.done if b > bit)
        self.done.append(bit)
        split = (outer, self.held.shape[0] // outer) + self.shape
        first = jnp.where(high, other, self.held).reshape(split)
        second = jnp.where(high, self.held, other).reshape(split)
        self.held = jnp.stack([first, second], axis=1).reshape((-1,) + self.shape)

    def top_two(self, low, high):
        me = lax.axis_index("fsdp")
        mine = ((me & low) != 0) * 1 + ((me & high) != 0) * 2
        got = [swap(self.held, "fsdp", peer) for peer in (low, high, low | high)]
        four = jnp.stack([self.held] + got)
        self.done += [low, high]
        self.held = jnp.concatenate(
            [lax.dynamic_index_in_dim(four, z ^ mine, 0, keepdims=False) for z in range(4)], 0
        )


def tie(value, *others):
    return lax.optimization_barrier((value,) + others)[0]


def chain_orders():
    rest = list(reversed(bits_of(lax.axis_size("fsdp"))))[1:-1]
    up = rest[::-1]
    return [up + ["seq"], rest[:-1] + ["seq"] + rest[-1:], ["seq"] + up]


def receive(held, stage):
    return swap(held, "seq", 1) if stage == "seq" else swap(held, "fsdp", stage)


def more_slots(slots, stage):
    if stage == "seq":
        return slots + [(a ^ 1, code) for a, code in slots]
    return slots + [(a, code ^ stage) for a, code in slots]


def join(held, got):
    return jnp.concatenate([held, got], axis=0)


def sort_pieces(own, other, slots):
    me = lax.axis_index("fsdp")
    side = lax.axis_index("seq")
    count = len(slots)
    both = jnp.concatenate([own, other], axis=0)
    place = [[0] * count, [0] * count]
    for s, (a, code) in enumerate(slots):
        place[a][code] = s
        place[a][code ^ 1] = s + count
    halves = [
        jnp.take(both, jnp.take(jnp.array(place[a], jnp.int32), jnp.arange(count) ^ me), axis=0)
        for a in range(2)
    ]
    joined = jnp.where(
        side == 0, jnp.concatenate(halves, -1), jnp.concatenate(halves[::-1], -1)
    )
    return joined.transpose(1, 0, 2, 3)


class Reduction:
    def __init__(self, terms, order):
        self.terms = terms
        self.order = order
        self.me = lax.axis_index("fsdp")
        self.side = lax.axis_index("seq")

    def pick(self, own):
        stage = self.order[0]
        picked = []
        for array in self.terms:
            if stage == "seq":
                size = array.shape[3] // 2
                index = self.side if own else 1 - self.side
                picked.append(lax.dynamic_slice_in_dim(array, index * size, size, 3))
            else:
                low = sum(1 for b in self.order if b != "seq" and b < stage)
                shape = array.shape
                array = array.reshape(
                    (shape[0], shape[1] >> (low + 1), 2, 1 << low) + shape[2:]
                )
                mine = ((self.me & stage) != 0).astype(jnp.int32)
                array = lax.dynamic_index_in_dim(
                    array, mine if own else 1 - mine, 2, keepdims=False
                )
                picked.append(array.reshape((shape[0], shape[1] // 2) + shape[2:]))
        total = picked[0].astype(f32)
        for other in picked[1:]:
            total = total + other.astype(f32)
        return total.astype(bf16)

    def sent(self):
        return self.pick(False)

    def launch(self, sent):
        kept = self.pick(True)
        stage = self.order[0]
        self.order = self.order[1:]
        axis, bit = ("seq", 1) if stage == "seq" else ("fsdp", stage)
        self.terms = [kept, swap(sent, axis, bit)]


def pack_kernel(where_ref, *refs):
    w_qkv, w_out, w_in, w_back = refs[:4]
    vectors, (qkv_ref, nine_ref, small_ref) = refs[4:13], refs[13:]
    r, width = w_out.shape
    half = width // 2
    columns = pl.ds(pl.multiple_of(where_ref[1] * half, 128), half)
    nine_ref[0, 0] = w_out[:, columns]
    for c in range(4):
        nine_ref[0, 1 + c] = w_in[:, pl.ds(pl.multiple_of(c * width + where_ref[1] * half, 128), half)]
        nine_ref[0, 5 + c] = w_back[c * r : (c + 1) * r, columns]
    for kind in range(3):
        for t in range(3):
            start = kind * width + where_ref[1] * half + t * 128
            qkv_ref[:, (3 * t + kind) * 128 : (3 * t + kind + 1) * 128] = w_qkv[
                :, pl.ds(pl.multiple_of(start, 128), 128)
            ]
    small_ref[...] = jnp.zeros_like(small_ref)
    for k, vector in enumerate(vectors):
        small_ref[k : k + 1, : vector.shape[1]] = vector[...].astype(f32)


def pack(where, w_qkv, w_out, w_in, w_back, vectors):
    r, width = w_out.shape
    vmem = pl.BlockSpec(memory_space=pltpu.VMEM)
    return pl.pallas_call(
        pack_kernel,
        in_specs=[pl.BlockSpec(memory_space=pltpu.SMEM)] + [vmem] * 13,
        out_specs=[vmem] * 3,
        out_shape=[
            jax.ShapeDtypeStruct((r, 3 * width // 2), bf16),
            jax.ShapeDtypeStruct((1, 9, r, width // 2), bf16),
            jax.ShapeDtypeStruct((16, 256), f32),
        ],
        name="pack",
    )(where, w_qkv, w_out, w_in, w_back, *[vector[None] for vector in vectors])


def attend_kernel(length_ref, q_ref, k_ref, v_ref, own_ref, other_ref, prior_ref, *refs):
    raw_ref, prob_ref, ctx_own_ref, ctx_sent_ref, ctx = refs[-5:]
    step = pl.program_id(1)
    block = q_ref.shape[0]
    keys = k_ref.shape[0]
    lane = lax.broadcasted_iota(jnp.int32, (1, 2 * HD), 1)
    seen = lax.broadcasted_iota(jnp.int32, (1, keys), 1) < length_ref[0]
    q = q_ref[...] * jnp.asarray(1.0 / math.sqrt(HD), bf16)
    k = k_ref[...]
    v = v_ref[...]
    parts = []
    for h in range(2):
        mine = (lane >= HD) if h else (lane < HD)
        scores = mm(jnp.where(mine, q, jnp.zeros_like(q)), k, NT) + prior_ref[h].astype(f32)
        raw_ref[h] = scores.astype(bf16)
        masked = jnp.where(seen, scores, masked_fill)
        largest = jnp.max(masked, axis=-1, keepdims=True)
        exponent = jnp.exp(masked - largest)
        inverse = 1.0 / jnp.sum(exponent, axis=-1, keepdims=True)
        prob = (exponent * inverse).astype(bf16)
        prob_ref[h] = prob
        parts.append(mm(prob, v))
    ctx[pl.ds(pl.multiple_of(step * block, block), block), :] = jnp.where(
        lane < HD, parts[0], parts[1]
    ).astype(bf16)

    @pl.when(step == pl.num_programs(1) - 1)
    def _():
        position = lax.broadcasted_iota(jnp.int32, (own_ref.shape[0], keys), 1)
        placed = ctx[...]
        for order_ref, out_ref in ((other_ref, ctx_sent_ref), (own_ref, ctx_own_ref)):
            pick = jnp.where(position == order_ref[...], 1.0, 0.0).astype(bf16)
            out_ref[...] = mm(pick, placed).astype(bf16)


def attend(joint, prior, scalars, order_column, block, first, pairs, held):
    heads, total, _ = prior.shape
    wide = 2 * HD
    square = pl.BlockSpec((2, block, total), lambda t, i, *_: (first + t, i, 0))
    hbm = pl.BlockSpec(memory_space=pl.ANY)
    local = order_column.shape[0] // 2
    stored = pl.BlockSpec((local, wide), lambda t, i, *_: (0, t))
    return pl.pallas_call(
        attend_kernel,
        grid_spec=pltpu.PrefetchScalarGridSpec(
            num_scalar_prefetch=1,
            grid=(pairs, total // block),
            in_specs=[
                pl.BlockSpec((block, wide), lambda t, i, *_: (i, 3 * (first + t))),
                pl.BlockSpec((total, wide), lambda t, i, *_: (0, 3 * (first + t) + 1)),
                pl.BlockSpec((total, wide), lambda t, i, *_: (0, 3 * (first + t) + 2)),
                pl.BlockSpec((local, 1), lambda t, i, scalars: (scalars[1], 0)),
                pl.BlockSpec((local, 1), lambda t, i, scalars: (1 - scalars[1], 0)),
                square,
            ]
            + [hbm] * len(held),
            out_specs=[square, square, stored, stored],
            scratch_shapes=[pltpu.VMEM((total, wide), bf16)],
        ),
        out_shape=[
            jax.ShapeDtypeStruct(prior.shape, bf16),
            jax.ShapeDtypeStruct(prior.shape, bf16),
            jax.ShapeDtypeStruct((local, pairs * wide), bf16),
            jax.ShapeDtypeStruct((local, pairs * wide), bf16),
        ],
        input_output_aliases={7 + k: k for k in range(len(held))},
        cost_estimate=pl.CostEstimate(flops=1000, transcendentals=0, bytes_accessed=1000),
        compiler_params=pltpu.CompilerParams(vmem_limit_bytes=56 << 20),
        name="attend",
    )(scalars, joint, joint, joint, order_column, order_column, prior, *held)


def place_kernel(own_order_ref, other_order_ref, own_ref, other_ref, out_ref):
    block = out_ref.shape[0]
    count = own_ref.shape[0]
    position = lax.broadcasted_iota(jnp.int32, (block, count), 0) + pl.program_id(0) * block
    parts = []
    for order_ref, ref in ((own_order_ref, own_ref), (other_order_ref, other_ref)):
        pick = jnp.where(position == order_ref[...], 1.0, 0.0).astype(bf16)
        parts.append(mm(pick, ref[...]))
    out_ref[...] = (parts[0] + parts[1]).astype(bf16)


def place(own_order, other_order, own, other, block):
    count, width = own.shape
    whole = lambda *shape: pl.BlockSpec(shape, lambda i: (0, 0))
    return pl.pallas_call(
        place_kernel,
        grid=(2 * count // block,),
        in_specs=[whole(1, count)] * 2 + [whole(count, width)] * 2,
        out_specs=pl.BlockSpec((block, width), lambda i: (i, 0)),
        out_shape=jax.ShapeDtypeStruct((2 * count, width), bf16),
        compiler_params=pltpu.CompilerParams(vmem_limit_bytes=56 << 20),
        name="place",
    )(own_order, other_order, own, other)


def rows_back_kernel(dj_ref, w_ref, own_ref, other_ref, sent_ref, d_own_ref, rows):
    step = pl.program_id(0)
    block = dj_ref.shape[0]
    rows[pl.ds(pl.multiple_of(step * block, block), block), :] = mm(
        dj_ref[...], w_ref[...], NT
    ).astype(bf16)

    @pl.when(step == pl.num_programs(0) - 1)
    def _():
        position = lax.broadcasted_iota(jnp.int32, (own_ref.shape[0], rows.shape[0]), 1)
        for order_ref, out_ref in ((other_ref, sent_ref), (own_ref, d_own_ref)):
            pick = jnp.where(position == order_ref[...], 1.0, 0.0).astype(bf16)
            out_ref[...] = mm(pick, rows[...]).astype(out_ref.dtype)


def rows_back(d_joint, weight, own_column, other_column, block):
    total, joined = d_joint.shape
    width = weight.shape[0]
    local = own_column.shape[0]
    whole = lambda *shape: pl.BlockSpec(shape, lambda i: (0, 0))
    return pl.pallas_call(
        rows_back_kernel,
        grid=(total // block,),
        in_specs=[
            pl.BlockSpec((block, joined), lambda i: (i, 0)),
            whole(width, joined),
            whole(local, 1),
            whole(local, 1),
        ],
        out_specs=[whole(local, width)] * 2,
        out_shape=[
            jax.ShapeDtypeStruct((local, width), bf16),
            jax.ShapeDtypeStruct((local, width), f32),
        ],
        scratch_shapes=[pltpu.VMEM((total, width), bf16)],
        compiler_params=pltpu.CompilerParams(vmem_limit_bytes=56 << 20),
        name="rows_back",
    )(d_joint, weight, own_column, other_column)


def attend_back_kernel(q_ref, k_ref, v_ref, dc_ref, prob_ref, *refs):
    dprior_ref, dj_ref, bias_ref, dk_acc, dv_acc = refs[-5:]
    step = pl.program_id(1)
    block = q_ref.shape[0]
    wide_lanes = 2 * HD
    lane = lax.broadcasted_iota(jnp.int32, (1, wide_lanes), 1)
    scale = 1.0 / math.sqrt(HD)
    q = q_ref[...]
    k = k_ref[...]
    v = v_ref[...]
    dc = dc_ref[...]

    @pl.when(step == 0)
    def _():
        dk_acc[...] = jnp.zeros_like(dk_acc)
        dv_acc[...] = jnp.zeros_like(dv_acc)
        bias_ref[...] = jnp.zeros_like(bias_ref)

    dq, dk, dv = [], [], []
    for h in range(2):
        mine = (lane >= HD) if h else (lane < HD)
        prob = prob_ref[h]
        wide = prob.astype(f32)
        d_prob = mm(jnp.where(mine, dc, jnp.zeros_like(dc)), v, NT)
        row_term = jnp.sum(wide * d_prob, axis=-1, keepdims=True)
        d_scores = (wide * (d_prob - row_term)).astype(bf16)
        dprior_ref[h] = d_scores
        dq.append(mm(d_scores, k))
        dk.append(mm(d_scores, q, TN))
        dv.append(mm(prob, dc, TN))
    first = lane < HD
    d_query = (jnp.where(first, dq[0], dq[1]) * scale).astype(bf16)
    dj_ref[pl.ds(pl.multiple_of(step * block, block), block), 0:wide_lanes] = d_query
    bias_ref[0:1, :] += jnp.sum(d_query.astype(f32), axis=0, keepdims=True)
    dk_acc[...] += jnp.where(first, dk[0], dk[1])
    dv_acc[...] += jnp.where(first, dv[0], dv[1])

    @pl.when(step == pl.num_programs(1) - 1)
    def _():
        dj_ref[:, wide_lanes : 2 * wide_lanes] = (dk_acc[...] * scale).astype(bf16)
        d_value = dv_acc[...].astype(bf16)
        dj_ref[:, 2 * wide_lanes : 3 * wide_lanes] = d_value
        bias_ref[1:2, :] = jnp.sum(d_value.astype(f32), axis=0, keepdims=True)


def attend_back(joint, d_context, prob, block, first, pairs, held):
    heads, total, _ = prob.shape
    wide = 2 * HD
    square = pl.BlockSpec((2, block, total), lambda t, i: (first + t, i, 0))
    return pl.pallas_call(
        attend_back_kernel,
        grid=(pairs, total // block),
        in_specs=[
            pl.BlockSpec((block, wide), lambda t, i: (i, 3 * (first + t))),
            pl.BlockSpec((total, wide), lambda t, i: (0, 3 * (first + t) + 1)),
            pl.BlockSpec((total, wide), lambda t, i: (0, 3 * (first + t) + 2)),
            pl.BlockSpec((block, wide), lambda t, i: (i, first + t)),
            square,
        ]
        + [pl.BlockSpec(memory_space=pl.ANY)] * len(held),
        out_specs=[
            square,
            pl.BlockSpec((total, 3 * wide), lambda t, i: (0, first + t)),
            pl.BlockSpec((8, wide), lambda t, i: (0, first + t)),
        ],
        out_shape=[
            jax.ShapeDtypeStruct(prob.shape, bf16),
            jax.ShapeDtypeStruct((total, 3 * heads * HD), bf16),
            jax.ShapeDtypeStruct((8, heads * HD), f32),
        ],
        input_output_aliases={5 + k: k for k in range(len(held))},
        scratch_shapes=[pltpu.VMEM((total, wide), f32)] * 2,
        cost_estimate=pl.CostEstimate(flops=1000, transcendentals=0, bytes_accessed=1000),
        compiler_params=pltpu.CompilerParams(vmem_limit_bytes=56 << 20),
        name="attend_back",
    )(joint, joint, joint, d_context, prob, *held)


def put_blocks(sent_ref, kept_ref, odd, unit, first, blocks):
    blocks = blocks.astype(bf16)
    lower, upper = blocks[:, 0], blocks[:, 1]
    at = pl.ds(first, blocks.shape[0])
    sent_ref[unit, at] = jnp.where(odd, lower, upper)
    kept_ref[unit, at] = jnp.where(odd, upper, lower)


def back_grads_kernel(where_ref, act_ref, d_branch_ref, sent_ref, kept_ref):
    odd = (where_ref[0] & 1) == 1
    chunks, half_groups, r, width = sent_ref.shape
    each = half_groups // chunks
    d_branch = d_branch_ref[...]

    def chunk(c, carry):
        part = mm(act_ref[:, pl.ds(pl.multiple_of(c * width, 128), width)], d_branch, TN)
        part = part.reshape(each, 2, chunks, r, width)
        for q in range(chunks):
            put_blocks(sent_ref, kept_ref, odd, q, c * each, part[:, :, q])
        return carry

    lax.fori_loop(0, chunks, chunk, 0)


def grads_kernel(where_ref, *refs):
    ctx_own_refs, ctx_got_refs, refs = refs[:2], refs[2:4], refs[4:]
    d_att_ref, low_ref, d_inner_ref, first_sent, first_kept, rest_sent, rest_kept = refs
    odd = (where_ref[0] & 1) == 1
    side = where_ref[1]
    r, width = first_sent.shape[2:]
    groups = 2 * first_sent.shape[1]
    low = low_ref[...]

    def inner(c):
        return mm(low, d_inner_ref[c], TN).reshape(groups // 2, 2, r, width)

    def chunk(c, carry):
        put_blocks(rest_sent, rest_kept, odd, c, 0, inner(1 + c))
        return carry

    put_blocks(first_sent, first_kept, odd, 1, 0, inner(0))
    lax.fori_loop(0, rest_sent.shape[0], chunk, 0)
    d_att = d_att_ref[...]
    for part_refs, start in ((ctx_own_refs, side), (ctx_got_refs, 1 - side)):
        part = mm(jnp.concatenate([ref[...] for ref in part_refs], 1), d_att, TN)
        part = part.reshape(groups // 4, 2, r, width)
        put_blocks(first_sent, first_kept, odd, 0, start * (groups // 4), part)


def kernel_grads(kernel, units, where, arrays, groups, name):
    rows, width = arrays[-1].shape[-2:]
    vmem = pl.BlockSpec(memory_space=pltpu.VMEM)
    parts = [
        jax.ShapeDtypeStruct((count, groups // 2, width // groups, width), bf16)
        for count in units
        for _ in range(2)
    ]
    return pl.pallas_call(
        kernel,
        in_specs=[pl.BlockSpec(memory_space=pltpu.SMEM)] + [vmem] * len(arrays),
        out_specs=[vmem] * len(parts),
        out_shape=parts,
        cost_estimate=pl.CostEstimate(flops=1000, transcendentals=0, bytes_accessed=1000),
        compiler_params=pltpu.CompilerParams(vmem_limit_bytes=60 << 20),
        name=name,
    )(where, *arrays)


def feed_kernel(
    where_ref, *refs, codes, chunks,
):
    ctx_own_refs, ctx_got_refs, refs = refs[:2], refs[2:4], refs[4:]
    (tokens_ref, cot_ref, valid_ref, vec_ref, bias_in_ref), refs = refs[:5], refs[5:]
    weight_count = 2 if codes is None else 6
    weights, refs = refs[:weight_count], refs[weight_count:]
    (out_ref, low_ref, act_ref, d_branch_ref, d_inner_ref, d_att_ref, d_res_ref,
     d_own_ref, d_sent_ref, sums_ref, w_five, w_back, slope, sems) = refs
    me = where_ref[0]
    side = where_ref[1]
    width = tokens_ref.shape[1]
    half = width // 2

    def copies(chain):
        if codes is None:
            if chain == 2:
                return []
            target = (w_five, w_back)[chain]
            return [pltpu.make_async_copy(weights[chain], target, sems.at[chain])]
        made = []
        r = weights[0].shape[2]
        for b in range(2):
            source = weights[2 * chain + b]
            for s, (a, code) in enumerate(codes[chain]):
                column = pl.ds(pl.multiple_of((side ^ a) * half, 128), half)
                block = me ^ (code ^ b)
                rows = pl.ds(pl.multiple_of(block * r, 16), r)
                moves = (
                    ((0, 3, w_five.at[0:3, rows, column]),),
                    ((0, 2, w_five.at[3:5, rows, column]), (2, 1, w_back.at[block, 0:1, :, column])),
                    ((0, 3, w_back.at[block, 1:4, :, column]),),
                )[chain]
                for first, count, target in moves:
                    made.append(pltpu.make_async_copy(
                        source.at[s, pl.ds(first, count)], target, sems.at[chain]))
        return made

    groups = [copies(chain) for chain in range(3)]
    for group in groups:
        for copy in group:
            copy.start()

    def back_rows(c):
        if codes is None:
            return w_back[pl.ds(pl.multiple_of(c * width, 128), width), :]
        per = w_back.shape[0] // chunks
        return w_back[pl.ds(c * per, per)].reshape(width, width)

    vec = vec_ref[...]
    proj_bias, first_gain, first_shift, outer_bias, second_gain, second_shift = (
        vec[k : k + 1] for k in range(2, 8)
    )
    own_rows = pl.ds(pl.multiple_of(side * half, 128), half)
    other_rows = pl.ds(pl.multiple_of((1 - side) * half, 128), half)
    sums_ref[...] = jnp.zeros_like(sums_ref)
    block = tokens_ref.shape[0] // 2

    def rows_half(i, carry):
        rs = pl.ds(pl.multiple_of(i * block, block), block)
        valid = valid_ref[rs, :]
        @pl.when(i == 0)
        def _():
            for copy in groups[0]:
                copy.wait()

        ctx_own = jnp.concatenate([ref[rs, :] for ref in ctx_own_refs], 1)
        ctx_got = jnp.concatenate([ref[rs, :] for ref in ctx_got_refs], 1)
        attended = (
            mm(ctx_own, w_five[0, own_rows, :]) + mm(ctx_got, w_five[0, other_rows, :]) + proj_bias
        )
        tokens_f = tokens_ref[rs, :].astype(f32)

        def stat(row, values):
            total = jnp.sum(jnp.sum(values, axis=0, keepdims=True), axis=1, keepdims=True)
            sums_ref[row : row + 1, :] += jnp.broadcast_to(total, (1, width))

        def column_sum(row, values):
            sums_ref[row : row + 1, :] += jnp.sum(values, axis=0, keepdims=True)

        def normalize(values):
            centered = values - jnp.mean(values, axis=-1, keepdims=True)
            spread = lax.rsqrt(jnp.mean(centered * centered, axis=-1, keepdims=True) + eps_norm)
            return centered * spread, spread

        def normalize_back(grad, gain, normal, spread):
            e = grad * gain
            return spread * (
                e - jnp.mean(e, axis=-1, keepdims=True)
                - normal * jnp.mean(e * normal, axis=-1, keepdims=True)
            )

        stat(10, valid * tokens_f * tokens_f)
        stat(11, valid * attended * attended)
        stat(13, valid * jnp.ones((1, 128), f32) * (1.0 / 128.0))
        normal_one, spread_one = normalize(tokens_f + attended)
        hidden = normal_one * first_gain + first_shift
        hidden_low = hidden.astype(bf16)
        low_ref[rs, :] = hidden_low

        @pl.when(i == 0)
        def _():
            for copy in groups[1] + groups[2]:
                copy.wait()

        def forward(c, branch):
            inner = mm(hidden_low, w_five[1 + c]) + bias_in_ref[pl.ds(c, 1), :]
            below = 0.5 + 0.5 * lax.erf(inner * math.sqrt(0.5))
            slope[c] = below + inner * (jnp.exp(inner * inner * -0.5) * (1.0 / math.sqrt(2.0 * math.pi)))
            activated = (inner * below).astype(bf16)
            act_ref[rs, pl.ds(pl.multiple_of(c * width, 128), width)] = activated
            return branch + mm(activated, back_rows(c))

        branch = lax.fori_loop(0, chunks, forward, jnp.zeros_like(hidden))
        branch = branch + outer_bias
        stat(12, valid * branch * branch)
        normal_two, spread_two = normalize(hidden + branch)
        out_ref[rs, :] = (normal_two * second_gain + second_shift).astype(bf16)
        d_output = cot_ref[rs, :].astype(f32) * valid
        column_sum(4, d_output * normal_two)
        column_sum(5, d_output)
        d_hidden = normalize_back(d_output, second_gain, normal_two, spread_two)
        d_branch = d_hidden.astype(bf16)
        d_branch_ref[rs, :] = d_branch
        column_sum(3, d_branch.astype(f32))

        def backward(c, d_hidden):
            d_inner = (mm(d_branch, back_rows(c), NT) * slope[c]).astype(bf16)
            d_inner_ref[c, rs, :] = d_inner
            sums_ref[pl.ds(6 + c, 1), :] += jnp.sum(d_inner.astype(f32), axis=0, keepdims=True)
            return d_hidden + mm(d_inner, w_five[1 + c], NT)

        d_hidden = lax.fori_loop(0, chunks, backward, d_hidden)
        column_sum(1, d_hidden * normal_one)
        column_sum(2, d_hidden)
        d_res = normalize_back(d_hidden, first_gain, normal_one, spread_one)
        d_res_ref[rs, :] = d_res
        d_att = d_res.astype(bf16)
        d_att_ref[rs, :] = d_att
        column_sum(0, d_att.astype(f32))
        d_sent_ref[rs, :] = mm(d_att, w_five[0, other_rows, :], NT).astype(bf16)
        d_own_ref[rs, :] = mm(d_att, w_five[0, own_rows, :], NT).astype(bf16)
        return carry

    lax.fori_loop(0, 2, rows_half, 0)


def feed(where, ctx_own, ctx_got, tokens, cot, valid, vec, bias_in, weights, codes, groups):
    rows, width = tokens.shape
    chunks = bias_in.shape[0]
    vmem = pl.BlockSpec(memory_space=pltpu.VMEM)
    hbm = pl.BlockSpec(memory_space=pl.ANY)
    flat = lambda *shape: jax.ShapeDtypeStruct(shape, bf16)
    return pl.pallas_call(
        functools.partial(feed_kernel, codes=codes, chunks=chunks),
        in_specs=[pl.BlockSpec(memory_space=pltpu.SMEM)] + [vmem] * 9 + [hbm] * len(weights),
        out_specs=[vmem] * 10,
        out_shape=[
            flat(rows, width),
            flat(rows, width),
            flat(rows, chunks * width),
            flat(rows, width),
            flat(chunks, rows, width),
            flat(rows, width),
            jax.ShapeDtypeStruct((rows, width), f32),
        ]
        + [flat(rows, width // 2)] * 2
        + [
            jax.ShapeDtypeStruct((16, width), f32),
        ],
        scratch_shapes=[
            pltpu.VMEM((chunks + 1, width, width), bf16),
            pltpu.VMEM((groups, 4, width // groups, width) if codes else (chunks * width, width), bf16),
            pltpu.VMEM((chunks, rows // 2, width), f32),
            pltpu.SemaphoreType.DMA((3,)),
        ],
        cost_estimate=pl.CostEstimate(
            flops=2 * rows * width * width * (4 * chunks + 2),
            transcendentals=2 * rows * width * chunks,
            bytes_accessed=2 * width * width * (2 * chunks + 1) + 2 * rows * width * (2 * chunks + 8),
        ),
        compiler_params=pltpu.CompilerParams(vmem_limit_bytes=60 << 20),
        name="feed",
    )(where, *ctx_own, *ctx_got, tokens, cot, valid, vec, bias_in, *weights)


def plain_grads(ctx_own, ctx_got, d_attended, hidden_low, d_inner, activated, d_branch, chain_order):
    side = lax.axis_index("seq")
    mine = lax.axis_index("fsdp") & 1
    groups = lax.axis_size("fsdp")
    chunks, _, width = d_inner.shape
    piece = width // groups
    back = mm(activated, d_branch, TN).astype(bf16).reshape(groups // 2, 2, chunks, piece, width)
    own = jnp.concatenate(ctx_own, 1)
    got = jnp.concatenate(ctx_got, 1)
    context = jnp.where(side == 0, jnp.concatenate([own, got], 1), jnp.concatenate([got, own], 1))
    units = [mm(context, d_attended, TN)] + [mm(hidden_low, d_inner[c], TN) for c in range(chunks)]
    units = [unit.astype(bf16).reshape(groups // 2, 2, piece, width) for unit in units]
    units = units + [back[:, :, q] for q in range(chunks)]
    reductions = []
    for c, (first, last) in enumerate(((0, 2), (2, 5), (5, 9))):
        stacked = jnp.stack(units[first:last])
        sent = lax.dynamic_index_in_dim(stacked, 1 - mine, 2, keepdims=False)
        kept = lax.dynamic_index_in_dim(stacked, mine, 2, keepdims=False)
        reductions.append(Reduction([kept, swap(sent, "fsdp", 1)], chain_order[c]))
    return reductions


def body(
    tokens, prior_logits, lengths, order, cotangent, w_qkv, w_out, w_in, w_back,
    bias_q, bias_v, bias_o, gain_one, shift_one, bias_in, bias_back, gain_two, shift_two,
):
    side = lax.axis_index("seq")
    me = lax.axis_index("fsdp")
    groups = lax.axis_size("fsdp")
    rows = tokens[0]
    local_count, width = rows.shape
    total = 2 * local_count
    heads_local = prior_logits.shape[1]
    local_width = heads_local * HD
    piece = bias_q.shape[0]
    chunks = w_in.shape[1] // width
    pairs = range(heads_local // 2)
    top, *middle = reversed(bits_of(groups))
    where = jnp.stack([me, side]).astype(jnp.int32)

    other_rows = swap(rows, "seq", 1)
    own_qkv, nine, small = pack(
        where, w_qkv, w_out, w_in, w_back,
        (bias_q, bias_v, bias_o, gain_one, shift_one, bias_back, gain_two, shift_two, bias_in),
    )
    ascending = bits_of(groups)
    small_chain = Gather(small.astype(bf16))
    qkv_chain = Gather(own_qkv)
    *lower, low_bit, high_bit = ascending
    small_chain.step(lower[0])
    qkv_chain.top_two(low_bit, high_bit)
    order_column = order[0][:, None]
    small_chain.held, rows, order_column, qkv_chain.held = lax.optimization_barrier(
        (small_chain.held, rows, order_column, qkv_chain.held)
    )
    for bit in lower[1:]:
        small_chain.step(bit)
    qkv_chain.step(lower[-1])
    order_row = order[0]
    length = lengths[0]
    scalars = jnp.stack([length, side]).astype(jnp.int32)
    own_order = lax.dynamic_slice_in_dim(order_row, side * local_count, local_count)
    other_order = lax.dynamic_slice_in_dim(order_row, (1 - side) * local_count, local_count)
    own_order, other_order = own_order[None], other_order[None]
    block = min(256, total)
    placed_rows = place(own_order, other_order, rows, other_rows, block)
    small_chain.held, qkv_chain.held, placed_rows = lax.optimization_barrier(
        (small_chain.held, qkv_chain.held, placed_rows)
    )
    small_chain.top_two(low_bit, high_bit)
    for bit in lower[:-1][::-1]:
        qkv_chain.step(bit)
    small_all = small_chain.held.astype(f32)
    qkv_weight = qkv_chain.held.reshape(width, 3 * local_width)
    vec = small_all[:, :8, :piece].transpose(1, 0, 2).reshape(8, width)
    inner_bias = small_all[:, 8, : chunks * piece].reshape(chunks, width)
    orders = chain_orders()
    nine = join(nine, receive(nine, top))
    chains = [nine[:, 3 * c : 3 * c + 3] for c in range(3)]
    codes = [[(0, 0), (0, top)]] * 3
    for step in range(len(orders[0])):
        codes = [more_slots(codes[c], orders[c][step]) for c in range(3)]
    for step in range(len(orders[0]) - 2):
        chains = [join(chains[c], receive(chains[c], orders[c][step])) for c in range(3)]
    third = [receive(chains[c], orders[c][-2]) for c in range(3)]

    own_cols = lambda vector: lax.dynamic_slice_in_dim(
        vector, side * local_width, local_width
    ).reshape(-1, 2 * HD)
    bias_cols = own_cols(vec[0])
    joint_bias = jnp.stack([bias_cols, jnp.zeros_like(bias_cols), own_cols(vec[1])], 1).reshape(-1)
    joint = (mm(placed_rows, qkv_weight) + joint_bias).astype(bf16)
    raw_buf, prob_buf, own, sent = attend(
        joint, prior_logits[0], scalars, order_column, block, 0, 1, []
    )
    ctx_got = [swap(sent, "seq", 1)]
    joint, own, *tied = lax.optimization_barrier((joint, own, *chains, *third))
    ctx_own = [own]
    chains = [join(tied[c], tied[3 + c]) for c in range(3)]
    joint, *chains = lax.optimization_barrier((joint, *chains))
    last = [receive(chains[c], orders[c][-1]) for c in range(3)]
    raw_buf, prob_buf, own, sent = attend(
        joint, prior_logits[0], scalars, order_column, block, 1, len(pairs) - 1, [raw_buf, prob_buf]
    )
    own, sent, *tied = lax.optimization_barrier((own, sent, *ctx_got, *chains, *last))
    chains = [join(tied[1 + c], tied[4 + c]) for c in range(3)]
    ctx_own.append(own)
    ctx_got = [tied[0], swap(sent, "seq", 1)]
    pieces = [(held, swap(held, "fsdp", 1)) for held in chains]
    if piece % 16 == 0:
        weights = [array for pair in pieces for array in pair]
    else:
        nine = jnp.concatenate([sort_pieces(*pieces[c], codes[c]) for c in range(3)], 0)
        weights = [
            nine[:5].reshape(5, width, width),
            nine[5:].transpose(1, 0, 2, 3).reshape(chunks * width, width),
        ]
        codes = None

    own_column = lax.dynamic_slice_in_dim(order_column, side * local_count, local_count)
    other_column = lax.dynamic_slice_in_dim(order_column, (1 - side) * local_count, local_count)
    valid_rows = (own_column < length).astype(f32)
    (out_rows, hidden_low, activated, d_branch, d_inner, d_attended, d_res_one,
     d_own, d_sent, sums) = feed(
        where, ctx_own, ctx_got, rows, cotangent[0], valid_rows, vec, inner_bias, weights, codes, groups
    )
    d_got = swap(d_sent, "seq", 1)

    chain_order = [orders[c][::-1] + [top] for c in range(3)]
    if codes is not None:
        back_parts = kernel_grads(
            back_grads_kernel, [chunks], where, [activated, d_branch], groups, "back_grads"
        )
        back_terms = [back_parts[1], swap(back_parts[0], "fsdp", 1)]
        d_inner, back_kept = lax.optimization_barrier((d_inner, back_parts[1]))
        parts = kernel_grads(
            grads_kernel, [2, chunks - 1], where,
            [*ctx_own, *ctx_got, d_attended, hidden_low, d_inner], groups, "grads",
        )
        d_got, *rest = lax.optimization_barrier((d_got, *parts[2:]))
        parts = list(parts[:2]) + rest
        back_terms[0] = back_kept
        reductions = [
            Reduction([parts[1], swap(parts[0], "fsdp", 1)], chain_order[0]),
            Reduction([parts[3], swap(parts[2], "fsdp", 1)], chain_order[1]),
            Reduction(back_terms, chain_order[2]),
        ]
    else:
        reductions = plain_grads(
            ctx_own, ctx_got, d_attended, hidden_low, d_inner, activated, d_branch, chain_order
        )

    def fence(*values):
        terms = tuple(term for reduction in reductions for term in reduction.terms)
        tied = lax.optimization_barrier(values + terms)
        for c, reduction in enumerate(reductions):
            reduction.terms = list(tied[len(values) + 2 * c : len(values) + 2 * c + 2])
        return tied[: len(values)]

    def advance(*values):
        sents = [reduction.sent() for reduction in reductions]
        tied = lax.optimization_barrier((*values, *sents))
        for reduction, sent in zip(reductions, tied[len(values) :]):
            reduction.launch(sent)
        return tied[: len(values)]

    d_context_pos = place(own_order, other_order, d_own, d_got, block)
    (d_context_pos,) = fence(d_context_pos)
    (d_context_pos,) = advance(d_context_pos)
    held = []
    held = attend_back(joint, d_context_pos, prob_buf, block, 0, len(pairs) - 1, held)
    held = advance(*fence(*held))
    held = attend_back(joint, d_context_pos, prob_buf, block, len(pairs) - 1, 1, held)
    dprior_buf, d_joint, bias_sums = fence(*held)
    grad_w_qkv = mm(placed_rows, d_joint, TN).astype(bf16).reshape(1, groups, piece, -1)
    qkv = Reduction([grad_w_qkv], bits_of(groups))
    bias_row = jnp.concatenate([bias_sums[0:1], bias_sums[1:2]], 1)
    own_row = lax.broadcasted_iota(jnp.int32, (2, width), 0) == side
    sums = jnp.concatenate([sums[:14], jnp.where(own_row, bias_row, 0.0)], 0)
    sent, sums, d_joint = advance(qkv.sent(), sums, d_joint)
    sums_got = [swap(sums, "fsdp", qkv.order[0])]
    qkv.launch(sent)
    d_rows_sent, d_rows_own = rows_back(d_joint, qkv_weight, own_column, other_column, block)
    while len(reductions[0].order) > 1:
        (d_rows_sent,) = fence(d_rows_sent)
        (d_rows_sent,) = advance(d_rows_sent)

    d_rows_sent, sums, *rest = fence(d_rows_sent, sums, *sums_got, *qkv.terms)
    sums = sums + sum(rest[:-2])
    qkv.terms = rest[-2:]
    nine = Reduction(
        [jnp.concatenate([reduction.terms[k] for reduction in reductions], 0) for k in range(2)],
        [top],
    )
    d_rows_sent, sums, nine_sent, sent = lax.optimization_barrier(
        (d_rows_sent, sums, nine.sent(), qkv.sent())
    )
    nine.launch(nine_sent)
    d_rows_got = swap(d_rows_sent, "seq", 1)
    sums_got = [swap(sums, "fsdp", qkv.order[0])]
    qkv.launch(sent)
    while len(qkv.order) > 2:
        sums, *rest = lax.optimization_barrier((sums, *sums_got, *qkv.terms))
        sums = sums + sum(rest[:-2])
        qkv.terms = rest[-2:]
        sums_got = [swap(sums, "fsdp", qkv.order[0])]
        qkv.launch(qkv.sent())
    low_bit, high_bit = qkv.order
    sums = sums + sums_got[0]
    sums_got = [swap(sums, "fsdp", low_bit)]

    d_rows_got, sums, sums_got[0], *rest = lax.optimization_barrier(
        (d_rows_got, sums, sums_got[0], *nine.terms, *qkv.terms)
    )
    sums = sums + sums_got[0]
    own_nine = (rest[0].astype(f32) + rest[1].astype(f32)).astype(bf16)[:, 0]
    four = (rest[2].astype(f32) + rest[3].astype(f32)).astype(bf16)[0]
    mine = ((me & low_bit) != 0) * 1 + ((me & high_bit) != 0) * 2
    peers = (low_bit, high_bit, low_bit | high_bit)
    blocks = [
        lax.dynamic_index_in_dim(four, mine ^ k, 0, keepdims=False) for k in range(4)
    ]
    own_nine, sums, *blocks = lax.optimization_barrier((own_nine, sums, *blocks))
    other_nine = swap(own_nine, "seq", 1)
    blocks[1:] = [swap(blocks[1 + k], "fsdp", peers[k]) for k in range(3)]
    sums_got = [swap(sums, "fsdp", high_bit)]
    tokens_grad = (d_res_one + d_rows_own + d_rows_got.astype(f32)).astype(bf16)

    other_nine, own_nine, sums, *rest = lax.optimization_barrier(
        (other_nine, own_nine, sums, *blocks, *sums_got)
    )
    own_qkv = sum(block.astype(f32) for block in rest[:4]).astype(bf16)
    sums = sums + sum(rest[4:])
    other_qkv = swap(own_qkv, "seq", 1)
    sums = sums + swap(sums, "seq", 1)

    def by_side(own, other, axis):
        return jnp.where(
            side == 0, jnp.concatenate([own, other], axis), jnp.concatenate([other, own], axis)
        ).astype(f32)

    out_nine = by_side(own_nine, other_nine, 2)
    shape = (piece, len(pairs), 3, 1, 2 * HD)
    out_qkv = by_side(own_qkv.reshape(shape), other_qkv.reshape(shape), 3)
    out_qkv = out_qkv.transpose(0, 2, 3, 1, 4).reshape(piece, 3 * width)
    rms = jnp.sqrt(sums[10:13, 0] / (sums[13, 0] * width))
    own_sums = lax.dynamic_slice_in_dim(sums, me * piece, piece, 1)
    bias_grads = jnp.concatenate(
        [sums[14:15].reshape(2, local_width), sums[15:16].reshape(2, local_width)], 1
    )
    bias_grads = lax.dynamic_slice_in_dim(bias_grads, me * piece, piece, 1)
    own_inner = lax.dynamic_slice_in_dim(
        sums[6 : 6 + chunks].reshape(-1), me * chunks * piece, chunks * piece
    )
    return (
        out_rows[None],
        raw_buf[None],
        tokens_grad[None],
        dprior_buf[None],
        out_qkv,
        out_nine[0],
        jnp.concatenate([out_nine[1 + c] for c in range(chunks)], 1),
        out_nine[5:9].reshape(chunks * piece, width),
        bias_grads[0],
        bias_grads[1],
        own_sums[0],
        own_sums[1],
        own_sums[2],
        own_inner,
        own_sums[3],
        own_sums[4],
        own_sums[5],
        rms,
    )


def solution(mesh):
    shard = P("fsdp", "seq", None)
    heads = P("fsdp", "seq", None, None)
    mat = P("fsdp", None)
    vec = P("fsdp")
    return jax.shard_map(
        body,
        mesh=mesh,
        in_specs=(shard, heads, vec, mat, shard) + (mat,) * 4 + (vec,) * 9,
        out_specs=(shard, heads, shard, heads) + (mat,) * 4 + (vec,) * 9 + (P(),),
        check_vma=False,
    )
```

```python
import functools
import math

import jax
import jax.numpy as jnp
from jax import lax
from jax.experimental import pallas as pl
from jax.experimental.pallas import tpu as pltpu
from jax.sharding import PartitionSpec as P

HD = 64
eps_norm = 1e-05
masked_fill = -1e30
f32 = jnp.float32
bf16 = jnp.bfloat16

NT = (((1,), (1,)), ((), ()))
TN = (((0,), (0,)), ((), ()))


def mm(left, right, dims=(((1,), (0,)), ((), ()))):
    return lax.dot_general(left, right, dims, preferred_element_type=f32)


def bits_of(count):
    return [1 << k for k in range(count.bit_length() - 1)]


def swap(value, axis, bit):
    count = lax.axis_size(axis)
    return lax.ppermute(value, axis, [(i, i ^ bit) for i in range(count)])


class Gather:
    def __init__(self, shard):
        self.shape = shard.shape
        self.held = shard[None]
        self.done = []

    def step(self, bit):
        other = swap(self.held, "fsdp", bit)
        high = (lax.axis_index("fsdp") & bit) != 0
        outer = 1 << sum(1 for b in self.done if b > bit)
        self.done.append(bit)
        split = (outer, self.held.shape[0] // outer) + self.shape
        first = jnp.where(high, other, self.held).reshape(split)
        second = jnp.where(high, self.held, other).reshape(split)
        self.held = jnp.stack([first, second], axis=1).reshape((-1,) + self.shape)

    def top_two(self, low, high):
        me = lax.axis_index("fsdp")
        mine = ((me & low) != 0) * 1 + ((me & high) != 0) * 2
        got = [swap(self.held, "fsdp", peer) for peer in (low, high, low | high)]
        four = jnp.stack([self.held] + got)
        self.done += [low, high]
        self.held = jnp.concatenate(
            [lax.dynamic_index_in_dim(four, z ^ mine, 0, keepdims=False) for z in range(4)], 0
        )


def tie(value, *others):
    return lax.optimization_barrier((value,) + others)[0]


def chain_orders():
    rest = list(reversed(bits_of(lax.axis_size("fsdp"))))[1:-1]
    up = rest[::-1]
    return [up + ["seq"], rest[:-1] + ["seq"] + rest[-1:], ["seq"] + up]


def receive(held, stage):
    return swap(held, "seq", 1) if stage == "seq" else swap(held, "fsdp", stage)


def more_slots(slots, stage):
    if stage == "seq":
        return slots + [(a ^ 1, code) for a, code in slots]
    return slots + [(a, code ^ stage) for a, code in slots]


def join(held, got):
    return jnp.concatenate([held, got], axis=0)


def sort_pieces(own, other, slots):
    me = lax.axis_index("fsdp")
    side = lax.axis_index("seq")
    count = len(slots)
    both = jnp.concatenate([own, other], axis=0)
    place = [[0] * count, [0] * count]
    for s, (a, code) in enumerate(slots):
        place[a][code] = s
        place[a][code ^ 1] = s + count
    halves = [
        jnp.take(both, jnp.take(jnp.array(place[a], jnp.int32), jnp.arange(count) ^ me), axis=0)
        for a in range(2)
    ]
    joined = jnp.where(
        side == 0, jnp.concatenate(halves, -1), jnp.concatenate(halves[::-1], -1)
    )
    return joined.transpose(1, 0, 2, 3)


class Reduction:
    def __init__(self, terms, order):
        self.terms = terms
        self.order = order
        self.me = lax.axis_index("fsdp")
        self.side = lax.axis_index("seq")

    def pick(self, own):
        stage = self.order[0]
        picked = []
        for array in self.terms:
            if stage == "seq":
                size = array.shape[3] // 2
                index = self.side if own else 1 - self.side
                picked.append(lax.dynamic_slice_in_dim(array, index * size, size, 3))
            else:
                low = sum(1 for b in self.order if b != "seq" and b < stage)
                shape = array.shape
                array = array.reshape(
                    (shape[0], shape[1] >> (low + 1), 2, 1 << low) + shape[2:]
                )
                mine = ((self.me & stage) != 0).astype(jnp.int32)
                array = lax.dynamic_index_in_dim(
                    array, mine if own else 1 - mine, 2, keepdims=False
                )
                picked.append(array.reshape((shape[0], shape[1] // 2) + shape[2:]))
        total = picked[0].astype(f32)
        for other in picked[1:]:
            total = total + other.astype(f32)
        return total.astype(bf16)

    def sent(self):
        return self.pick(False)

    def launch(self, sent, apart=True):
        if apart:
            *self.terms, _ = lax.optimization_barrier((*self.terms, sent))
        kept = self.pick(True)
        stage = self.order[0]
        self.order = self.order[1:]
        axis, bit = ("seq", 1) if stage == "seq" else ("fsdp", stage)
        self.terms = [kept, swap(sent, axis, bit)]


def pack_kernel(where_ref, *refs):
    w_qkv, w_out, w_in, w_back = refs[:4]
    vectors, (qkv_ref, nine_ref, small_ref) = refs[4:13], refs[13:]
    r, width = w_out.shape
    half = width // 2
    columns = pl.ds(pl.multiple_of(where_ref[1] * half, 128), half)
    nine_ref[0, 0] = w_out[:, columns]
    for c in range(4):
        nine_ref[0, 1 + c] = w_in[:, pl.ds(pl.multiple_of(c * width + where_ref[1] * half, 128), half)]
        nine_ref[0, 5 + c] = w_back[c * r : (c + 1) * r, columns]
    for kind in range(3):
        for t in range(3):
            start = kind * width + where_ref[1] * half + t * 128
            qkv_ref[:, (3 * t + kind) * 128 : (3 * t + kind + 1) * 128] = w_qkv[
                :, pl.ds(pl.multiple_of(start, 128), 128)
            ]
    small_ref[...] = jnp.zeros_like(small_ref)
    for k, vector in enumerate(vectors):
        small_ref[k : k + 1, : vector.shape[1]] = vector[...].astype(f32)


def pack(where, w_qkv, w_out, w_in, w_back, vectors):
    r, width = w_out.shape
    vmem = pl.BlockSpec(memory_space=pltpu.VMEM)
    return pl.pallas_call(
        pack_kernel,
        in_specs=[pl.BlockSpec(memory_space=pltpu.SMEM)] + [vmem] * 13,
        out_specs=[vmem] * 3,
        out_shape=[
            jax.ShapeDtypeStruct((r, 3 * width // 2), bf16),
            jax.ShapeDtypeStruct((1, 9, r, width // 2), bf16),
            jax.ShapeDtypeStruct((16, 256), f32),
        ],
        name="pack",
    )(where, w_qkv, w_out, w_in, w_back, *[vector[None] for vector in vectors])


def attend_kernel(length_ref, q_ref, k_ref, v_ref, own_ref, other_ref, prior_ref, *refs):
    raw_ref, prob_ref, ctx_own_ref, ctx_sent_ref, ctx = refs[-5:]
    step = pl.program_id(1)
    block = q_ref.shape[0]
    keys = k_ref.shape[0]
    lane = lax.broadcasted_iota(jnp.int32, (1, 2 * HD), 1)
    seen = lax.broadcasted_iota(jnp.int32, (1, keys), 1) < length_ref[0]
    q = q_ref[...] * jnp.asarray(1.0 / math.sqrt(HD), bf16)
    k = k_ref[...]
    v = v_ref[...]
    parts = []
    for h in range(2):
        mine = (lane >= HD) if h else (lane < HD)
        scores = mm(jnp.where(mine, q, jnp.zeros_like(q)), k, NT) + prior_ref[h].astype(f32)
        raw_ref[h] = scores.astype(bf16)
        masked = jnp.where(seen, scores, masked_fill)
        largest = jnp.max(masked, axis=-1, keepdims=True)
        exponent = jnp.exp(masked - largest)
        inverse = 1.0 / jnp.sum(exponent, axis=-1, keepdims=True)
        prob = (exponent * inverse).astype(bf16)
        prob_ref[h] = prob
        parts.append(mm(prob, v))
    ctx[pl.ds(pl.multiple_of(step * block, block), block), :] = jnp.where(
        lane < HD, parts[0], parts[1]
    ).astype(bf16)

    @pl.when(step == pl.num_programs(1) - 1)
    def _():
        position = lax.broadcasted_iota(jnp.int32, (own_ref.shape[0], keys), 1)
        placed = ctx[...]
        for order_ref, out_ref in ((other_ref, ctx_sent_ref), (own_ref, ctx_own_ref)):
            pick = jnp.where(position == order_ref[...], 1.0, 0.0).astype(bf16)
            out_ref[...] = mm(pick, placed).astype(bf16)


def attend(joint, prior, scalars, order_column, block, first, pairs, held):
    heads, total, _ = prior.shape
    wide = 2 * HD
    square = pl.BlockSpec((2, block, total), lambda t, i, *_: (first + t, i, 0))
    hbm = pl.BlockSpec(memory_space=pl.ANY)
    local = order_column.shape[0] // 2
    stored = pl.BlockSpec((local, wide), lambda t, i, *_: (0, t))
    return pl.pallas_call(
        attend_kernel,
        grid_spec=pltpu.PrefetchScalarGridSpec(
            num_scalar_prefetch=1,
            grid=(pairs, total // block),
            in_specs=[
                pl.BlockSpec((block, wide), lambda t, i, *_: (i, 3 * (first + t))),
                pl.BlockSpec((total, wide), lambda t, i, *_: (0, 3 * (first + t) + 1)),
                pl.BlockSpec((total, wide), lambda t, i, *_: (0, 3 * (first + t) + 2)),
                pl.BlockSpec((local, 1), lambda t, i, scalars: (scalars[1], 0)),
                pl.BlockSpec((local, 1), lambda t, i, scalars: (1 - scalars[1], 0)),
                square,
            ]
            + [hbm] * len(held),
            out_specs=[square, square, stored, stored],
            scratch_shapes=[pltpu.VMEM((total, wide), bf16)],
        ),
        out_shape=[
            jax.ShapeDtypeStruct(prior.shape, bf16),
            jax.ShapeDtypeStruct(prior.shape, bf16),
            jax.ShapeDtypeStruct((local, pairs * wide), bf16),
            jax.ShapeDtypeStruct((local, pairs * wide), bf16),
        ],
        input_output_aliases={7 + k: k for k in range(len(held))},
        cost_estimate=pl.CostEstimate(flops=1000, transcendentals=0, bytes_accessed=1000),
        compiler_params=pltpu.CompilerParams(vmem_limit_bytes=56 << 20),
        name="attend",
    )(scalars, joint, joint, joint, order_column, order_column, prior, *held)


def attend_back_kernel(q_ref, k_ref, v_ref, dc_ref, prob_ref, *refs):
    dprior_ref, dj_ref, bias_ref, dk_acc, dv_acc = refs[-5:]
    step = pl.program_id(1)
    block = q_ref.shape[0]
    wide_lanes = 2 * HD
    lane = lax.broadcasted_iota(jnp.int32, (1, wide_lanes), 1)
    scale = 1.0 / math.sqrt(HD)
    q = q_ref[...]
    k = k_ref[...]
    v = v_ref[...]
    dc = dc_ref[...]

    @pl.when(step == 0)
    def _():
        dk_acc[...] = jnp.zeros_like(dk_acc)
        dv_acc[...] = jnp.zeros_like(dv_acc)
        bias_ref[...] = jnp.zeros_like(bias_ref)

    dq, dk, dv = [], [], []
    for h in range(2):
        mine = (lane >= HD) if h else (lane < HD)
        prob = prob_ref[h]
        wide = prob.astype(f32)
        d_prob = mm(jnp.where(mine, dc, jnp.zeros_like(dc)), v, NT)
        row_term = jnp.sum(wide * d_prob, axis=-1, keepdims=True)
        d_scores = (wide * (d_prob - row_term)).astype(bf16)
        dprior_ref[h] = d_scores
        dq.append(mm(d_scores, k))
        dk.append(mm(d_scores, q, TN))
        dv.append(mm(prob, dc, TN))
    first = lane < HD
    d_query = (jnp.where(first, dq[0], dq[1]) * scale).astype(bf16)
    dj_ref[pl.ds(pl.multiple_of(step * block, block), block), 0:wide_lanes] = d_query
    bias_ref[0:1, :] += jnp.sum(d_query.astype(f32), axis=0, keepdims=True)
    dk_acc[...] += jnp.where(first, dk[0], dk[1])
    dv_acc[...] += jnp.where(first, dv[0], dv[1])

    @pl.when(step == pl.num_programs(1) - 1)
    def _():
        dj_ref[:, wide_lanes : 2 * wide_lanes] = (dk_acc[...] * scale).astype(bf16)
        d_value = dv_acc[...].astype(bf16)
        dj_ref[:, 2 * wide_lanes : 3 * wide_lanes] = d_value
        bias_ref[1:2, :] = jnp.sum(d_value.astype(f32), axis=0, keepdims=True)


def attend_back(joint, d_context, prob, block, first, pairs, held):
    heads, total, _ = prob.shape
    wide = 2 * HD
    square = pl.BlockSpec((2, block, total), lambda t, i: (first + t, i, 0))
    return pl.pallas_call(
        attend_back_kernel,
        grid=(pairs, total // block),
        in_specs=[
            pl.BlockSpec((block, wide), lambda t, i: (i, 3 * (first + t))),
            pl.BlockSpec((total, wide), lambda t, i: (0, 3 * (first + t) + 1)),
            pl.BlockSpec((total, wide), lambda t, i: (0, 3 * (first + t) + 2)),
            pl.BlockSpec((block, wide), lambda t, i: (i, first + t)),
            square,
        ]
        + [pl.BlockSpec(memory_space=pl.ANY)] * len(held),
        out_specs=[
            square,
            pl.BlockSpec((total, 3 * wide), lambda t, i: (0, first + t)),
            pl.BlockSpec((8, wide), lambda t, i: (0, first + t)),
        ],
        out_shape=[
            jax.ShapeDtypeStruct(prob.shape, bf16),
            jax.ShapeDtypeStruct((total, 3 * heads * HD), bf16),
            jax.ShapeDtypeStruct((8, heads * HD), f32),
        ],
        input_output_aliases={5 + k: k for k in range(len(held))},
        scratch_shapes=[pltpu.VMEM((total, wide), f32)] * 2,
        cost_estimate=pl.CostEstimate(flops=1000, transcendentals=0, bytes_accessed=1000),
        compiler_params=pltpu.CompilerParams(vmem_limit_bytes=56 << 20),
        name="attend_back",
    )(joint, joint, joint, d_context, prob, *held)


def put_blocks(sent_ref, kept_ref, odd, unit, first, blocks):
    blocks = blocks.astype(bf16)
    lower, upper = blocks[:, 0], blocks[:, 1]
    at = pl.ds(first, blocks.shape[0])
    sent_ref[unit, at] = jnp.where(odd, lower, upper)
    kept_ref[unit, at] = jnp.where(odd, upper, lower)


def back_grads_kernel(where_ref, act_ref, d_branch_ref, sent_ref, kept_ref):
    odd = (where_ref[0] & 1) == 1
    chunks, half_groups, r, width = sent_ref.shape
    each = half_groups // chunks
    d_branch = d_branch_ref[...]

    def chunk(c, carry):
        part = mm(act_ref[:, pl.ds(pl.multiple_of(c * width, 128), width)], d_branch, TN)
        part = part.reshape(each, 2, chunks, r, width)
        for q in range(chunks):
            put_blocks(sent_ref, kept_ref, odd, q, c * each, part[:, :, q])
        return carry

    lax.fori_loop(0, chunks, chunk, 0)


def grads_kernel(where_ref, *refs):
    ctx_own_refs, ctx_got_refs, refs = refs[:2], refs[2:4], refs[4:]
    d_att_ref, low_ref, d_inner_ref, first_sent, first_kept, rest_sent, rest_kept = refs
    odd = (where_ref[0] & 1) == 1
    side = where_ref[1]
    r, width = first_sent.shape[2:]
    groups = 2 * first_sent.shape[1]
    low = low_ref[...]

    def inner(c):
        return mm(low, d_inner_ref[c], TN).reshape(groups // 2, 2, r, width)

    def chunk(c, carry):
        put_blocks(rest_sent, rest_kept, odd, c, 0, inner(1 + c))
        return carry

    put_blocks(first_sent, first_kept, odd, 1, 0, inner(0))
    lax.fori_loop(0, rest_sent.shape[0], chunk, 0)
    d_att = d_att_ref[...]
    for part_refs, start in ((ctx_own_refs, side), (ctx_got_refs, 1 - side)):
        part = mm(jnp.concatenate([ref[...] for ref in part_refs], 1), d_att, TN)
        part = part.reshape(groups // 4, 2, r, width)
        put_blocks(first_sent, first_kept, odd, 0, start * (groups // 4), part)


def kernel_grads(kernel, units, where, arrays, groups, name):
    rows, width = arrays[-1].shape[-2:]
    vmem = pl.BlockSpec(memory_space=pltpu.VMEM)
    parts = [
        jax.ShapeDtypeStruct((count, groups // 2, width // groups, width), bf16)
        for count in units
        for _ in range(2)
    ]
    return pl.pallas_call(
        kernel,
        in_specs=[pl.BlockSpec(memory_space=pltpu.SMEM)] + [vmem] * len(arrays),
        out_specs=[vmem] * len(parts),
        out_shape=parts,
        cost_estimate=pl.CostEstimate(flops=1000, transcendentals=0, bytes_accessed=1000),
        compiler_params=pltpu.CompilerParams(vmem_limit_bytes=60 << 20),
        name=name,
    )(where, *arrays)


def feed_kernel(
    where_ref, *refs, codes, chunks,
):
    ctx_own_refs, ctx_got_refs, refs = refs[:2], refs[2:4], refs[4:]
    (tokens_ref, cot_ref, valid_ref, vec_ref, bias_in_ref), refs = refs[:5], refs[5:]
    weight_count = 2 if codes is None else 6
    weights, refs = refs[:weight_count], refs[weight_count:]
    (out_ref, low_ref, act_ref, d_branch_ref, d_inner_ref, d_att_ref, d_res_ref,
     d_own_ref, d_sent_ref, sums_ref, w_five, w_back, slope, sems) = refs
    me = where_ref[0]
    side = where_ref[1]
    width = tokens_ref.shape[1]
    half = width // 2

    def copies(chain):
        if codes is None:
            if chain == 2:
                return []
            target = (w_five, w_back)[chain]
            return [pltpu.make_async_copy(weights[chain], target, sems.at[chain])]
        made = []
        r = weights[0].shape[2]
        for b in range(2):
            source = weights[2 * chain + b]
            for s, (a, code) in enumerate(codes[chain]):
                column = pl.ds(pl.multiple_of((side ^ a) * half, 128), half)
                block = me ^ (code ^ b)
                rows = pl.ds(pl.multiple_of(block * r, 16), r)
                moves = (
                    ((0, 3, w_five.at[0:3, rows, column]),),
                    ((0, 2, w_five.at[3:5, rows, column]), (2, 1, w_back.at[block, 0:1, :, column])),
                    ((0, 3, w_back.at[block, 1:4, :, column]),),
                )[chain]
                for first, count, target in moves:
                    made.append(pltpu.make_async_copy(
                        source.at[s, pl.ds(first, count)], target, sems.at[chain]))
        return made

    groups = [copies(chain) for chain in range(3)]
    for group in groups:
        for copy in group:
            copy.start()

    def back_rows(c):
        if codes is None:
            return w_back[c * width : (c + 1) * width, :]
        per = w_back.shape[0] // chunks
        return w_back[c * per : (c + 1) * per].reshape(width, width)

    vec = vec_ref[...]
    proj_bias, first_gain, first_shift, outer_bias, second_gain, second_shift = (
        vec[k : k + 1] for k in range(2, 8)
    )
    own_rows = pl.ds(pl.multiple_of(side * half, 128), half)
    other_rows = pl.ds(pl.multiple_of((1 - side) * half, 128), half)
    valid = valid_ref[...]
    for copy in groups[0]:
        copy.wait()
    ctx_own = jnp.concatenate([ref[...] for ref in ctx_own_refs], 1)
    ctx_got = jnp.concatenate([ref[...] for ref in ctx_got_refs], 1)
    attended = (
        mm(ctx_own, w_five[0, own_rows, :]) + mm(ctx_got, w_five[0, other_rows, :]) + proj_bias
    )
    tokens_f = tokens_ref[...].astype(f32)

    def stat(row, values):
        total = jnp.sum(jnp.sum(values, axis=0, keepdims=True), axis=1, keepdims=True)
        sums_ref[row : row + 1, :] = jnp.broadcast_to(total, (1, width))

    def column_sum(row, values):
        sums_ref[row : row + 1, :] = jnp.sum(values, axis=0, keepdims=True)

    def normalize(values):
        centered = values - jnp.mean(values, axis=-1, keepdims=True)
        spread = lax.rsqrt(jnp.mean(centered * centered, axis=-1, keepdims=True) + eps_norm)
        return centered * spread, spread

    def normalize_back(grad, gain, normal, spread):
        e = grad * gain
        return spread * (
            e - jnp.mean(e, axis=-1, keepdims=True)
            - normal * jnp.mean(e * normal, axis=-1, keepdims=True)
        )

    stat(10, valid * tokens_f * tokens_f)
    stat(11, valid * attended * attended)
    stat(13, valid * jnp.ones((1, 128), f32) * (1.0 / 128.0))
    normal_one, spread_one = normalize(tokens_f + attended)
    hidden = normal_one * first_gain + first_shift
    hidden_low = hidden.astype(bf16)
    low_ref[...] = hidden_low
    for copy in groups[1] + groups[2]:
        copy.wait()
    branch = jnp.zeros_like(hidden)
    for c in range(chunks):
        inner = mm(hidden_low, w_five[1 + c]) + bias_in_ref[c : c + 1, :]
        below = 0.5 + 0.5 * lax.erf(inner * math.sqrt(0.5))
        slope[c] = below + inner * (jnp.exp(inner * inner * -0.5) * (1.0 / math.sqrt(2.0 * math.pi)))
        activated = (inner * below).astype(bf16)
        columns = slice(c * width, (c + 1) * width)
        act_ref[:, columns] = activated
        branch = branch + mm(activated, back_rows(c))
    branch = branch + outer_bias
    stat(12, valid * branch * branch)
    normal_two, spread_two = normalize(hidden + branch)
    out_ref[...] = (normal_two * second_gain + second_shift).astype(bf16)
    d_output = cot_ref[...].astype(f32) * valid
    column_sum(4, d_output * normal_two)
    column_sum(5, d_output)
    d_hidden = normalize_back(d_output, second_gain, normal_two, spread_two)
    d_branch = d_hidden.astype(bf16)
    d_branch_ref[...] = d_branch
    column_sum(3, d_branch.astype(f32))
    for c in range(chunks):
        columns = slice(c * width, (c + 1) * width)
        d_inner = (mm(d_branch, back_rows(c), NT) * slope[c]).astype(bf16)
        d_inner_ref[c] = d_inner
        column_sum(6 + c, d_inner.astype(f32))
        d_hidden = d_hidden + mm(d_inner, w_five[1 + c], NT)
    column_sum(1, d_hidden * normal_one)
    column_sum(2, d_hidden)
    d_res = normalize_back(d_hidden, first_gain, normal_one, spread_one)
    d_res_ref[...] = d_res
    d_att = d_res.astype(bf16)
    d_att_ref[...] = d_att
    column_sum(0, d_att.astype(f32))
    d_sent_ref[...] = mm(d_att, w_five[0, other_rows, :], NT).astype(bf16)
    d_own_ref[...] = mm(d_att, w_five[0, own_rows, :], NT).astype(bf16)


def feed(where, ctx_own, ctx_got, tokens, cot, valid, vec, bias_in, weights, codes, groups):
    rows, width = tokens.shape
    chunks = bias_in.shape[0]
    vmem = pl.BlockSpec(memory_space=pltpu.VMEM)
    hbm = pl.BlockSpec(memory_space=pl.ANY)
    flat = lambda *shape: jax.ShapeDtypeStruct(shape, bf16)
    return pl.pallas_call(
        functools.partial(feed_kernel, codes=codes, chunks=chunks),
        in_specs=[pl.BlockSpec(memory_space=pltpu.SMEM)] + [vmem] * 9 + [hbm] * len(weights),
        out_specs=[vmem] * 10,
        out_shape=[
            flat(rows, width),
            flat(rows, width),
            flat(rows, chunks * width),
            flat(rows, width),
            flat(chunks, rows, width),
            flat(rows, width),
            jax.ShapeDtypeStruct((rows, width), f32),
        ]
        + [flat(rows, width // 2)] * 2
        + [
            jax.ShapeDtypeStruct((16, width), f32),
        ],
        scratch_shapes=[
            pltpu.VMEM((chunks + 1, width, width), bf16),
            pltpu.VMEM((groups, 4, width // groups, width) if codes else (chunks * width, width), bf16),
            pltpu.VMEM((chunks, rows, width), f32),
            pltpu.SemaphoreType.DMA((3,)),
        ],
        cost_estimate=pl.CostEstimate(
            flops=2 * rows * width * width * (4 * chunks + 2),
            transcendentals=2 * rows * width * chunks,
            bytes_accessed=2 * width * width * (2 * chunks + 1) + 2 * rows * width * (2 * chunks + 8),
        ),
        compiler_params=pltpu.CompilerParams(vmem_limit_bytes=60 << 20),
        name="feed",
    )(where, *ctx_own, *ctx_got, tokens, cot, valid, vec, bias_in, *weights)


def plain_grads(ctx_own, ctx_got, d_attended, hidden_low, d_inner, activated, d_branch, chain_order):
    side = lax.axis_index("seq")
    mine = lax.axis_index("fsdp") & 1
    groups = lax.axis_size("fsdp")
    chunks, _, width = d_inner.shape
    piece = width // groups
    back = mm(activated, d_branch, TN).astype(bf16).reshape(groups // 2, 2, chunks, piece, width)
    own = jnp.concatenate(ctx_own, 1)
    got = jnp.concatenate(ctx_got, 1)
    context = jnp.where(side == 0, jnp.concatenate([own, got], 1), jnp.concatenate([got, own], 1))
    units = [mm(context, d_attended, TN)] + [mm(hidden_low, d_inner[c], TN) for c in range(chunks)]
    units = [unit.astype(bf16).reshape(groups // 2, 2, piece, width) for unit in units]
    units = units + [back[:, :, q] for q in range(chunks)]
    reductions = []
    for c, (first, last) in enumerate(((0, 2), (2, 5), (5, 9))):
        stacked = jnp.stack(units[first:last])
        sent = lax.dynamic_index_in_dim(stacked, 1 - mine, 2, keepdims=False)
        kept = lax.dynamic_index_in_dim(stacked, mine, 2, keepdims=False)
        reductions.append(Reduction([kept, swap(sent, "fsdp", 1)], chain_order[c]))
    return reductions


def body(
    tokens, prior_logits, lengths, order, cotangent, w_qkv, w_out, w_in, w_back,
    bias_q, bias_v, bias_o, gain_one, shift_one, bias_in, bias_back, gain_two, shift_two,
):
    side = lax.axis_index("seq")
    me = lax.axis_index("fsdp")
    groups = lax.axis_size("fsdp")
    rows = tokens[0]
    local_count, width = rows.shape
    total = 2 * local_count
    heads_local = prior_logits.shape[1]
    local_width = heads_local * HD
    piece = bias_q.shape[0]
    chunks = w_in.shape[1] // width
    pairs = range(heads_local // 2)
    top, *middle = reversed(bits_of(groups))
    where = jnp.stack([me, side]).astype(jnp.int32)

    other_rows = swap(rows, "seq", 1)
    own_qkv, nine, small = pack(
        where, w_qkv, w_out, w_in, w_back,
        (bias_q, bias_v, bias_o, gain_one, shift_one, bias_back, gain_two, shift_two, bias_in),
    )
    ascending = bits_of(groups)
    small_chain = Gather(small.astype(bf16))
    qkv_chain = Gather(own_qkv)
    *lower, low_bit, high_bit = ascending
    small_chain.step(lower[0])
    qkv_chain.top_two(low_bit, high_bit)
    order_column = order[0][:, None]
    small_chain.held, rows, order_column, qkv_chain.held = lax.optimization_barrier(
        (small_chain.held, rows, order_column, qkv_chain.held)
    )
    for bit in lower[1:]:
        small_chain.step(bit)
    qkv_chain.step(lower[-1])
    order_row = order[0]
    length = lengths[0]
    scalars = jnp.stack([length, side]).astype(jnp.int32)
    own_order = lax.dynamic_slice_in_dim(order_row, side * local_count, local_count)
    other_order = lax.dynamic_slice_in_dim(order_row, (1 - side) * local_count, local_count)
    own_order, other_order = own_order[None], other_order[None]
    block = min(256, total)
    positions = jnp.arange(total, dtype=jnp.int32)
    own_pick = (positions[:, None] == own_order).astype(bf16)
    other_pick = (positions[:, None] == other_order).astype(bf16)

    def to_positions(own, other):
        return (mm(own_pick, own) + mm(other_pick, other)).astype(bf16)

    placed_rows = to_positions(rows, other_rows)
    small_chain.held, qkv_chain.held, placed_rows = lax.optimization_barrier(
        (small_chain.held, qkv_chain.held, placed_rows)
    )
    small_chain.top_two(low_bit, high_bit)
    for bit in lower[:-1][::-1]:
        qkv_chain.step(bit)
    small_all = small_chain.held.astype(f32)
    qkv_weight = qkv_chain.held.reshape(width, 3 * local_width)
    vec = small_all[:, :8, :piece].transpose(1, 0, 2).reshape(8, width)
    inner_bias = small_all[:, 8, : chunks * piece].reshape(chunks, width)
    orders = chain_orders()
    nine = join(nine, receive(nine, top))
    chains = [nine[:, 3 * c : 3 * c + 3] for c in range(3)]
    codes = [[(0, 0), (0, top)]] * 3
    for step in range(len(orders[0])):
        codes = [more_slots(codes[c], orders[c][step]) for c in range(3)]
    for step in range(len(orders[0]) - 2):
        chains = [join(chains[c], receive(chains[c], orders[c][step])) for c in range(3)]
    third = [receive(chains[c], orders[c][-2]) for c in range(3)]

    own_cols = lambda vector: lax.dynamic_slice_in_dim(
        vector, side * local_width, local_width
    ).reshape(-1, 2 * HD)
    bias_cols = own_cols(vec[0])
    joint_bias = jnp.stack([bias_cols, jnp.zeros_like(bias_cols), own_cols(vec[1])], 1).reshape(-1)
    joint = (mm(placed_rows, qkv_weight) + joint_bias).astype(bf16)
    raw_buf, prob_buf, own, sent = attend(
        joint, prior_logits[0], scalars, order_column, block, 0, 1, []
    )
    ctx_got = [swap(sent, "seq", 1)]
    joint, own, *tied = lax.optimization_barrier((joint, own, *chains, *third))
    ctx_own = [own]
    chains = [join(tied[c], tied[3 + c]) for c in range(3)]
    joint, *chains = lax.optimization_barrier((joint, *chains))
    last = [receive(chains[c], orders[c][-1]) for c in range(3)]
    raw_buf, prob_buf, own, sent = attend(
        joint, prior_logits[0], scalars, order_column, block, 1, len(pairs) - 1, [raw_buf, prob_buf]
    )
    own, sent, *tied = lax.optimization_barrier((own, sent, *ctx_got, *chains, *last))
    chains = [join(tied[1 + c], tied[4 + c]) for c in range(3)]
    ctx_own.append(own)
    ctx_got = [tied[0], swap(sent, "seq", 1)]
    pieces = [(held, swap(held, "fsdp", 1)) for held in chains]
    if piece % 16 == 0:
        weights = [array for pair in pieces for array in pair]
    else:
        nine = jnp.concatenate([sort_pieces(*pieces[c], codes[c]) for c in range(3)], 0)
        weights = [
            nine[:5].reshape(5, width, width),
            nine[5:].transpose(1, 0, 2, 3).reshape(chunks * width, width),
        ]
        codes = None

    own_column = lax.dynamic_slice_in_dim(order_column, side * local_count, local_count)
    valid_rows = (own_column < length).astype(f32)
    (out_rows, hidden_low, activated, d_branch, d_inner, d_attended, d_res_one,
     d_own, d_sent, sums) = feed(
        where, ctx_own, ctx_got, rows, cotangent[0], valid_rows, vec, inner_bias, weights, codes, groups
    )
    d_got = swap(d_sent, "seq", 1)

    chain_order = [orders[c][::-1] + [top] for c in range(3)]
    if codes is not None:
        back_parts = kernel_grads(
            back_grads_kernel, [chunks], where, [activated, d_branch], groups, "back_grads"
        )
        back_terms = [back_parts[1], swap(back_parts[0], "fsdp", 1)]
        d_inner, back_kept = lax.optimization_barrier((d_inner, back_parts[1]))
        parts = kernel_grads(
            grads_kernel, [2, chunks - 1], where,
            [*ctx_own, *ctx_got, d_attended, hidden_low, d_inner], groups, "grads",
        )
        d_got, *rest = lax.optimization_barrier((d_got, *parts[2:]))
        parts = list(parts[:2]) + rest
        back_terms[0] = back_kept
        reductions = [
            Reduction([parts[1], swap(parts[0], "fsdp", 1)], chain_order[0]),
            Reduction([parts[3], swap(parts[2], "fsdp", 1)], chain_order[1]),
            Reduction(back_terms, chain_order[2]),
        ]
    else:
        reductions = plain_grads(
            ctx_own, ctx_got, d_attended, hidden_low, d_inner, activated, d_branch, chain_order
        )

    def fence(*values):
        terms = tuple(term for reduction in reductions for term in reduction.terms)
        tied = lax.optimization_barrier(values + terms)
        for c, reduction in enumerate(reductions):
            reduction.terms = list(tied[len(values) + 2 * c : len(values) + 2 * c + 2])
        return tied[: len(values)]

    def advance(*values):
        sents = [reduction.sent() for reduction in reductions]
        tied = lax.optimization_barrier((*values, *sents))
        for reduction, sent in zip(reductions, tied[len(values) :]):
            reduction.launch(sent)
        return tied[: len(values)]

    d_context_pos = to_positions(d_own, d_got)
    (d_context_pos,) = fence(d_context_pos)
    (d_context_pos,) = advance(d_context_pos)
    held = []
    held = attend_back(joint, d_context_pos, prob_buf, block, 0, len(pairs) - 1, held)
    held = advance(*fence(*held))
    held = attend_back(joint, d_context_pos, prob_buf, block, len(pairs) - 1, 1, held)
    dprior_buf, d_joint, bias_sums = fence(*held)
    grad_w_qkv = mm(placed_rows, d_joint, TN).astype(bf16).reshape(1, groups, piece, -1)
    qkv = Reduction([grad_w_qkv], bits_of(groups))
    bias_row = jnp.concatenate([bias_sums[0:1], bias_sums[1:2]], 1)
    own_row = lax.broadcasted_iota(jnp.int32, (2, width), 0) == side
    sums = jnp.concatenate([sums[:14], jnp.where(own_row, bias_row, 0.0)], 0)
    sent, sums, d_joint = advance(qkv.sent(), sums, d_joint)
    sums_got = [swap(sums, "fsdp", qkv.order[0])]
    qkv.launch(sent)
    d_rows = mm(d_joint, qkv_weight, NT).astype(bf16)
    d_rows_sent = mm(other_pick, d_rows, TN).astype(bf16)
    while len(reductions[0].order) > 1:
        (d_rows_sent,) = fence(d_rows_sent)
        (d_rows_sent,) = advance(d_rows_sent)

    d_rows_sent, sums, *rest = fence(d_rows_sent, sums, *sums_got, *qkv.terms)
    sums = sums + sum(rest[:-2])
    qkv.terms = rest[-2:]
    nine = Reduction(
        [jnp.concatenate([reduction.terms[k] for reduction in reductions], 0) for k in range(2)],
        [top],
    )
    d_rows_sent, sums, nine_sent, sent = lax.optimization_barrier(
        (d_rows_sent, sums, nine.sent(), qkv.sent())
    )
    nine.launch(nine_sent, False)
    d_rows_got = swap(d_rows_sent, "seq", 1)
    sums_got = [swap(sums, "fsdp", qkv.order[0])]
    qkv.launch(sent, False)
    while len(qkv.order) > 2:
        sums, *rest = lax.optimization_barrier((sums, *sums_got, *qkv.terms))
        sums = sums + sum(rest[:-2])
        qkv.terms = rest[-2:]
        sums_got = [swap(sums, "fsdp", qkv.order[0])]
        qkv.launch(qkv.sent())
    d_rows_own = mm(own_pick, d_rows, TN)
    low_bit, high_bit = qkv.order
    sums = sums + sums_got[0]
    sums_got = [swap(sums, "fsdp", low_bit)]

    d_rows_got, sums, sums_got[0], *rest = lax.optimization_barrier(
        (d_rows_got, sums, sums_got[0], *nine.terms, *qkv.terms)
    )
    sums = sums + sums_got[0]
    own_nine = (rest[0].astype(f32) + rest[1].astype(f32)).astype(bf16)[:, 0]
    four = (rest[2].astype(f32) + rest[3].astype(f32)).astype(bf16)[0]
    mine = ((me & low_bit) != 0) * 1 + ((me & high_bit) != 0) * 2
    peers = (low_bit, high_bit, low_bit | high_bit)
    blocks = [
        lax.dynamic_index_in_dim(four, mine ^ k, 0, keepdims=False) for k in range(4)
    ]
    own_nine, sums, *blocks = lax.optimization_barrier((own_nine, sums, *blocks))
    other_nine = swap(own_nine, "seq", 1)
    blocks[1:] = [swap(blocks[1 + k], "fsdp", peers[k]) for k in range(3)]
    sums_got = [swap(sums, "fsdp", high_bit)]
    tokens_grad = (d_res_one + d_rows_own + d_rows_got.astype(f32)).astype(bf16)

    other_nine, own_nine, sums, *rest = lax.optimization_barrier(
        (other_nine, own_nine, sums, *blocks, *sums_got)
    )
    own_qkv = sum(block.astype(f32) for block in rest[:4]).astype(bf16)
    sums = sums + sum(rest[4:])
    other_qkv = swap(own_qkv, "seq", 1)
    sums = sums + swap(sums, "seq", 1)

    def by_side(own, other, axis):
        return jnp.where(
            side == 0, jnp.concatenate([own, other], axis), jnp.concatenate([other, own], axis)
        ).astype(f32)

    out_nine = by_side(own_nine, other_nine, 2)
    shape = (piece, len(pairs), 3, 1, 2 * HD)
    out_qkv = by_side(own_qkv.reshape(shape), other_qkv.reshape(shape), 3)
    out_qkv = out_qkv.transpose(0, 2, 3, 1, 4).reshape(piece, 3 * width)
    rms = jnp.sqrt(sums[10:13, 0] / (sums[13, 0] * width))
    own_sums = lax.dynamic_slice_in_dim(sums, me * piece, piece, 1)
    bias_grads = jnp.concatenate(
        [sums[14:15].reshape(2, local_width), sums[15:16].reshape(2, local_width)], 1
    )
    bias_grads = lax.dynamic_slice_in_dim(bias_grads, me * piece, piece, 1)
    own_inner = lax.dynamic_slice_in_dim(
        sums[6 : 6 + chunks].reshape(-1), me * chunks * piece, chunks * piece
    )
    return (
        out_rows[None],
        raw_buf[None],
        tokens_grad[None],
        dprior_buf[None],
        out_qkv,
        out_nine[0],
        jnp.concatenate([out_nine[1 + c] for c in range(chunks)], 1),
        out_nine[5:9].reshape(chunks * piece, width),
        bias_grads[0],
        bias_grads[1],
        own_sums[0],
        own_sums[1],
        own_sums[2],
        own_inner,
        own_sums[3],
        own_sums[4],
        own_sums[5],
        rms,
    )


def solution(mesh):
    shard = P("fsdp", "seq", None)
    heads = P("fsdp", "seq", None, None)
    mat = P("fsdp", None)
    vec = P("fsdp")
    return jax.shard_map(
        body,
        mesh=mesh,
        in_specs=(shard, heads, vec, mat, shard) + (mat,) * 4 + (vec,) * 9,
        out_specs=(shard, heads, shard, heads) + (mat,) * 4 + (vec,) * 9 + (P(),),
        check_vma=False,
    )
```

```python
import functools
import math

import jax
import jax.numpy as jnp
from jax import lax
from jax.experimental import pallas as pl
from jax.experimental.pallas import tpu as pltpu
from jax.sharding import PartitionSpec as P

HD = 64
eps_norm = 1e-05
masked_fill = -1e30
f32 = jnp.float32
bf16 = jnp.bfloat16

NT = (((1,), (1,)), ((), ()))
TN = (((0,), (0,)), ((), ()))


def mm(left, right, dims=(((1,), (0,)), ((), ()))):
    return lax.dot_general(left, right, dims, preferred_element_type=f32)


def bits_of(count):
    return [1 << k for k in range(count.bit_length() - 1)]


def swap(value, axis, bit):
    count = lax.axis_size(axis)
    return lax.ppermute(value, axis, [(i, i ^ bit) for i in range(count)])


class Gather:
    def __init__(self, shard):
        self.shape = shard.shape
        self.held = shard[None]
        self.done = []

    def step(self, bit):
        other = swap(self.held, "fsdp", bit)
        high = (lax.axis_index("fsdp") & bit) != 0
        outer = 1 << sum(1 for b in self.done if b > bit)
        self.done.append(bit)
        split = (outer, self.held.shape[0] // outer) + self.shape
        first = jnp.where(high, other, self.held).reshape(split)
        second = jnp.where(high, self.held, other).reshape(split)
        self.held = jnp.stack([first, second], axis=1).reshape((-1,) + self.shape)

    def top_two(self, low, high):
        me = lax.axis_index("fsdp")
        mine = ((me & low) != 0) * 1 + ((me & high) != 0) * 2
        got = [swap(self.held, "fsdp", peer) for peer in (low, high, low | high)]
        four = jnp.stack([self.held] + got)
        self.done += [low, high]
        self.held = jnp.concatenate(
            [lax.dynamic_index_in_dim(four, z ^ mine, 0, keepdims=False) for z in range(4)], 0
        )


def tie(value, *others):
    return lax.optimization_barrier((value,) + others)[0]


def chain_orders():
    rest = list(reversed(bits_of(lax.axis_size("fsdp"))))[1:-1]
    up = rest[::-1]
    return [up + ["seq"], rest[:-1] + ["seq"] + rest[-1:], ["seq"] + up]


def receive(held, stage):
    return swap(held, "seq", 1) if stage == "seq" else swap(held, "fsdp", stage)


def more_slots(slots, stage):
    if stage == "seq":
        return slots + [(a ^ 1, code) for a, code in slots]
    return slots + [(a, code ^ stage) for a, code in slots]


def join(held, got):
    return jnp.concatenate([held, got], axis=0)


def sort_pieces(own, other, slots):
    me = lax.axis_index("fsdp")
    side = lax.axis_index("seq")
    count = len(slots)
    both = jnp.concatenate([own, other], axis=0)
    place = [[0] * count, [0] * count]
    for s, (a, code) in enumerate(slots):
        place[a][code] = s
        place[a][code ^ 1] = s + count
    halves = [
        jnp.take(both, jnp.take(jnp.array(place[a], jnp.int32), jnp.arange(count) ^ me), axis=0)
        for a in range(2)
    ]
    joined = jnp.where(
        side == 0, jnp.concatenate(halves, -1), jnp.concatenate(halves[::-1], -1)
    )
    return joined.transpose(1, 0, 2, 3)


class Reduction:
    def __init__(self, terms, order):
        self.terms = terms
        self.order = order
        self.me = lax.axis_index("fsdp")
        self.side = lax.axis_index("seq")

    def pick(self, own):
        stage = self.order[0]
        picked = []
        for array in self.terms:
            if stage == "seq":
                size = array.shape[3] // 2
                index = self.side if own else 1 - self.side
                picked.append(lax.dynamic_slice_in_dim(array, index * size, size, 3))
            else:
                low = sum(1 for b in self.order if b != "seq" and b < stage)
                shape = array.shape
                array = array.reshape(
                    (shape[0], shape[1] >> (low + 1), 2, 1 << low) + shape[2:]
                )
                mine = ((self.me & stage) != 0).astype(jnp.int32)
                array = lax.dynamic_index_in_dim(
                    array, mine if own else 1 - mine, 2, keepdims=False
                )
                picked.append(array.reshape((shape[0], shape[1] // 2) + shape[2:]))
        total = picked[0].astype(f32)
        for other in picked[1:]:
            total = total + other.astype(f32)
        return total.astype(bf16)

    def sent(self):
        return self.pick(False)

    def launch(self, sent, apart=True):
        if apart:
            *self.terms, _ = lax.optimization_barrier((*self.terms, sent))
        kept = self.pick(True)
        stage = self.order[0]
        self.order = self.order[1:]
        axis, bit = ("seq", 1) if stage == "seq" else ("fsdp", stage)
        self.terms = [kept, swap(sent, axis, bit)]


def pack_kernel(where_ref, *refs):
    w_qkv, w_out, w_in, w_back = refs[:4]
    vectors, (qkv_ref, nine_ref, small_ref) = refs[4:13], refs[13:]
    r, width = w_out.shape
    half = width // 2
    columns = pl.ds(pl.multiple_of(where_ref[1] * half, 128), half)
    nine_ref[0, 0] = w_out[:, columns]
    for c in range(4):
        nine_ref[0, 1 + c] = w_in[:, pl.ds(pl.multiple_of(c * width + where_ref[1] * half, 128), half)]
        nine_ref[0, 5 + c] = w_back[c * r : (c + 1) * r, columns]
    for kind in range(3):
        for t in range(3):
            start = kind * width + where_ref[1] * half + t * 128
            qkv_ref[:, (3 * t + kind) * 128 : (3 * t + kind + 1) * 128] = w_qkv[
                :, pl.ds(pl.multiple_of(start, 128), 128)
            ]
    small_ref[...] = jnp.zeros_like(small_ref)
    for k, vector in enumerate(vectors):
        small_ref[k : k + 1, : vector.shape[1]] = vector[...].astype(f32)


def pack(where, w_qkv, w_out, w_in, w_back, vectors):
    r, width = w_out.shape
    vmem = pl.BlockSpec(memory_space=pltpu.VMEM)
    return pl.pallas_call(
        pack_kernel,
        in_specs=[pl.BlockSpec(memory_space=pltpu.SMEM)] + [vmem] * 13,
        out_specs=[vmem] * 3,
        out_shape=[
            jax.ShapeDtypeStruct((r, 3 * width // 2), bf16),
            jax.ShapeDtypeStruct((1, 9, r, width // 2), bf16),
            jax.ShapeDtypeStruct((16, 256), f32),
        ],
        name="pack",
    )(where, w_qkv, w_out, w_in, w_back, *[vector[None] for vector in vectors])


def attend_kernel(length_ref, q_ref, k_ref, v_ref, own_ref, other_ref, prior_ref, *refs):
    raw_ref, prob_ref, ctx_own_ref, ctx_sent_ref, ctx = refs[-5:]
    step = pl.program_id(0)
    block = q_ref.shape[0]
    keys = k_ref.shape[0]
    lane = lax.broadcasted_iota(jnp.int32, (1, 2 * HD), 1)
    seen = lax.broadcasted_iota(jnp.int32, (1, keys), 1) < length_ref[0]
    q = q_ref[...] * jnp.asarray(1.0 / math.sqrt(HD), bf16)
    k = k_ref[...]
    v = v_ref[...]
    parts = []
    for h in range(2):
        mine = (lane >= HD) if h else (lane < HD)
        scores = mm(jnp.where(mine, q, jnp.zeros_like(q)), k, NT) + prior_ref[h].astype(f32)
        raw_ref[h] = scores.astype(bf16)
        masked = jnp.where(seen, scores, masked_fill)
        largest = jnp.max(masked, axis=-1, keepdims=True)
        exponent = jnp.exp(masked - largest)
        inverse = 1.0 / jnp.sum(exponent, axis=-1, keepdims=True)
        prob = (exponent * inverse).astype(bf16)
        prob_ref[h] = prob
        parts.append(mm(prob, v))
    ctx[pl.ds(pl.multiple_of(step * block, block), block), :] = jnp.where(
        lane < HD, parts[0], parts[1]
    ).astype(bf16)

    @pl.when(step == pl.num_programs(0) - 1)
    def _():
        position = lax.broadcasted_iota(jnp.int32, (own_ref.shape[0], keys), 1)
        placed = ctx[...]
        for order_ref, out_ref in ((other_ref, ctx_sent_ref), (own_ref, ctx_own_ref)):
            pick = jnp.where(position == order_ref[...], 1.0, 0.0).astype(bf16)
            out_ref[...] = mm(pick, placed).astype(bf16)


def attend(joint, prior, scalars, order_column, block, pair, held):
    heads, total, _ = prior.shape
    wide = 2 * HD
    square = pl.BlockSpec((2, block, total), lambda i, *_: (pair, i, 0))
    hbm = pl.BlockSpec(memory_space=pl.ANY)
    local = order_column.shape[0] // 2
    stored = pl.BlockSpec((local, wide), lambda i, *_: (0, 0))
    return pl.pallas_call(
        attend_kernel,
        grid_spec=pltpu.PrefetchScalarGridSpec(
            num_scalar_prefetch=1,
            grid=(total // block,),
            in_specs=[
                pl.BlockSpec((block, wide), lambda i, *_: (i, 3 * pair)),
                pl.BlockSpec((total, wide), lambda i, *_: (0, 3 * pair + 1)),
                pl.BlockSpec((total, wide), lambda i, *_: (0, 3 * pair + 2)),
                pl.BlockSpec((local, 1), lambda i, scalars: (scalars[1], 0)),
                pl.BlockSpec((local, 1), lambda i, scalars: (1 - scalars[1], 0)),
                square,
            ]
            + [hbm] * len(held),
            out_specs=[square, square, stored, stored],
            scratch_shapes=[pltpu.VMEM((total, wide), bf16)],
        ),
        out_shape=[
            jax.ShapeDtypeStruct(prior.shape, bf16),
            jax.ShapeDtypeStruct(prior.shape, bf16),
            jax.ShapeDtypeStruct((local, wide), bf16),
            jax.ShapeDtypeStruct((local, wide), bf16),
        ],
        input_output_aliases={7 + k: k for k in range(len(held))},
        cost_estimate=pl.CostEstimate(flops=1000, transcendentals=0, bytes_accessed=1000),
        compiler_params=pltpu.CompilerParams(vmem_limit_bytes=56 << 20),
        name="attend",
    )(scalars, joint, joint, joint, order_column, order_column, prior, *held)


def attend_back_kernel(q_ref, k_ref, v_ref, dc_ref, prob_ref, *refs):
    dprior_ref, dj_ref, bias_ref, dk_acc, dv_acc = refs[-5:]
    step = pl.program_id(1)
    block = q_ref.shape[0]
    wide_lanes = 2 * HD
    lane = lax.broadcasted_iota(jnp.int32, (1, wide_lanes), 1)
    scale = 1.0 / math.sqrt(HD)
    q = q_ref[...]
    k = k_ref[...]
    v = v_ref[...]
    dc = dc_ref[...]

    @pl.when(step == 0)
    def _():
        dk_acc[...] = jnp.zeros_like(dk_acc)
        dv_acc[...] = jnp.zeros_like(dv_acc)
        bias_ref[...] = jnp.zeros_like(bias_ref)

    dq, dk, dv = [], [], []
    for h in range(2):
        mine = (lane >= HD) if h else (lane < HD)
        prob = prob_ref[h]
        wide = prob.astype(f32)
        d_prob = mm(jnp.where(mine, dc, jnp.zeros_like(dc)), v, NT)
        row_term = jnp.sum(wide * d_prob, axis=-1, keepdims=True)
        d_scores = (wide * (d_prob - row_term)).astype(bf16)
        dprior_ref[h] = d_scores
        dq.append(mm(d_scores, k))
        dk.append(mm(d_scores, q, TN))
        dv.append(mm(prob, dc, TN))
    first = lane < HD
    d_query = (jnp.where(first, dq[0], dq[1]) * scale).astype(bf16)
    dj_ref[pl.ds(pl.multiple_of(step * block, block), block), 0:wide_lanes] = d_query
    bias_ref[0:1, :] += jnp.sum(d_query.astype(f32), axis=0, keepdims=True)
    dk_acc[...] += jnp.where(first, dk[0], dk[1])
    dv_acc[...] += jnp.where(first, dv[0], dv[1])

    @pl.when(step == pl.num_programs(1) - 1)
    def _():
        dj_ref[:, wide_lanes : 2 * wide_lanes] = (dk_acc[...] * scale).astype(bf16)
        d_value = dv_acc[...].astype(bf16)
        dj_ref[:, 2 * wide_lanes : 3 * wide_lanes] = d_value
        bias_ref[1:2, :] = jnp.sum(d_value.astype(f32), axis=0, keepdims=True)


def attend_back(joint, d_context, prob, block, first, pairs, held):
    heads, total, _ = prob.shape
    wide = 2 * HD
    square = pl.BlockSpec((2, block, total), lambda t, i: (first + t, i, 0))
    return pl.pallas_call(
        attend_back_kernel,
        grid=(pairs, total // block),
        in_specs=[
            pl.BlockSpec((block, wide), lambda t, i: (i, 3 * (first + t))),
            pl.BlockSpec((total, wide), lambda t, i: (0, 3 * (first + t) + 1)),
            pl.BlockSpec((total, wide), lambda t, i: (0, 3 * (first + t) + 2)),
            pl.BlockSpec((block, wide), lambda t, i: (i, first + t)),
            square,
        ]
        + [pl.BlockSpec(memory_space=pl.ANY)] * len(held),
        out_specs=[
            square,
            pl.BlockSpec((total, 3 * wide), lambda t, i: (0, first + t)),
            pl.BlockSpec((8, wide), lambda t, i: (0, first + t)),
        ],
        out_shape=[
            jax.ShapeDtypeStruct(prob.shape, bf16),
            jax.ShapeDtypeStruct((total, 3 * heads * HD), bf16),
            jax.ShapeDtypeStruct((8, heads * HD), f32),
        ],
        input_output_aliases={5 + k: k for k in range(len(held))},
        scratch_shapes=[pltpu.VMEM((total, wide), f32)] * 2,
        cost_estimate=pl.CostEstimate(flops=1000, transcendentals=0, bytes_accessed=1000),
        compiler_params=pltpu.CompilerParams(vmem_limit_bytes=56 << 20),
        name="attend_back",
    )(joint, joint, joint, d_context, prob, *held)


def put_blocks(sent_ref, kept_ref, odd, unit, first, blocks):
    blocks = blocks.astype(bf16)
    lower, upper = blocks[:, 0], blocks[:, 1]
    at = pl.ds(first, blocks.shape[0])
    sent_ref[unit, at] = jnp.where(odd, lower, upper)
    kept_ref[unit, at] = jnp.where(odd, upper, lower)


def back_grads_kernel(where_ref, act_ref, d_branch_ref, sent_ref, kept_ref):
    odd = (where_ref[0] & 1) == 1
    chunks, half_groups, r, width = sent_ref.shape
    each = half_groups // chunks
    d_branch = d_branch_ref[...]

    def chunk(c, carry):
        part = mm(act_ref[:, pl.ds(pl.multiple_of(c * width, 128), width)], d_branch, TN)
        part = part.reshape(each, 2, chunks, r, width)
        for q in range(chunks):
            put_blocks(sent_ref, kept_ref, odd, q, c * each, part[:, :, q])
        return carry

    lax.fori_loop(0, chunks, chunk, 0)


def grads_kernel(where_ref, *refs):
    ctx_own_refs, ctx_got_refs, refs = refs[:3], refs[3:6], refs[6:]
    d_att_ref, low_ref, d_inner_ref, first_sent, first_kept, rest_sent, rest_kept = refs
    odd = (where_ref[0] & 1) == 1
    side = where_ref[1]
    r, width = first_sent.shape[2:]
    groups = 2 * first_sent.shape[1]
    low = low_ref[...]

    def inner(c):
        return mm(low, d_inner_ref[c], TN).reshape(groups // 2, 2, r, width)

    def chunk(c, carry):
        put_blocks(rest_sent, rest_kept, odd, c, 0, inner(1 + c))
        return carry

    put_blocks(first_sent, first_kept, odd, 1, 0, inner(0))
    lax.fori_loop(0, rest_sent.shape[0], chunk, 0)
    d_att = d_att_ref[...]
    for part_refs, start in ((ctx_own_refs, side), (ctx_got_refs, 1 - side)):
        part = mm(jnp.concatenate([ref[...] for ref in part_refs], 1), d_att, TN)
        part = part.reshape(groups // 4, 2, r, width)
        put_blocks(first_sent, first_kept, odd, 0, start * (groups // 4), part)


def kernel_grads(kernel, units, where, arrays, groups, name):
    rows, width = arrays[-1].shape[-2:]
    vmem = pl.BlockSpec(memory_space=pltpu.VMEM)
    parts = [
        jax.ShapeDtypeStruct((count, groups // 2, width // groups, width), bf16)
        for count in units
        for _ in range(2)
    ]
    return pl.pallas_call(
        kernel,
        in_specs=[pl.BlockSpec(memory_space=pltpu.SMEM)] + [vmem] * len(arrays),
        out_specs=[vmem] * len(parts),
        out_shape=parts,
        cost_estimate=pl.CostEstimate(flops=1000, transcendentals=0, bytes_accessed=1000),
        compiler_params=pltpu.CompilerParams(vmem_limit_bytes=60 << 20),
        name=name,
    )(where, *arrays)


def feed_kernel(
    where_ref, *refs, codes, chunks,
):
    ctx_own_refs, ctx_got_refs, refs = refs[:3], refs[3:6], refs[6:]
    (tokens_ref, cot_ref, valid_ref, vec_ref, bias_in_ref), refs = refs[:5], refs[5:]
    weight_count = 2 if codes is None else 6
    weights, refs = refs[:weight_count], refs[weight_count:]
    (out_ref, low_ref, act_ref, d_branch_ref, d_inner_ref, d_att_ref, d_res_ref,
     d_own_ref, d_sent_ref, sums_ref, w_five, w_back, slope, sems) = refs
    me = where_ref[0]
    side = where_ref[1]
    width = tokens_ref.shape[1]
    half = width // 2

    def copies(chain):
        if codes is None:
            if chain == 2:
                return []
            target = (w_five, w_back)[chain]
            return [pltpu.make_async_copy(weights[chain], target, sems.at[chain])]
        made = []
        r = weights[0].shape[2]
        for b in range(2):
            source = weights[2 * chain + b]
            for s, (a, code) in enumerate(codes[chain]):
                column = pl.ds(pl.multiple_of((side ^ a) * half, 128), half)
                block = me ^ (code ^ b)
                rows = pl.ds(pl.multiple_of(block * r, 16), r)
                moves = (
                    ((0, 3, w_five.at[0:3, rows, column]),),
                    ((0, 2, w_five.at[3:5, rows, column]), (2, 1, w_back.at[block, 0:1, :, column])),
                    ((0, 3, w_back.at[block, 1:4, :, column]),),
                )[chain]
                for first, count, target in moves:
                    made.append(pltpu.make_async_copy(
                        source.at[s, pl.ds(first, count)], target, sems.at[chain]))
        return made

    groups = [copies(chain) for chain in range(3)]
    for group in groups:
        for copy in group:
            copy.start()

    def back_rows(c):
        if codes is None:
            return w_back[c * width : (c + 1) * width, :]
        per = w_back.shape[0] // chunks
        return w_back[c * per : (c + 1) * per].reshape(width, width)

    vec = vec_ref[...]
    proj_bias, first_gain, first_shift, outer_bias, second_gain, second_shift = (
        vec[k : k + 1] for k in range(2, 8)
    )
    own_rows = pl.ds(pl.multiple_of(side * half, 128), half)
    other_rows = pl.ds(pl.multiple_of((1 - side) * half, 128), half)
    valid = valid_ref[...]
    for copy in groups[0]:
        copy.wait()
    ctx_own = jnp.concatenate([ref[...] for ref in ctx_own_refs], 1)
    ctx_got = jnp.concatenate([ref[...] for ref in ctx_got_refs], 1)
    attended = (
        mm(ctx_own, w_five[0, own_rows, :]) + mm(ctx_got, w_five[0, other_rows, :]) + proj_bias
    )
    tokens_f = tokens_ref[...].astype(f32)

    def stat(row, values):
        total = jnp.sum(jnp.sum(values, axis=0, keepdims=True), axis=1, keepdims=True)
        sums_ref[row : row + 1, :] = jnp.broadcast_to(total, (1, width))

    def column_sum(row, values):
        sums_ref[row : row + 1, :] = jnp.sum(values, axis=0, keepdims=True)

    def normalize(values):
        centered = values - jnp.mean(values, axis=-1, keepdims=True)
        spread = lax.rsqrt(jnp.mean(centered * centered, axis=-1, keepdims=True) + eps_norm)
        return centered * spread, spread

    def normalize_back(grad, gain, normal, spread):
        e = grad * gain
        return spread * (
            e - jnp.mean(e, axis=-1, keepdims=True)
            - normal * jnp.mean(e * normal, axis=-1, keepdims=True)
        )

    stat(10, valid * tokens_f * tokens_f)
    stat(11, valid * attended * attended)
    stat(13, valid * jnp.ones((1, 128), f32) * (1.0 / 128.0))
    normal_one, spread_one = normalize(tokens_f + attended)
    hidden = normal_one * first_gain + first_shift
    hidden_low = hidden.astype(bf16)
    low_ref[...] = hidden_low
    for copy in groups[1] + groups[2]:
        copy.wait()
    branch = jnp.zeros_like(hidden)
    for c in range(chunks):
        inner = mm(hidden_low, w_five[1 + c]) + bias_in_ref[c : c + 1, :]
        below = 0.5 + 0.5 * lax.erf(inner * math.sqrt(0.5))
        slope[c] = below + inner * (jnp.exp(inner * inner * -0.5) * (1.0 / math.sqrt(2.0 * math.pi)))
        activated = (inner * below).astype(bf16)
        columns = slice(c * width, (c + 1) * width)
        act_ref[:, columns] = activated
        branch = branch + mm(activated, back_rows(c))
    branch = branch + outer_bias
    stat(12, valid * branch * branch)
    normal_two, spread_two = normalize(hidden + branch)
    out_ref[...] = (normal_two * second_gain + second_shift).astype(bf16)
    d_output = cot_ref[...].astype(f32) * valid
    column_sum(4, d_output * normal_two)
    column_sum(5, d_output)
    d_hidden = normalize_back(d_output, second_gain, normal_two, spread_two)
    d_branch = d_hidden.astype(bf16)
    d_branch_ref[...] = d_branch
    column_sum(3, d_branch.astype(f32))
    for c in range(chunks):
        columns = slice(c * width, (c + 1) * width)
        d_inner = (mm(d_branch, back_rows(c), NT) * slope[c]).astype(bf16)
        d_inner_ref[c] = d_inner
        column_sum(6 + c, d_inner.astype(f32))
        d_hidden = d_hidden + mm(d_inner, w_five[1 + c], NT)
    column_sum(1, d_hidden * normal_one)
    column_sum(2, d_hidden)
    d_res = normalize_back(d_hidden, first_gain, normal_one, spread_one)
    d_res_ref[...] = d_res
    d_att = d_res.astype(bf16)
    d_att_ref[...] = d_att
    column_sum(0, d_att.astype(f32))
    d_sent_ref[...] = mm(d_att, w_five[0, other_rows, :], NT).astype(bf16)
    d_own_ref[...] = mm(d_att, w_five[0, own_rows, :], NT).astype(bf16)


def feed(where, ctx_own, ctx_got, tokens, cot, valid, vec, bias_in, weights, codes, groups):
    rows, width = tokens.shape
    chunks = bias_in.shape[0]
    vmem = pl.BlockSpec(memory_space=pltpu.VMEM)
    hbm = pl.BlockSpec(memory_space=pl.ANY)
    flat = lambda *shape: jax.ShapeDtypeStruct(shape, bf16)
    return pl.pallas_call(
        functools.partial(feed_kernel, codes=codes, chunks=chunks),
        in_specs=[pl.BlockSpec(memory_space=pltpu.SMEM)] + [vmem] * 11 + [hbm] * len(weights),
        out_specs=[vmem] * 10,
        out_shape=[
            flat(rows, width),
            flat(rows, width),
            flat(rows, chunks * width),
            flat(rows, width),
            flat(chunks, rows, width),
            flat(rows, width),
            jax.ShapeDtypeStruct((rows, width), f32),
        ]
        + [flat(rows, width // 2)] * 2
        + [
            jax.ShapeDtypeStruct((16, width), f32),
        ],
        scratch_shapes=[
            pltpu.VMEM((chunks + 1, width, width), bf16),
            pltpu.VMEM((groups, 4, width // groups, width) if codes else (chunks * width, width), bf16),
            pltpu.VMEM((chunks, rows, width), f32),
            pltpu.SemaphoreType.DMA((3,)),
        ],
        cost_estimate=pl.CostEstimate(
            flops=2 * rows * width * width * (4 * chunks + 2),
            transcendentals=2 * rows * width * chunks,
            bytes_accessed=2 * width * width * (2 * chunks + 1) + 2 * rows * width * (2 * chunks + 8),
        ),
        compiler_params=pltpu.CompilerParams(vmem_limit_bytes=60 << 20),
        name="feed",
    )(where, *ctx_own, *ctx_got, tokens, cot, valid, vec, bias_in, *weights)


def plain_grads(ctx_own, ctx_got, d_attended, hidden_low, d_inner, activated, d_branch, chain_order):
    side = lax.axis_index("seq")
    mine = lax.axis_index("fsdp") & 1
    groups = lax.axis_size("fsdp")
    chunks, _, width = d_inner.shape
    piece = width // groups
    back = mm(activated, d_branch, TN).astype(bf16).reshape(groups // 2, 2, chunks, piece, width)
    own = jnp.concatenate(ctx_own, 1)
    got = jnp.concatenate(ctx_got, 1)
    context = jnp.where(side == 0, jnp.concatenate([own, got], 1), jnp.concatenate([got, own], 1))
    units = [mm(context, d_attended, TN)] + [mm(hidden_low, d_inner[c], TN) for c in range(chunks)]
    units = [unit.astype(bf16).reshape(groups // 2, 2, piece, width) for unit in units]
    units = units + [back[:, :, q] for q in range(chunks)]
    reductions = []
    for c, (first, last) in enumerate(((0, 2), (2, 5), (5, 9))):
        stacked = jnp.stack(units[first:last])
        sent = lax.dynamic_index_in_dim(stacked, 1 - mine, 2, keepdims=False)
        kept = lax.dynamic_index_in_dim(stacked, mine, 2, keepdims=False)
        reductions.append(Reduction([kept, swap(sent, "fsdp", 1)], chain_order[c]))
    return reductions


def body(
    tokens, prior_logits, lengths, order, cotangent, w_qkv, w_out, w_in, w_back,
    bias_q, bias_v, bias_o, gain_one, shift_one, bias_in, bias_back, gain_two, shift_two,
):
    side = lax.axis_index("seq")
    me = lax.axis_index("fsdp")
    groups = lax.axis_size("fsdp")
    rows = tokens[0]
    local_count, width = rows.shape
    total = 2 * local_count
    heads_local = prior_logits.shape[1]
    local_width = heads_local * HD
    piece = bias_q.shape[0]
    chunks = w_in.shape[1] // width
    pairs = range(heads_local // 2)
    top, *middle = reversed(bits_of(groups))
    where = jnp.stack([me, side]).astype(jnp.int32)

    other_rows = swap(rows, "seq", 1)
    own_qkv, nine, small = pack(
        where, w_qkv, w_out, w_in, w_back,
        (bias_q, bias_v, bias_o, gain_one, shift_one, bias_back, gain_two, shift_two, bias_in),
    )
    ascending = bits_of(groups)
    small_chain = Gather(small.astype(bf16))
    qkv_chain = Gather(own_qkv)
    *lower, low_bit, high_bit = ascending
    small_chain.step(lower[0])
    qkv_chain.top_two(low_bit, high_bit)
    order_column = order[0][:, None]
    small_chain.held, rows, order_column, qkv_chain.held = lax.optimization_barrier(
        (small_chain.held, rows, order_column, qkv_chain.held)
    )
    for bit in lower[1:]:
        small_chain.step(bit)
    for k, bit in enumerate(lower[::-1]):
        qkv_chain.step(bit)
        if k == 0:
            small_chain.held, qkv_chain.held = lax.optimization_barrier(
                (small_chain.held, qkv_chain.held)
            )
            small_chain.top_two(low_bit, high_bit)
    small_all = small_chain.held.astype(f32)
    qkv_weight = qkv_chain.held.reshape(width, 3 * local_width)
    vec = small_all[:, :8, :piece].transpose(1, 0, 2).reshape(8, width)
    inner_bias = small_all[:, 8, : chunks * piece].reshape(chunks, width)
    orders = chain_orders()
    nine = join(nine, receive(nine, top))
    chains = [nine[:, 3 * c : 3 * c + 3] for c in range(3)]
    codes = [[(0, 0), (0, top)]] * 3
    for step in range(len(orders[0])):
        codes = [more_slots(codes[c], orders[c][step]) for c in range(3)]
    for step in range(len(orders[0]) - 2):
        chains = [join(chains[c], receive(chains[c], orders[c][step])) for c in range(3)]
    third = [receive(chains[c], orders[c][-2]) for c in range(3)]

    order_row = order[0]
    length = lengths[0]
    scalars = jnp.stack([length, side]).astype(jnp.int32)
    own_order = lax.dynamic_slice_in_dim(order_row, side * local_count, local_count)
    other_order = lax.dynamic_slice_in_dim(order_row, (1 - side) * local_count, local_count)
    positions = jnp.arange(total, dtype=jnp.int32)
    own_pick = (positions[:, None] == own_order[None, :]).astype(bf16)
    other_pick = (positions[:, None] == other_order[None, :]).astype(bf16)

    def to_positions(own, other):
        return (mm(own_pick, own) + mm(other_pick, other)).astype(bf16)

    placed_rows = to_positions(rows, other_rows)
    own_cols = lambda vector: lax.dynamic_slice_in_dim(
        vector, side * local_width, local_width
    ).reshape(-1, 2 * HD)
    bias_cols = own_cols(vec[0])
    joint_bias = jnp.stack([bias_cols, jnp.zeros_like(bias_cols), own_cols(vec[1])], 1).reshape(-1)
    joint = (mm(placed_rows, qkv_weight) + joint_bias).astype(bf16)
    held = []
    ctx_own, ctx_got = [], []
    for t in pairs:
        raw_buf, prob_buf, own, sent = attend(
            joint, prior_logits[0], scalars, order_column, min(256, total), t, held
        )
        held = [raw_buf, prob_buf]
        if t == 0:
            joint, own, *tied = lax.optimization_barrier((joint, own, *chains, *third))
            chains = [join(tied[c], tied[3 + c]) for c in range(3)]
            joint, *chains = lax.optimization_barrier((joint, *chains))
            last = [receive(chains[c], orders[c][-1]) for c in range(3)]
        if t == len(pairs) - 1:
            own, sent, *tied = lax.optimization_barrier((own, sent, *ctx_got, *chains, *last))
            ctx_got = tied[:t]
            chains = [join(tied[t + c], tied[t + 3 + c]) for c in range(3)]
        ctx_own.append(own)
        ctx_got.append(swap(sent, "seq", 1))
    pieces = [(held, swap(held, "fsdp", 1)) for held in chains]
    if piece % 16 == 0:
        weights = [array for pair in pieces for array in pair]
    else:
        nine = jnp.concatenate([sort_pieces(*pieces[c], codes[c]) for c in range(3)], 0)
        weights = [
            nine[:5].reshape(5, width, width),
            nine[5:].transpose(1, 0, 2, 3).reshape(chunks * width, width),
        ]
        codes = None

    valid_rows = (own_order < length).astype(f32)[:, None]
    (out_rows, hidden_low, activated, d_branch, d_inner, d_attended, d_res_one,
     d_own, d_sent, sums) = feed(
        where, ctx_own, ctx_got, rows, cotangent[0], valid_rows, vec, inner_bias, weights, codes, groups
    )
    d_got = swap(d_sent, "seq", 1)

    chain_order = [orders[c][::-1] + [top] for c in range(3)]
    if codes is not None:
        back_parts = kernel_grads(
            back_grads_kernel, [chunks], where, [activated, d_branch], groups, "back_grads"
        )
        back_terms = [back_parts[1], swap(back_parts[0], "fsdp", 1)]
        d_inner, back_kept = lax.optimization_barrier((d_inner, back_parts[1]))
        parts = kernel_grads(
            grads_kernel, [2, chunks - 1], where,
            [*ctx_own, *ctx_got, d_attended, hidden_low, d_inner], groups, "grads",
        )
        d_got, *rest = lax.optimization_barrier((d_got, *parts[2:]))
        parts = list(parts[:2]) + rest
        back_terms[0] = back_kept
        reductions = [
            Reduction([parts[1], swap(parts[0], "fsdp", 1)], chain_order[0]),
            Reduction([parts[3], swap(parts[2], "fsdp", 1)], chain_order[1]),
            Reduction(back_terms, chain_order[2]),
        ]
    else:
        reductions = plain_grads(
            ctx_own, ctx_got, d_attended, hidden_low, d_inner, activated, d_branch, chain_order
        )

    def fence(*values):
        terms = tuple(term for reduction in reductions for term in reduction.terms)
        tied = lax.optimization_barrier(values + terms)
        for c, reduction in enumerate(reductions):
            reduction.terms = list(tied[len(values) + 2 * c : len(values) + 2 * c + 2])
        return tied[: len(values)]

    def advance(*values):
        sents = [reduction.sent() for reduction in reductions]
        tied = lax.optimization_barrier((*values, *sents))
        for reduction, sent in zip(reductions, tied[len(values) :]):
            reduction.launch(sent)
        return tied[: len(values)]

    d_context_pos = to_positions(d_own, d_got)
    (d_context_pos,) = fence(d_context_pos)
    (d_context_pos,) = advance(d_context_pos)
    block = min(256, total)
    held = []
    held = attend_back(joint, d_context_pos, prob_buf, block, 0, len(pairs) - 1, held)
    held = advance(*fence(*held))
    held = attend_back(joint, d_context_pos, prob_buf, block, len(pairs) - 1, 1, held)
    dprior_buf, d_joint, bias_sums = fence(*held)
    grad_w_qkv = mm(placed_rows, d_joint, TN).astype(bf16).reshape(1, groups, piece, -1)
    qkv = Reduction([grad_w_qkv], bits_of(groups))
    bias_row = jnp.concatenate([bias_sums[0:1], bias_sums[1:2]], 1)
    own_row = lax.broadcasted_iota(jnp.int32, (2, width), 0) == side
    sums = jnp.concatenate([sums[:14], jnp.where(own_row, bias_row, 0.0)], 0)
    sent, sums, d_joint = advance(qkv.sent(), sums, d_joint)
    sums_got = [swap(sums, "fsdp", qkv.order[0])]
    qkv.launch(sent)
    d_rows = mm(d_joint, qkv_weight, NT).astype(bf16)
    d_rows_sent = mm(other_pick, d_rows, TN).astype(bf16)
    while len(reductions[0].order) > 1:
        (d_rows_sent,) = fence(d_rows_sent)
        (d_rows_sent,) = advance(d_rows_sent)

    d_rows_sent, sums, *rest = fence(d_rows_sent, sums, *sums_got, *qkv.terms)
    sums = sums + sum(rest[:-2])
    qkv.terms = rest[-2:]
    nine = Reduction(
        [jnp.concatenate([reduction.terms[k] for reduction in reductions], 0) for k in range(2)],
        [top],
    )
    d_rows_sent, sums, nine_sent, sent = lax.optimization_barrier(
        (d_rows_sent, sums, nine.sent(), qkv.sent())
    )
    nine.launch(nine_sent, False)
    d_rows_got = swap(d_rows_sent, "seq", 1)
    sums_got = [swap(sums, "fsdp", qkv.order[0])]
    qkv.launch(sent, False)
    while len(qkv.order) > 2:
        sums, *rest = lax.optimization_barrier((sums, *sums_got, *qkv.terms))
        sums = sums + sum(rest[:-2])
        qkv.terms = rest[-2:]
        sums_got = [swap(sums, "fsdp", qkv.order[0])]
        qkv.launch(qkv.sent())
    d_rows_own = mm(own_pick, d_rows, TN)
    low_bit, high_bit = qkv.order
    sums = sums + sums_got[0]
    sums_got = [swap(sums, "fsdp", low_bit)]

    d_rows_got, sums, sums_got[0], *rest = lax.optimization_barrier(
        (d_rows_got, sums, sums_got[0], *nine.terms, *qkv.terms)
    )
    sums = sums + sums_got[0]
    own_nine = (rest[0].astype(f32) + rest[1].astype(f32)).astype(bf16)[:, 0]
    four = (rest[2].astype(f32) + rest[3].astype(f32)).astype(bf16)[0]
    mine = ((me & low_bit) != 0) * 1 + ((me & high_bit) != 0) * 2
    peers = (low_bit, high_bit, low_bit | high_bit)
    blocks = [
        lax.dynamic_index_in_dim(four, mine ^ k, 0, keepdims=False) for k in range(4)
    ]
    own_nine, sums, *blocks = lax.optimization_barrier((own_nine, sums, *blocks))
    other_nine = swap(own_nine, "seq", 1)
    blocks[1:] = [swap(blocks[1 + k], "fsdp", peers[k]) for k in range(3)]
    sums_got = [swap(sums, "fsdp", high_bit)]
    tokens_grad = (d_res_one + d_rows_own + d_rows_got.astype(f32)).astype(bf16)

    other_nine, own_nine, sums, *rest = lax.optimization_barrier(
        (other_nine, own_nine, sums, *blocks, *sums_got)
    )
    own_qkv = sum(block.astype(f32) for block in rest[:4]).astype(bf16)
    sums = sums + sum(rest[4:])
    other_qkv = swap(own_qkv, "seq", 1)
    sums = sums + swap(sums, "seq", 1)

    def by_side(own, other, axis):
        return jnp.where(
            side == 0, jnp.concatenate([own, other], axis), jnp.concatenate([other, own], axis)
        ).astype(f32)

    out_nine = by_side(own_nine, other_nine, 2)
    shape = (piece, len(pairs), 3, 1, 2 * HD)
    out_qkv = by_side(own_qkv.reshape(shape), other_qkv.reshape(shape), 3)
    out_qkv = out_qkv.transpose(0, 2, 3, 1, 4).reshape(piece, 3 * width)
    rms = jnp.sqrt(sums[10:13, 0] / (sums[13, 0] * width))
    own_sums = lax.dynamic_slice_in_dim(sums, me * piece, piece, 1)
    bias_grads = jnp.concatenate(
        [sums[14:15].reshape(2, local_width), sums[15:16].reshape(2, local_width)], 1
    )
    bias_grads = lax.dynamic_slice_in_dim(bias_grads, me * piece, piece, 1)
    own_inner = lax.dynamic_slice_in_dim(
        sums[6 : 6 + chunks].reshape(-1), me * chunks * piece, chunks * piece
    )
    return (
        out_rows[None],
        raw_buf[None],
        tokens_grad[None],
        dprior_buf[None],
        out_qkv,
        out_nine[0],
        jnp.concatenate([out_nine[1 + c] for c in range(chunks)], 1),
        out_nine[5:9].reshape(chunks * piece, width),
        bias_grads[0],
        bias_grads[1],
        own_sums[0],
        own_sums[1],
        own_sums[2],
        own_inner,
        own_sums[3],
        own_sums[4],
        own_sums[5],
        rms,
    )


def solution(mesh):
    shard = P("fsdp", "seq", None)
    heads = P("fsdp", "seq", None, None)
    mat = P("fsdp", None)
    vec = P("fsdp")
    return jax.shard_map(
        body,
        mesh=mesh,
        in_specs=(shard, heads, vec, mat, shard) + (mat,) * 4 + (vec,) * 9,
        out_specs=(shard, heads, shard, heads) + (mat,) * 4 + (vec,) * 9 + (P(),),
        check_vma=False,
    )
```
